32 devices in a mesh: ctx: 8 (over y, x, core), fsdp: 4 (over z).
Axes of the slice: x: 2, y: 2, z: 4, core: 2. Of those that a mesh axis runs over, the one named last changes fastest.
Arguments:
- hidden_in: bfloat16 [4, 1024, 1024], P('fsdp', 'ctx'), may hold values from -6 to 6
- encoder_out: bfloat16 [4, 2048, 1024], P('fsdp', 'ctx'), may hold values from -6 to 6
- doc_ids: int32 [4, 1024], P('fsdp'), may hold values from 0 to 3, as said below
- enc_offsets: int32 [4, 4], P('fsdp'), may hold values from 0 to 1536, as said below
- cotangent: bfloat16 [4, 1024, 1024], P('fsdp', 'ctx'), may hold values from -6 to 6
- self_qkv: bfloat16 [1024, 3072], P('fsdp'), may hold values from -0.09375 to 0.09375
- self_out: bfloat16 [1024, 1024], P('fsdp'), may hold values from -0.75 to 0.75
- rel_bias: bfloat16 [32, 16], P('fsdp'), may hold values from -4 to 4
- cross_q: bfloat16 [1024, 1024], P('fsdp'), may hold values from -0.09375 to 0.09375
- cross_kv: bfloat16 [1024, 2048], P('fsdp'), may hold values from -0.09375 to 0.09375
- cross_out: bfloat16 [1024, 1024], P('fsdp'), may hold values from -0.75 to 0.75
- ffn_in: bfloat16 [1024, 5632], P('fsdp'), may hold values from -0.1875 to 0.1875
- ffn_out: bfloat16 [2816, 1024], P('fsdp'), may hold values from -0.109375 to 0.109375
- norm_gains: bfloat16 [3, 1024], P(None, 'fsdp'), may hold values from 0.5 to 1.5
Outputs:
- output: bfloat16 [4, 1024, 1024], P('fsdp', 'ctx')
- grad_hidden: float32 [4, 1024, 1024], P('fsdp', 'ctx')
- grad_encoder: float32 [4, 2048, 1024], P('fsdp', 'ctx')
- grad_self_qkv: float32 [1024, 3072], P('fsdp')
- grad_self_out: float32 [1024, 1024], P('fsdp')
- grad_rel_bias: float32 [32, 16], P('fsdp')
- grad_cross_q: float32 [1024, 1024], P('fsdp')
- grad_cross_kv: float32 [1024, 2048], P('fsdp')
- grad_cross_out: float32 [1024, 1024], P('fsdp')
- grad_ffn_in: float32 [1024, 5632], P('fsdp')
- grad_ffn_out: float32 [2816, 1024], P('fsdp')
- grad_norm_gains: float32 [3, 1024], P(None, 'fsdp')
The draws below stay inside these ranges and needn't reach their ends.
Inputs may be any that keep to these rules, and one draw needn't show every extreme that they name: In each stream doc_ids never falls along positions; each of the 4 documents has 1 to 682 tokens, and one has exactly 682. In each stream the offsets are distinct multiples of 512; document d attends encoder rows enc_offsets[d] to enc_offsets[d] + 511 of its stream.
All inputs are finite; a program needn't handle non-finite values.
Results may differ from the reference program's by a relative error of at most 0.034.
The reference program's roundings to bfloat16 on the way count: a program that leaves them out, or rounds other values in their place, can miss the bound.
Values may be sent and summed in bfloat16 or wider, within the bound.
No kernel may reach another device: no remote copies, remote signals or barrier semaphores. Data moves between devices by JAX's collectives and lax.ppermute only.
A program may use at most 320 MiB of HBM per device.

```python
import math
import jax
import jax.numpy as jnp
import numpy as np
from jax import lax

D = 1024
H = 16
DK = 64
FF = 2816
BUCKETS = 32
ENC_ROWS = 512
TOK_DEV = 128
STREAM = 1024
STREAMS = 4
DOCS = 4
DOC_MAX = 682
ENC_ALL = 2048


def draw_doc_ids(key, part):

    def one(index):
        sub = jax.random.fold_in(jax.random.fold_in(key, 7), index)
        first, second = jax.random.split(sub)
        others = DOCS - 1
        rest = STREAM - DOC_MAX
        base = rest // others
        extra = rest - base * others
        shift = jax.random.randint(first, (others,), 0, base // 2 + 1)
        spans = base + shift - jnp.roll(shift, 1)
        spans = spans + jnp.where(jnp.arange(others) == 0, extra, 0)
        spot = jax.random.randint(second, (), 0, DOCS)
        order = jnp.arange(DOCS)
        pick = jnp.clip(order - (order > spot).astype(jnp.int32), 0, others - 1)
        lengths = jnp.where(order == spot, DOC_MAX, spans[pick])
        starts = jnp.cumsum(lengths) - lengths
        places = jnp.arange(STREAM)
        return jnp.sum((places[:, None] >= starts[None, :]).astype(jnp.int32), axis=1) - 1
    return jax.vmap(one)(jnp.arange(STREAMS)).astype(jnp.int32)


def draw_enc_offsets(key, part):

    def one(index):
        sub = jax.random.fold_in(jax.random.fold_in(key, 13), index)
        return ENC_ROWS * jax.random.permutation(sub, jnp.arange(DOCS))
    return jax.vmap(one)(jnp.arange(STREAMS)).astype(jnp.int32)


def level_of(key, shape, pieces, low, high):
    level = 1.0
    for axis_at, parts in pieces:
        steps = jax.random.uniform(jax.random.fold_in(jax.random.fold_in(key, 6), axis_at), (parts,), jnp.float32, low / len(pieces), high / len(pieces))
        level = level * jnp.repeat(jnp.exp(steps), shape[axis_at] // parts).reshape((-1,) + (1,) * (len(shape) - 1 - axis_at))
    return level


def gaussian(stream_key, extent, spread, bound, pieces=(), kind=jnp.bfloat16):
    level = level_of(stream_key, extent, pieces, -0.22, 0.18) if pieces else 1.0
    entries = jax.random.normal(stream_key, extent, jnp.float32) * spread * level
    return jnp.minimum(jnp.maximum(entries, -bound), bound).astype(kind)


def setup_inputs(seed: int = 0) -> dict:
    streams_of = jax.random.split(jax.random.key(seed), 15)
    hidden_in = gaussian(streams_of[0], (STREAMS, STREAM, D), 1.0, 6.0, ((0, 4), (1, 8)))
    encoder_out = gaussian(streams_of[1], (STREAMS, ENC_ALL, D), 1.0, 6.0, ((0, 4), (1, 8)))
    doc_ids = draw_doc_ids(jax.random.fold_in(streams_of[14], 71), 0)
    enc_offsets = draw_enc_offsets(jax.random.fold_in(streams_of[14], 71), 0)
    cotangent = gaussian(streams_of[4], (STREAMS, STREAM, D), 1.0, 6.0, ((0, 4), (1, 8)))
    self_qkv = gaussian(streams_of[5], (D, 3 * H * DK), (4 * D) ** -0.5, 0.09375, ((0, 4),))
    self_out = gaussian(streams_of[6], (H * DK, D), (H * DK // 16) ** -0.5, 0.75, ((0, 4),))
    rel_bias = gaussian(streams_of[7], (BUCKETS, H), 1.0, 4.0, ((0, 4),))
    cross_q = gaussian(streams_of[8], (D, H * DK), (4 * D) ** -0.5, 0.09375, ((0, 4),))
    cross_kv = gaussian(streams_of[9], (D, 2 * H * DK), (4 * D) ** -0.5, 0.09375, ((0, 4),))
    cross_out = gaussian(streams_of[10], (H * DK, D), (H * DK // 16) ** -0.5, 0.75, ((0, 4),))
    ffn_in = gaussian(streams_of[11], (D, 2 * FF), D ** -0.5, 0.1875, ((0, 4),))
    ffn_out = gaussian(streams_of[12], (FF, D), FF ** -0.5, 0.109375, ((0, 4),))
    norm_gains = jnp.clip(1.0 + 0.1 * jax.random.normal(streams_of[13], (3, D), jnp.float32), 0.5, 1.5).astype(jnp.bfloat16)
    return {"hidden_in": hidden_in, "encoder_out": encoder_out, "doc_ids": doc_ids, "enc_offsets": enc_offsets, "cotangent": cotangent, "self_qkv": self_qkv, "self_out": self_out, "rel_bias": rel_bias, "cross_q": cross_q, "cross_kv": cross_kv, "cross_out": cross_out, "ffn_in": ffn_in, "ffn_out": ffn_out, "norm_gains": norm_gains}


@jax.custom_vjp
def low(v):
    return lax.optimization_barrier(v.astype(jnp.bfloat16)).astype(jnp.float32)

@jax.custom_vjp
def low_back(v):
    return v

def low_keep(v):
    return (low(v), None)

def low_pass(kept, grad):
    return (grad,)

def back_keep(v):
    return (v, None)

def back_low(kept, grad):
    return (low(grad),)
low.defvjp(low_keep, low_pass)
low_back.defvjp(back_keep, back_low)
EDGES = np.ceil(16.0 * 8.0 ** (np.arange(1, 16) / 16.0)).astype(np.int32)
HIGH = lax.Precision.HIGHEST
NEG = -1e+30

def bucket_ids(distance):
    steps = jnp.maximum(distance, 0)
    far = 16 + lax.optimization_barrier(jnp.sum((steps[..., None] >= jnp.asarray(EDGES)).astype(jnp.int32), axis=-1))
    return jnp.where(steps < 16, steps, far).astype(jnp.int32)

def rms_norm(value, gain):
    return value * lax.rsqrt(lax.optimization_barrier(jnp.mean(value * value, axis=-1, keepdims=True)) + 1e-06) * gain

def matmul(left, right):
    return jnp.dot(left, right, precision=HIGH)

def rounded_both(value):
    return low(low_back(value))

def masked_softmax(score, mask):
    masked = jnp.where(mask[None], score, NEG)
    top = lax.optimization_barrier(jnp.max(masked, axis=-1, keepdims=True))
    weights = jnp.where(mask[None], jnp.exp(masked - top), 0.0)
    return weights / lax.optimization_barrier(jnp.sum(weights, axis=-1, keepdims=True))

def mirrored_places(length):
    rows = jnp.arange(length, dtype=jnp.int32)
    half = TOK_DEV // 2
    groups = length // TOK_DEV
    group = rows // TOK_DEV
    within = rows % TOK_DEV
    return jnp.where(within < half, group * half + within, (2 * groups - 1 - group) * half + within - half).astype(jnp.int32)

def stream_forward(params, hidden, encoder, ids, offsets):
    w_qkv, w_out, table, w_cq, w_ckv, w_cout, w_in, w_down, gains = params
    length = hidden.shape[0]
    width = H * DK
    places = mirrored_places(length)
    row_docs = ids[places]
    block = math.gcd(512, length)
    count = length // block
    low1 = low(rms_norm(hidden, gains[0]))
    proj = rounded_both(matmul(low1, w_qkv))
    query = proj[:, :width].reshape(length, H, DK)
    keys = proj[:, width:2 * width].reshape(length, H, DK)
    values = proj[:, 2 * width:].reshape(length, H, DK)

    def self_block(item):
        q_rows, q_places, q_docs = item
        score = jnp.einsum('qhd,khd->hqk', q_rows, keys, precision=HIGH)
        bias = table[bucket_ids(q_places[:, None] - places[None, :])]
        score = low_back(score + jnp.transpose(bias, (2, 0, 1)))
        mask = (q_docs[:, None] == row_docs[None, :]) & (places[None, :] <= q_places[:, None])
        probs = low(masked_softmax(score, mask))
        return jnp.einsum('hqk,khd->qhd', probs, values, precision=HIGH)
    attended = lax.map(jax.checkpoint(self_block), (query.reshape(count, block, H, DK), places.reshape(count, block), row_docs.reshape(count, block)))
    attended = rounded_both(attended.reshape(length, width))
    mid = hidden + low_back(matmul(attended, w_out))
    low2 = low(rms_norm(mid, gains[1]))
    cross_query = rounded_both(matmul(low2, w_cq)).reshape(length, H, DK)
    pairs = rounded_both(matmul(encoder, w_ckv))
    rows = encoder.shape[0]
    cross_keys = pairs[:, :width].reshape(rows, H, DK)
    cross_values = pairs[:, width:].reshape(rows, H, DK)
    row_ids = jnp.arange(rows, dtype=jnp.int32)
    starts = offsets[row_docs]

    def cross_block(item):
        q_rows, q_starts = item
        score = low_back(jnp.einsum('qhd,khd->hqk', q_rows, cross_keys, precision=HIGH))
        mask = (row_ids[None, :] >= q_starts[:, None]) & (row_ids[None, :] < q_starts[:, None] + ENC_ROWS)
        probs = low(masked_softmax(score, mask))
        return jnp.einsum('hqk,khd->qhd', probs, cross_values, precision=HIGH)
    crossed = lax.map(jax.checkpoint(cross_block), (cross_query.reshape(count, block, H, DK), starts.reshape(count, block)))
    crossed = rounded_both(crossed.reshape(length, width))
    late = mid + low_back(matmul(crossed, w_cout))
    low3 = low(rms_norm(late, gains[2]))
    gate_up = low_back(matmul(low3, w_in))
    act = low(jax.nn.gelu(gate_up[:, :FF], approximate=True) * gate_up[:, FF:])
    return late + low_back(matmul(act, w_down))

def reference(hidden_in, encoder_out, doc_ids, enc_offsets, cotangent, self_qkv, self_out, rel_bias, cross_q, cross_kv, cross_out, ffn_in, ffn_out, norm_gains):
    params = tuple((p.astype(jnp.float32) for p in (self_qkv, self_out, rel_bias, cross_q, cross_kv, cross_out, ffn_in, ffn_out, norm_gains)))

    def one_stream(acc, item):
        hidden, encoder, ids, offsets, grad_out = item

        def forward(weights, rows, enc_rows):
            return stream_forward(weights, rows, enc_rows, ids, offsets)
        result, pull = jax.vjp(forward, params, hidden.astype(jnp.float32), encoder.astype(jnp.float32))
        grad_params, grad_rows, grad_enc = pull(grad_out.astype(jnp.float32))
        acc = jax.tree.map(lambda left, right: left + right, acc, grad_params)
        return (acc, (result.astype(jnp.bfloat16), grad_rows, grad_enc))
    start = tuple((jnp.zeros_like(p) for p in params))
    grads, (results, grad_rows, grad_enc) = lax.scan(one_stream, start, (hidden_in, encoder_out, doc_ids, enc_offsets, cotangent))
    return (results, grad_rows, grad_enc, grads[0], grads[1], grads[2], grads[3], grads[4], grads[5], grads[6], grads[7], grads[8])
```

```python
import functools
import math

import jax
import jax.numpy as jnp
import numpy as np
from jax import lax
from jax.experimental import pallas as pl
from jax.experimental.pallas import tpu as pltpu
from jax.sharding import PartitionSpec as P

D = 1024
H = 16
DK = 64
FF = 2816
BUCKETS = 32
ENC_ROWS = 512
QB = 128
NEG = -1e30
EPSILON = 1e-06
BF = jnp.bfloat16
F32 = jnp.float32

EDGES = np.ceil(16.0 * 8.0 ** (np.arange(1, 16) / 16.0)).astype(np.int32)


def near_buckets():
    steps = np.arange(2)[:, None, None] * QB + np.arange(QB)[None, None, :] - np.arange(QB)[None, :, None]
    steps = np.maximum(steps, 0)
    far = 16 + np.sum(steps[..., None] >= EDGES, axis=-1)
    return np.where(steps < 16, steps, far).astype(np.int32)


def dot(a, b):
    return jnp.dot(a, b, preferred_element_type=F32)


def dot_nt(a, b):
    return lax.dot_general(a, b, (((1,), (1,)), ((), ())), preferred_element_type=F32)


def dot_tn(a, b):
    return lax.dot_general(a, b, (((0,), (0,)), ((), ())), preferred_element_type=F32)


def send(value, axis, count, target):
    return lax.ppermute(value, axis, [(i, target(i)) for i in range(count)])


def first_way(i):
    return i ^ 2 if i % 2 == 0 else i ^ 4


def second_way(i):
    return i ^ 4 if i % 2 == 0 else i ^ 2


def ctx_order(me, count):
    if count == 8:
        even = (me % 2) == 0
        one, two = jnp.where(even, 2, 4), jnp.where(even, 4, 2)
        rel = [0, one, two, 6, 1, jnp.where(even, 5, 3), jnp.where(even, 3, 5), 7]
    else:
        rel = list(range(count))
    return [me ^ r for r in rel]


def ctx_gather(value, count):
    if count == 8:
        near, other = send(value, "ctx", 8, first_way), send(value, "ctx", 8, second_way)
        far = send(near, "ctx", 8, second_way)
        mine = [value, near, other, far]
        return mine + [send(v, "ctx", 8, lambda i: i ^ 1) for v in mine]
    return [value] + [send(value, "ctx", count, lambda i, d=d: i ^ d) for d in range(1, count)]


def ctx_reduce(pieces, count):
    if count == 8:
        theirs = send(jnp.stack([pieces[d ^ 1] for d in (0, 2, 4, 6)]), "ctx", 8, lambda i: i ^ 1)
        pairs = [pieces[d].astype(F32) + theirs[k].astype(F32) for k, d in enumerate((0, 2, 4, 6))]
        total = pairs[0]
        for k, d in ((3, 6), (1, 2), (2, 4)):
            total = total + send(pairs[k].astype(BF), "ctx", 8, lambda i, d=d: i ^ d).astype(F32)
        return total
    total = pieces[0].astype(F32)
    for d in range(1, count):
        total = total + send(pieces[d], "ctx", count, lambda i, d=d: i ^ d).astype(F32)
    return total


def stack_heads(rows, heads):
    if heads == 1:
        return rows
    lane = lax.broadcasted_iota(jnp.int32, rows.shape, 1) // DK
    return jnp.concatenate([jnp.where(lane == h, rows, jnp.zeros_like(rows)) for h in range(heads)], axis=0)


def unstack_heads(cols, heads):
    parts = [cols[h * DK : (h + 1) * DK, h * QB : (h + 1) * QB] for h in range(heads)]
    return jnp.concatenate(parts, axis=0).T if heads > 1 else parts[0].T


def tile_lanes(row, heads):
    return jnp.concatenate([row] * heads, axis=1) if heads > 1 else row


def self_scores(q_ref, k_ref, near_ref, start_ref, block, heads):
    rows = pl.ds(block * QB, QB)
    stacked = stack_heads(q_ref[rows, :], heads)
    starts = tile_lanes(start_ref[:, rows], heads)
    tiles = []
    for kb in range(block + 1):
        score = dot_nt(k_ref[pl.ds(kb * QB, QB), :], stacked)
        if block - kb < 2:
            score = score + near_ref[block - kb]
        at = lax.broadcasted_iota(jnp.int32, score.shape, 0) + kb * QB
        keep = at >= starts
        if kb == block:
            lane = lax.broadcasted_iota(jnp.int32, score.shape, 1) % QB + block * QB
            keep = keep & (at <= lane)
        tiles.append(jnp.where(keep, score, NEG))
    return stacked, tiles


def self_forward_kernel(heads, q_ref, k_ref, v_ref, near_ref, start_ref, o_ref, lse_ref, vt_ref):
    stream = q_ref.shape[0]
    vt_ref[...] = v_ref[...].T
    for block in range(stream // QB):
        _, tiles = self_scores(q_ref, k_ref, near_ref, start_ref, block, heads)
        top = functools.reduce(jnp.maximum, [jnp.max(t, axis=0, keepdims=True) for t in tiles])
        tiles = [jnp.exp(t - top) for t in tiles]
        total = functools.reduce(jnp.add, [jnp.sum(t, axis=0, keepdims=True) for t in tiles])
        inverse = 1.0 / total
        probs = jnp.concatenate([(t * inverse).astype(BF) for t in tiles], axis=0)
        out = dot(vt_ref[:, pl.ds(0, (block + 1) * QB)], probs)
        o_ref[pl.ds(block * QB, QB), :] = unstack_heads(out, heads).astype(BF)
        lse_ref[:, pl.ds(block * QB * heads, QB * heads)] = top + jnp.log(total)


def self_forward(q, k, v, near, starts, heads):
    stream, width = q.shape
    return pl.pallas_call(
        functools.partial(self_forward_kernel, heads),
        out_shape=(
            jax.ShapeDtypeStruct((stream, width), BF),
            jax.ShapeDtypeStruct((1, stream * heads), F32),
        ),
        scratch_shapes=[pltpu.VMEM((width, stream), BF)],
        compiler_params=pltpu.CompilerParams(vmem_limit_bytes=48 << 20),
        cost_estimate=pl.CostEstimate(flops=2 * stream * stream * width, bytes_accessed=8 * stream * width, transcendentals=stream * stream * heads // 2),
        name="self_forward",
    )(q, k, v, near, starts)


def self_backward_kernel(heads, q_ref, k_ref, v_ref, do_ref, lse_ref, near_ref, start_ref, dq_ref, dk_ref, dv_ref, dnear_ref, dfar_ref, ds_ref, p_ref, kt_ref):
    stream = q_ref.shape[0]
    blocks = stream // QB
    kt_ref[...] = k_ref[...].T
    near = [jnp.zeros((QB, heads * QB), F32)] * 2
    far = jnp.zeros((1, heads * QB), F32)
    for block in range(blocks):
        lanes = pl.ds(block * QB * heads, QB * heads)
        _, tiles = self_scores(q_ref, k_ref, near_ref, start_ref, block, heads)
        douts = stack_heads(do_ref[pl.ds(block * QB, QB), :], heads)
        lse = lse_ref[:, lanes]
        probs = [jnp.exp(t - lse) for t in tiles]
        dprobs = [dot_nt(v_ref[pl.ds(kb * QB, QB), :], douts) for kb in range(block + 1)]
        delta = functools.reduce(jnp.add, [jnp.sum(a * b, axis=0, keepdims=True) for a, b in zip(probs, dprobs)])
        for kb in range(block + 1):
            dscore = (probs[kb] * (dprobs[kb] - delta)).astype(BF)
            ds_ref[pl.ds(kb * QB, QB), lanes] = dscore
            p_ref[pl.ds(kb * QB, QB), lanes] = probs[kb].astype(BF)
            wide = dscore.astype(F32)
            if block - kb < 2:
                near[block - kb] = near[block - kb] + wide
            else:
                far = far + jnp.sum(wide, axis=0, keepdims=True)
        dq = dot(kt_ref[:, pl.ds(0, (block + 1) * QB)], ds_ref[pl.ds(0, (block + 1) * QB), lanes])
        dq_ref[pl.ds(block * QB, QB), :] = unstack_heads(dq, heads).astype(BF)
    dnear_ref[0] = near[0]
    dnear_ref[1] = near[1]
    dfar_ref[...] = far
    queries = jnp.concatenate([stack_heads(q_ref[pl.ds(b * QB, QB), :], heads) for b in range(blocks)], axis=0)
    douts = jnp.concatenate([stack_heads(do_ref[pl.ds(b * QB, QB), :], heads) for b in range(blocks)], axis=0)
    for kb in range(blocks):
        rows, lanes = pl.ds(kb * QB, QB), pl.ds(kb * QB * heads, (blocks - kb) * QB * heads)
        dk_ref[rows, :] = dot(ds_ref[rows, lanes], queries[kb * QB * heads :]).astype(BF)
        dv_ref[rows, :] = dot(p_ref[rows, lanes], douts[kb * QB * heads :]).astype(BF)


def self_backward(q, k, v, do, lse, near, starts, heads):
    stream, width = q.shape
    row = jax.ShapeDtypeStruct((stream, width), BF)
    return pl.pallas_call(
        functools.partial(self_backward_kernel, heads),
        out_shape=(row, row, row, jax.ShapeDtypeStruct((2, QB, heads * QB), F32), jax.ShapeDtypeStruct((1, heads * QB), F32)),
        scratch_shapes=[
            pltpu.VMEM((stream, stream * heads), BF),
            pltpu.VMEM((stream, stream * heads), BF),
            pltpu.VMEM((width, stream), BF),
        ],
        compiler_params=pltpu.CompilerParams(vmem_limit_bytes=56 << 20),
        cost_estimate=pl.CostEstimate(flops=5 * stream * stream * width, bytes_accessed=16 * stream * width, transcendentals=stream * stream * heads // 2),
        name="self_backward",
    )(q, k, v, do, lse, near, starts)


def cross_forward_kernel(heads, count_ref, blocks_ref, docs_ref, offs_ref, q_ref, k_ref, v_ref, doc_ref, o_ref, lse_ref, vt_ref, acc_ref, norm_ref):
    stream = q_ref.shape[0]
    for part in range(v_ref.shape[0] // ENC_ROWS):
        vt_ref[part] = v_ref[pl.ds(part * ENC_ROWS, ENC_ROWS), :].T
    acc_ref[...] = jnp.zeros_like(acc_ref)
    norm_ref[...] = jnp.zeros_like(norm_ref)

    def step(t, carry):
        block, doc, off = blocks_ref[t], docs_ref[t], offs_ref[t]
        stacked = stack_heads(q_ref[pl.ds(pl.multiple_of(block * QB, QB), QB), :], heads)
        keys = k_ref[pl.ds(pl.multiple_of(off * ENC_ROWS, ENC_ROWS), ENC_ROWS), :]
        score = dot_nt(keys, stacked)
        top = jnp.max(score, axis=0, keepdims=True)
        weights = jnp.exp(score - top)
        total = jnp.sum(weights, axis=0, keepdims=True)
        probs = (weights * (1.0 / total)).astype(BF)
        out = dot(vt_ref[off], probs)
        mine = tile_lanes(doc_ref[block], heads) == doc
        acc_ref[block] = jnp.where(mine, out, acc_ref[block])
        norm_ref[block] = jnp.where(mine, top + jnp.log(total), norm_ref[block])
        return carry

    lax.fori_loop(0, count_ref[0], step, 0)
    for block in range(stream // QB):
        o_ref[pl.ds(block * QB, QB), :] = unstack_heads(acc_ref[block], heads).astype(BF)
    lse_ref[...] = norm_ref[...]


def cross_forward(work, q, k, v, docs, heads):
    stream, width = q.shape
    rows = k.shape[0]
    smem = pl.BlockSpec(memory_space=pltpu.SMEM)
    vmem = pl.BlockSpec(memory_space=pltpu.VMEM)
    return pl.pallas_call(
        functools.partial(cross_forward_kernel, heads),
        in_specs=[smem] * 4 + [vmem] * 4,
        out_shape=(
            jax.ShapeDtypeStruct((stream, width), BF),
            jax.ShapeDtypeStruct((stream // QB, 1, QB * heads), F32),
        ),
        scratch_shapes=[
            pltpu.VMEM((rows // ENC_ROWS, width, ENC_ROWS), BF),
            pltpu.VMEM((stream // QB, width, QB * heads), F32),
            pltpu.VMEM((stream // QB, 1, QB * heads), F32),
        ],
        compiler_params=pltpu.CompilerParams(vmem_limit_bytes=48 << 20),
        cost_estimate=pl.CostEstimate(flops=2 * stream * ENC_ROWS * width * 2, bytes_accessed=8 * stream * width, transcendentals=stream * ENC_ROWS * heads),
        name="cross_forward",
    )(*work, q, k, v, docs)


def cross_backward_kernel(heads, count_ref, blocks_ref, docs_ref, offs_ref, q_ref, k_ref, v_ref, do_ref, doc_ref, lse_ref, dq_ref, dk_ref, dv_ref, kt_ref, acc_ref, dka_ref, dva_ref):
    stream = q_ref.shape[0]
    for part in range(k_ref.shape[0] // ENC_ROWS):
        kt_ref[part] = k_ref[pl.ds(part * ENC_ROWS, ENC_ROWS), :].T
    acc_ref[...] = jnp.zeros_like(acc_ref)
    dka_ref[...] = jnp.zeros_like(dka_ref)
    dva_ref[...] = jnp.zeros_like(dva_ref)

    def step(t, carry):
        block, doc, off = blocks_ref[t], docs_ref[t], offs_ref[t]
        at = pl.ds(pl.multiple_of(block * QB, QB), QB)
        enc = pl.ds(pl.multiple_of(off * ENC_ROWS, ENC_ROWS), ENC_ROWS)
        stacked, douts = stack_heads(q_ref[at, :], heads), stack_heads(do_ref[at, :], heads)
        mine = tile_lanes(doc_ref[block], heads) == doc
        probs = jnp.where(mine, jnp.exp(dot_nt(k_ref[enc, :], stacked) - lse_ref[block]), 0.0)
        dprobs = dot_nt(v_ref[enc, :], douts)
        delta = jnp.sum(probs * dprobs, axis=0, keepdims=True)
        dscore = (probs * (dprobs - delta)).astype(BF)
        acc_ref[block] += dot(kt_ref[off], dscore)
        dka_ref[enc, :] += dot(dscore, stacked)
        dva_ref[enc, :] += dot(probs.astype(BF), douts)
        return carry

    lax.fori_loop(0, count_ref[0], step, 0)
    for block in range(stream // QB):
        dq_ref[pl.ds(block * QB, QB), :] = unstack_heads(acc_ref[block], heads).astype(BF)
    dk_ref[...] = dka_ref[...].astype(BF)
    dv_ref[...] = dva_ref[...].astype(BF)


def cross_backward(work, q, k, v, do, docs, lse, heads):
    stream, width = q.shape
    rows = k.shape[0]
    smem = pl.BlockSpec(memory_space=pltpu.SMEM)
    vmem = pl.BlockSpec(memory_space=pltpu.VMEM)
    return pl.pallas_call(
        functools.partial(cross_backward_kernel, heads),
        in_specs=[smem] * 4 + [vmem] * 6,
        out_shape=(
            jax.ShapeDtypeStruct((stream, width), BF),
            jax.ShapeDtypeStruct((rows, width), BF),
            jax.ShapeDtypeStruct((rows, width), BF),
        ),
        scratch_shapes=[
            pltpu.VMEM((rows // ENC_ROWS, width, ENC_ROWS), BF),
            pltpu.VMEM((stream // QB, width, QB * heads), F32),
            pltpu.VMEM((rows, width), F32),
            pltpu.VMEM((rows, width), F32),
        ],
        compiler_params=pltpu.CompilerParams(vmem_limit_bytes=48 << 20),
        cost_estimate=pl.CostEstimate(flops=5 * stream * ENC_ROWS * width * 2, bytes_accessed=16 * stream * width, transcendentals=stream * ENC_ROWS * heads),
        name="cross_backward",
    )(*work, q, k, v, do, docs, lse)


def norm_forward(value, gain):
    scale = lax.rsqrt(jnp.mean(value * value, axis=-1, keepdims=True) + EPSILON)
    return (value * scale * gain).astype(BF)


def norm_backward(grad, value, gain):
    scale = lax.rsqrt(jnp.mean(value * value, axis=-1, keepdims=True) + EPSILON)
    normed = value * scale
    dnormed = grad * gain
    dvalue = scale * (dnormed - normed * jnp.mean(dnormed * normed, axis=-1, keepdims=True))
    return (dvalue, jnp.sum(grad * normed, axis=0, keepdims=True))


def activation(gate, up):
    return jax.nn.gelu(gate, approximate=True) * up


def body(
    hidden_in,
    encoder_out,
    doc_ids,
    enc_offsets,
    cotangent,
    self_qkv,
    self_out,
    rel_bias,
    cross_q,
    cross_kv,
    cross_out,
    ffn_in,
    ffn_out,
    norm_gains,
):
    count, depth = lax.axis_size("ctx"), lax.axis_size("fsdp")
    me = lax.axis_index("ctx")
    tokens = hidden_in.shape[1]
    half = tokens // 2
    stream = tokens * count
    width = H * DK // count
    heads = H // count
    slab = D // depth
    piece = FF // (depth * count)
    order = ctx_order(me, count)

    def by_position(pieces):
        rows = jnp.zeros((2 * count, half, D), BF)
        for source, rows_in in zip(order, pieces):
            rows = lax.dynamic_update_slice(rows, rows_in[None, :half], (source, 0, 0))
            rows = lax.dynamic_update_slice(rows, rows_in[None, half:], (2 * count - 1 - source, 0, 0))
        return rows.reshape(stream, D)

    def by_column(pieces):
        cols = jnp.zeros((stream, H * DK), BF)
        for source, cols_in in zip(order, pieces):
            cols = lax.dynamic_update_slice(cols, cols_in, (0, source * width))
        return cols

    def rows_of(value, device):
        low = lax.dynamic_slice_in_dim(value, device * half, half)
        high = lax.dynamic_slice_in_dim(value, (2 * count - 1 - device) * half, half)
        return jnp.concatenate([low, high], axis=0)

    def reduce_rows(value):
        return ctx_reduce([rows_of(value, me ^ d) for d in range(count)], count)

    def columns(value, start, size):
        return lax.dynamic_slice_in_dim(value, start, size, 1)

    def gather_z(value):
        return lax.all_gather(value, "fsdp", axis=0, tiled=True)

    own = me * width
    w_qkv = gather_z(jnp.concatenate([columns(self_qkv, p * H * DK + own, width) for p in range(3)], axis=1))
    mixed = jnp.concatenate([self_out, cross_q, cross_out], axis=1)
    w_mixed = gather_z(jnp.concatenate([columns(mixed, p * D + own, width) for p in range(3)], axis=1))
    w_ckv = gather_z(jnp.concatenate([columns(cross_kv, p * H * DK + own, width) for p in range(2)], axis=1))
    picks = [g * FF + z * (FF // depth) for g in range(2) for z in range(depth)]
    w_in = gather_z(jnp.concatenate([columns(ffn_in, p + me * piece, piece) for p in picks], axis=1))
    w_down = gather_z(lax.dynamic_slice_in_dim(ffn_out, me * piece, piece))
    table = gather_z(rel_bias).astype(F32)
    gains = lax.all_gather(norm_gains, "fsdp", axis=1, tiled=True).astype(F32)
    full = lax.all_gather(w_mixed, "ctx", axis=0)
    w_out, w_cq, w_cout = [
        jnp.transpose(full[:, :, p * width : (p + 1) * width], (1, 0, 2)).reshape(D, D) for p in range(3)
    ]

    ids = doc_ids[0]
    offsets = enc_offsets[0]
    docs = offsets.shape[0]
    doc_range = jnp.arange(docs, dtype=jnp.int32)
    doc_starts = jnp.sum((ids[None, :] < doc_range[:, None]).astype(jnp.int32), axis=1)
    starts = jnp.sum(jnp.where(ids[None, :] == doc_range[:, None], doc_starts[:, None], 0), axis=0)[None]
    q_blocks = stream // QB
    first_doc = ids[:: QB]
    last_doc = ids[QB - 1 :: QB]
    spans = last_doc - first_doc + 1
    at_or_before = np.arange(q_blocks)[:, None] >= np.arange(q_blocks)[None, :]
    ends = jnp.sum(jnp.where(at_or_before, spans[None, :], 0), axis=1)
    slots = jnp.arange(q_blocks + docs, dtype=jnp.int32)
    slot_block = jnp.minimum(jnp.sum((slots[:, None] >= ends[None, :]).astype(jnp.int32), axis=1), q_blocks - 1)
    in_block = slot_block[:, None] == jnp.arange(q_blocks)[None, :]
    slot_doc = slots + jnp.sum(jnp.where(in_block, (first_doc - ends + spans)[None, :], 0), axis=1)
    slot_doc = jnp.clip(slot_doc, 0, docs - 1)
    slot_part = jnp.sum(jnp.where(slot_doc[:, None] == doc_range[None, :], (offsets // ENC_ROWS)[None, :], 0), axis=1)
    work = (jnp.sum(spans)[None], slot_block, slot_doc, slot_part)
    doc_rows = ids.reshape(q_blocks, 1, QB)

    mine = lax.dynamic_slice_in_dim(table, me * heads, heads, 1)
    mine = mine - mine[BUCKETS - 1 :]
    near_ids = jnp.asarray(near_buckets())
    onehot = (near_ids[..., None] == jnp.arange(BUCKETS, dtype=jnp.int32)).astype(F32)
    near = jnp.einsum("akqb,bh->akhq", onehot, mine, precision=lax.Precision.HIGHEST).reshape(2, QB, heads * QB)

    x = by_position(ctx_gather(hidden_in[0], count)).astype(F32)
    h1 = norm_forward(x, gains[0])
    qkv = dot(h1, w_qkv).astype(BF)
    query, key, value = [qkv[:, p * width : (p + 1) * width] for p in range(3)]
    attended, lse = self_forward(query, key, value, near, starts, heads)
    ob = by_column(ctx_gather(attended, count))
    x1 = x + dot(ob, w_out)
    h2 = norm_forward(x1, gains[1])
    cquery = dot(h2, w_mixed[:, width : 2 * width]).astype(BF)
    enc = lax.all_gather(encoder_out[0], "ctx", axis=0, tiled=True)
    kvc = dot(enc, w_ckv).astype(BF)
    ckey, cvalue = kvc[:, :width], kvc[:, width:]
    crossed, clse = cross_forward(work, cquery, ckey, cvalue, doc_rows, heads)
    ocb = by_column(ctx_gather(crossed, count))
    x2 = x1 + dot(ocb, w_cout)
    h3 = norm_forward(x2, gains[2])
    gate_up = dot(h3, w_in)
    gate, up = gate_up[:, : piece * depth], gate_up[:, piece * depth :]
    act = activation(gate, up).astype(BF)
    x2_own = rows_of(x2, me)
    result = (x2_own + reduce_rows(dot(act, w_down).astype(BF))).astype(BF)

    g = by_position(ctx_gather(cotangent[0], count))
    grad_down = dot_tn(act, g).astype(BF)
    dact = dot_nt(g, w_down)
    _, pull = jax.vjp(activation, gate, up)
    dgu = jnp.concatenate(pull(dact), axis=1).astype(BF)
    grad_in = dot_tn(h3, dgu).astype(BF)
    dh3 = reduce_rows(dot_nt(dgu, w_in).astype(BF))
    dx2, dgain3 = norm_backward(dh3, x2_own, gains[2])
    gx2_own = cotangent[0].astype(F32) + dx2
    gb2 = by_position(ctx_gather(gx2_own.astype(BF), count))
    grad_cout = dot_tn(ocb, columns(gb2, own, width)).astype(BF)
    dcross = dot_nt(gb2, lax.dynamic_slice_in_dim(w_cout, own, width)).astype(BF)
    dcq, dck, dcv = cross_backward(work, cquery, ckey, cvalue, dcross, doc_rows, clse, heads)
    dkvc = jnp.concatenate([dck, dcv], axis=1)
    grad_ckv = dot_tn(enc, dkvc).astype(BF)
    grad_enc = lax.psum_scatter(dot_nt(dkvc, w_ckv).astype(BF), "ctx", scatter_dimension=0, tiled=True).astype(F32)
    grad_cq = dot_tn(h2, dcq).astype(BF)
    dh2 = dot_nt(by_column(ctx_gather(dcq, count)), w_cq)
    dx1, dgain2 = norm_backward(dh2, x1, gains[1])
    gx1_own = gx2_own + rows_of(dx1, me)
    gb1 = (gb2.astype(F32) + dx1).astype(BF)
    grad_out = dot_tn(ob, columns(gb1, own, width)).astype(BF)
    dattn = dot_nt(gb1, lax.dynamic_slice_in_dim(w_out, own, width)).astype(BF)
    dq, dk, dv, dnear, dfar = self_backward(query, key, value, dattn, lse, near, starts, heads)
    dqkv = jnp.concatenate([dq, dk, dv], axis=1)
    grad_qkv = dot_tn(h1, dqkv).astype(BF)
    dh1 = reduce_rows(dot_nt(dqkv, w_qkv).astype(BF))
    dx, dgain1 = norm_backward(dh1, hidden_in[0].astype(F32), gains[0])
    grad_hidden = gx1_own + dx

    dnear = dnear.reshape(2, QB, heads, QB)
    dtable = jnp.einsum("akqb,akhq->bh", onehot, dnear, precision=lax.Precision.HIGHEST)
    far = jnp.sum(dfar.reshape(heads, QB), axis=1)
    dtable = dtable + jnp.where(jnp.arange(BUCKETS)[:, None] == BUCKETS - 1, far[None, :], 0.0)
    dtable = lax.psum_scatter(dtable.astype(BF), "fsdp", scatter_dimension=0, tiled=True)
    grad_table = lax.all_gather(dtable, "ctx", axis=1, tiled=True).astype(F32)
    dgain2 = jnp.where(me == 0, dgain2, 0.0)
    dgains = jnp.concatenate([dgain1, dgain2, dgain3], axis=0)
    dgains = lax.psum_scatter(dgains.astype(BF), "fsdp", scatter_dimension=1, tiled=True)
    grad_gains = lax.psum(dgains, "ctx").astype(F32)

    def finish(value):
        part = lax.psum_scatter(value, "fsdp", scatter_dimension=0, tiled=True)
        return lax.all_gather(part, "ctx", axis=0)

    def side_by_side(parts, groups):
        parts = parts.reshape(count, slab, groups, -1)
        return jnp.transpose(parts, (1, 2, 0, 3)).reshape(slab, -1).astype(F32)

    grad_self_qkv = side_by_side(finish(grad_qkv), 3)
    grad_self_out = side_by_side(finish(grad_out), 1)
    grad_cross_q = side_by_side(finish(grad_cq), 1)
    grad_cross_kv = side_by_side(finish(grad_ckv), 2)
    grad_cross_out = side_by_side(finish(grad_cout), 1)
    grad_ffn_in = side_by_side(finish(grad_in), 2 * depth)
    grad_ffn_out = finish(grad_down).reshape(FF // depth, D).astype(F32)
    return (
        result[None],
        grad_hidden[None],
        grad_enc[None],
        grad_self_qkv,
        grad_self_out,
        grad_table,
        grad_cross_q,
        grad_cross_kv,
        grad_cross_out,
        grad_ffn_in,
        grad_ffn_out,
        grad_gains,
    )


def solution(mesh):
    split = P("fsdp", "ctx", None)
    rows = P("fsdp", None)
    return jax.shard_map(
        body,
        mesh=mesh,
        in_specs=(split, split, rows, rows, split) + (rows,) * 8 + (P(None, "fsdp"),),
        out_specs=(split,) * 3 + (rows,) * 8 + (P(None, "fsdp"),),
        check_vma=False,
    )
```

```python
import functools
import math

import jax
import jax.numpy as jnp
import numpy as np
from jax import lax
from jax.experimental import pallas as pl
from jax.experimental.pallas import tpu as pltpu
from jax.sharding import PartitionSpec as P

D = 1024
H = 16
DK = 64
FF = 2816
BUCKETS = 32
ENC_ROWS = 512
QB = 128
NEG = -1e30
EPSILON = 1e-06
BF = jnp.bfloat16
F32 = jnp.float32

EDGES = np.ceil(16.0 * 8.0 ** (np.arange(1, 16) / 16.0)).astype(np.int32)


def near_buckets():
    steps = np.arange(2)[:, None, None] * QB + np.arange(QB)[None, None, :] - np.arange(QB)[None, :, None]
    steps = np.maximum(steps, 0)
    far = 16 + np.sum(steps[..., None] >= EDGES, axis=-1)
    return np.where(steps < 16, steps, far).astype(np.int32)


def dot(a, b):
    return jnp.dot(a, b, preferred_element_type=F32)


def dot_nt(a, b):
    return lax.dot_general(a, b, (((1,), (1,)), ((), ())), preferred_element_type=F32)


def dot_tn(a, b):
    return lax.dot_general(a, b, (((0,), (0,)), ((), ())), preferred_element_type=F32)


def send(value, axis, count, target):
    return lax.ppermute(value, axis, [(i, target(i)) for i in range(count)])


def first_way(i):
    return i ^ 2 if i % 2 == 0 else i ^ 4


def second_way(i):
    return i ^ 4 if i % 2 == 0 else i ^ 2


def ctx_order(me, count):
    if count == 8:
        even = (me % 2) == 0
        one, two = jnp.where(even, 2, 4), jnp.where(even, 4, 2)
        rel = [0, one, two, 6, 1, jnp.where(even, 5, 3), jnp.where(even, 3, 5), 7]
    else:
        rel = list(range(count))
    return [me ^ r for r in rel]


def ctx_gather(value, count):
    if count == 8:
        near, other = send(value, "ctx", 8, first_way), send(value, "ctx", 8, second_way)
        far = send(near, "ctx", 8, second_way)
        mine = [value, near, other, far]
        return mine + [send(v, "ctx", 8, lambda i: i ^ 1) for v in mine]
    return [value] + [send(value, "ctx", count, lambda i, d=d: i ^ d) for d in range(1, count)]


def ctx_reduce(keep, away, count):
    if count == 8:
        theirs = send(away, "ctx", 8, lambda i: i ^ 1)
        pairs = keep.astype(F32) + theirs.astype(F32)
        low = pairs.astype(BF)
        return pairs[0], [send(low[d // 2], "ctx", 8, lambda i, d=d: i ^ d) for d in (6, 2, 4)]
    return keep[0].astype(F32), [send(keep[d], "ctx", count, lambda i, d=d: i ^ d) for d in range(1, count)]


def z_gather(value, depth):
    return [value] + [send(value, "fsdp", depth, lambda i, d=d: i ^ d) for d in range(1, depth)]


def stack_heads(rows, heads):
    if heads == 1:
        return rows
    lane = lax.broadcasted_iota(jnp.int32, rows.shape, 1) // DK
    return jnp.concatenate([jnp.where(lane == h, rows, jnp.zeros_like(rows)) for h in range(heads)], axis=0)


def unstack_heads(cols, heads):
    parts = [cols[h * DK : (h + 1) * DK, h * QB : (h + 1) * QB] for h in range(heads)]
    return jnp.concatenate(parts, axis=0).T if heads > 1 else parts[0].T


def tile_lanes(row, heads):
    return jnp.concatenate([row] * heads, axis=1) if heads > 1 else row


def self_scores(q_ref, k_ref, near_ref, start_ref, block, heads):
    rows = pl.ds(block * QB, QB)
    stacked = stack_heads(q_ref[rows, :], heads)
    starts = tile_lanes(start_ref[:, rows], heads)
    tiles = []
    for kb in range(block + 1):
        score = dot_nt(k_ref[pl.ds(kb * QB, QB), :], stacked)
        if block - kb < 2:
            score = score + near_ref[block - kb]
        at = lax.broadcasted_iota(jnp.int32, score.shape, 0) + kb * QB
        keep = at >= starts
        if kb == block:
            lane = lax.broadcasted_iota(jnp.int32, score.shape, 1) % QB + block * QB
            keep = keep & (at <= lane)
        tiles.append(jnp.where(keep, score, NEG))
    return stacked, tiles


def self_forward(heads, q_ref, k_ref, v_ref, near_ref, start_ref, o_ref, lse_ref, vt_ref):
    stream = q_ref.shape[0]
    vt_ref[...] = v_ref[...].T
    for block in range(stream // QB):
        _, tiles = self_scores(q_ref, k_ref, near_ref, start_ref, block, heads)
        top = functools.reduce(jnp.maximum, [jnp.max(t, axis=0, keepdims=True) for t in tiles])
        tiles = [jnp.exp(t - top) for t in tiles]
        total = functools.reduce(jnp.add, [jnp.sum(t, axis=0, keepdims=True) for t in tiles])
        inverse = 1.0 / total
        probs = jnp.concatenate([(t * inverse).astype(BF) for t in tiles], axis=0)
        out = dot(vt_ref[:, pl.ds(0, (block + 1) * QB)], probs)
        o_ref[pl.ds(block * QB, QB), :] = unstack_heads(out, heads).astype(BF)
        lse_ref[:, pl.ds(block * QB * heads, QB * heads)] = top + jnp.log(total)


def self_backward(heads, q_ref, k_ref, v_ref, do_ref, lse_ref, near_ref, start_ref, dq_ref, dk_ref, dv_ref, dnear_ref, dfar_ref, ds_ref, p_ref, kt_ref):
    stream = q_ref.shape[0]
    blocks = stream // QB
    wide = heads * QB

    def spot(kb, block):
        row, first = (kb, 0) if kb < blocks // 2 else (blocks - 1 - kb, kb + 1)
        return row, pl.ds((first + block - kb) * wide, wide)

    kt_ref[...] = k_ref[...].T
    near = [jnp.zeros((QB, heads * QB), F32)] * 2
    far = jnp.zeros((1, heads * QB), F32)
    for block in range(blocks):
        lanes = pl.ds(block * QB * heads, QB * heads)
        _, tiles = self_scores(q_ref, k_ref, near_ref, start_ref, block, heads)
        douts = stack_heads(do_ref[pl.ds(block * QB, QB), :], heads)
        lse = lse_ref[:, lanes]
        probs = [jnp.exp(t - lse) for t in tiles]
        dprobs = [dot_nt(v_ref[pl.ds(kb * QB, QB), :], douts) for kb in range(block + 1)]
        delta = functools.reduce(jnp.add, [jnp.sum(a * b, axis=0, keepdims=True) for a, b in zip(probs, dprobs)])
        dscores = []
        for kb in range(block + 1):
            dscore = (probs[kb] * (dprobs[kb] - delta)).astype(BF)
            row, at = spot(kb, block)
            ds_ref[row, :, at] = dscore
            p_ref[row, :, at] = probs[kb].astype(BF)
            dscores.append(dscore)
            exact = dscore.astype(F32)
            if block - kb < 2:
                near[block - kb] = near[block - kb] + exact
            else:
                far = far + jnp.sum(exact, axis=0, keepdims=True)
        dq = dot(kt_ref[:, pl.ds(0, (block + 1) * QB)], jnp.concatenate(dscores, axis=0))
        dq_ref[pl.ds(block * QB, QB), :] = unstack_heads(dq, heads).astype(BF)
    dnear_ref[0] = near[0]
    dnear_ref[1] = near[1]
    dfar_ref[...] = far
    queries = jnp.concatenate([stack_heads(q_ref[pl.ds(b * QB, QB), :], heads) for b in range(blocks)], axis=0)
    douts = jnp.concatenate([stack_heads(do_ref[pl.ds(b * QB, QB), :], heads) for b in range(blocks)], axis=0)
    for kb in range(blocks):
        row, at = spot(kb, kb)
        rows, lanes = pl.ds(kb * QB, QB), pl.ds(at.start, (blocks - kb) * wide)
        dk_ref[rows, :] = dot(ds_ref[row, :, lanes], queries[kb * wide :]).astype(BF)
        dv_ref[rows, :] = dot(p_ref[row, :, lanes], douts[kb * wide :]).astype(BF)


def cross_forward(heads, count_ref, blocks_ref, docs_ref, offs_ref, q_ref, k_ref, v_ref, doc_ref, o_ref, lse_ref, vt_ref, acc_ref, norm_ref):
    stream = q_ref.shape[0]
    for part in range(v_ref.shape[0] // ENC_ROWS):
        vt_ref[part] = v_ref[pl.ds(part * ENC_ROWS, ENC_ROWS), :].T
    acc_ref[...] = jnp.zeros_like(acc_ref)
    norm_ref[...] = jnp.zeros_like(norm_ref)

    def step(t, carry):
        block, doc, off = blocks_ref[t], docs_ref[t], offs_ref[t]
        stacked = stack_heads(q_ref[pl.ds(pl.multiple_of(block * QB, QB), QB), :], heads)
        keys = k_ref[pl.ds(pl.multiple_of(off * ENC_ROWS, ENC_ROWS), ENC_ROWS), :]
        score = dot_nt(keys, stacked)
        top = jnp.max(score, axis=0, keepdims=True)
        weights = jnp.exp(score - top)
        total = jnp.sum(weights, axis=0, keepdims=True)
        probs = (weights * (1.0 / total)).astype(BF)
        out = dot(vt_ref[off], probs)
        mine = tile_lanes(doc_ref[block], heads) == doc
        acc_ref[block] = jnp.where(mine, out, acc_ref[block])
        norm_ref[block] = jnp.where(mine, top + jnp.log(total), norm_ref[block])
        return carry

    lax.fori_loop(0, count_ref[0], step, 0)
    for block in range(stream // QB):
        o_ref[pl.ds(block * QB, QB), :] = unstack_heads(acc_ref[block], heads).astype(BF)
    lse_ref[...] = norm_ref[...]


def cross_backward(heads, count_ref, blocks_ref, docs_ref, offs_ref, q_ref, k_ref, v_ref, do_ref, doc_ref, lse_ref, dq_ref, dk_ref, dv_ref, kt_ref, acc_ref, dka_ref, dva_ref):
    stream = q_ref.shape[0]
    for part in range(k_ref.shape[0] // ENC_ROWS):
        kt_ref[part] = k_ref[pl.ds(part * ENC_ROWS, ENC_ROWS), :].T
    acc_ref[...] = jnp.zeros_like(acc_ref)
    dka_ref[...] = jnp.zeros_like(dka_ref)
    dva_ref[...] = jnp.zeros_like(dva_ref)

    def step(t, carry):
        block, doc, off = blocks_ref[t], docs_ref[t], offs_ref[t]
        at = pl.ds(pl.multiple_of(block * QB, QB), QB)
        enc = pl.ds(pl.multiple_of(off * ENC_ROWS, ENC_ROWS), ENC_ROWS)
        stacked, douts = stack_heads(q_ref[at, :], heads), stack_heads(do_ref[at, :], heads)
        mine = tile_lanes(doc_ref[block], heads) == doc
        probs = jnp.where(mine, jnp.exp(dot_nt(k_ref[enc, :], stacked) - lse_ref[block]), 0.0)
        dprobs = dot_nt(v_ref[enc, :], douts)
        delta = jnp.sum(probs * dprobs, axis=0, keepdims=True)
        dscore = (probs * (dprobs - delta)).astype(BF)
        acc_ref[block] += dot(kt_ref[off], dscore)
        dka_ref[enc, :] += dot(dscore, stacked)
        dva_ref[enc, :] += dot(probs.astype(BF), douts)
        return carry

    lax.fori_loop(0, count_ref[0], step, 0)
    for block in range(stream // QB):
        dq_ref[pl.ds(block * QB, QB), :] = unstack_heads(acc_ref[block], heads).astype(BF)
    dk_ref[...] = dka_ref[...].astype(BF)
    dv_ref[...] = dva_ref[...].astype(BF)


def rows_at(start, size):
    return pl.ds(pl.multiple_of(start, size), size)


def assemble_cols(dst, refs, order):
    if len(refs) == 1:
        dst[...] = refs[0][...]
        return
    width = refs[0].shape[1]
    for j, ref in enumerate(refs):
        dst[:, rows_at(order[j] * width, width)] = ref[...]


def assemble_weight(dst, refs, order, zorder):
    depth, slab, width = refs[0].shape
    if len(refs) == 1:
        dst[...] = refs[0][0]
        return
    for j, ref in enumerate(refs):
        for p in range(depth):
            dst[rows_at(zorder[p] * slab, slab), rows_at(order[j] * width, width)] = ref[p]


def assemble_slabs(dst, refs, zorder, first=0, slab=None):
    slab = slab or refs[0].shape[0]
    width = dst.shape[1]
    for p, ref in enumerate(refs):
        dst[rows_at(zorder[p] * slab, slab), :] = ref[pl.ds(0, slab), pl.ds(first, width)]


def token_rows(device, count, half):
    return rows_at(device * half, half), rows_at((2 * count - 1 - device) * half, half)


def inverse_rms(value):
    return lax.rsqrt(jnp.mean(value * value, axis=-1, keepdims=True) + EPSILON)


def norm_backward(grad, value, gain):
    scale = inverse_rms(value)
    normed = value * scale
    dnormed = grad * gain
    dvalue = scale * (dnormed - normed * jnp.mean(dnormed * normed, axis=-1, keepdims=True))
    return dvalue, jnp.sum(grad * normed, axis=0, keepdims=True)


def store_pieces(value_rows, order, count, half, keep_ref, away_ref):
    for d in range(count):
        low, high = token_rows(order[0] ^ d, count, half)
        rows = jnp.concatenate([value_rows(low), value_rows(high)], axis=0).astype(BF)
        if count == 8:
            (away_ref if d % 2 else keep_ref)[d // 2] = rows
        else:
            keep_ref[d] = rows


def run(kernel, scalars, arrays, outs, scratch, name, flops, moved):
    smem = pl.BlockSpec(memory_space=pltpu.SMEM)
    vmem = pl.BlockSpec(memory_space=pltpu.VMEM)
    return pl.pallas_call(
        kernel,
        in_specs=[smem] * len(scalars) + [vmem] * len(arrays),
        out_specs=[vmem] * len(outs),
        out_shape=[jax.ShapeDtypeStruct(shape, kind) for shape, kind in outs],
        scratch_shapes=[pltpu.VMEM(shape, kind) for shape, kind in scratch],
        compiler_params=pltpu.CompilerParams(vmem_limit_bytes=60 << 20),
        cost_estimate=pl.CostEstimate(flops=int(flops), bytes_accessed=int(moved), transcendentals=0),
        name=name,
    )(*scalars, *arrays)


def self_block(n, depth, heads, order, zorder, ids_ref, start_ref, *refs):
    hidden, weights = refs[:n], refs[n : n + depth]
    x_ref, h_ref, q_ref, k_ref, v_ref, o_ref, lse_ref, near_ref, gains_ref, w_ref, vt_ref = refs[n + depth :]
    half = hidden[0].shape[0] // 2
    slab = D // depth
    width = heads * DK
    aux = [w[pl.ds(slab, 16), :].astype(F32) for w in weights]
    for p in range(depth):
        gains_ref[:, rows_at(zorder[p] * slab, slab)] = aux[p][8:, :slab]
    assemble_slabs(w_ref, weights, zorder, 0, slab)
    per = BUCKETS // depth
    for h in range(heads):
        far = sum(jnp.where(zorder[p] == depth - 1, aux[p][per - 1 : per, h : h + 1], 0.0) for p in range(depth))
        for a in range(2):
            tile = jnp.zeros((QB, QB), F32)
            for p in range(depth):
                for r in range(per):
                    tile = jnp.where(ids_ref[a] == zorder[p] * per + r, aux[p][r : r + 1, h : h + 1] - far, tile)
            near_ref[a, :, pl.ds(h * QB, QB)] = tile
    gain = gains_ref[0:1, :]
    for p in range(n):
        rows = hidden[p][...]
        value = rows.astype(F32)
        low = (value * inverse_rms(value) * gain).astype(BF)
        for part, at in enumerate(token_rows(order[p], n, half)):
            x_ref[at, :] = rows[part * half : (part + 1) * half]
            h_ref[at, :] = low[part * half : (part + 1) * half]
    stream = x_ref.shape[0]
    for r in range(0, stream, 256):
        at = pl.ds(r, 256)
        proj = dot(h_ref[at, :], w_ref[...]).astype(BF)
        for part, ref in enumerate((q_ref, k_ref, v_ref)):
            ref[at, :] = proj[:, part * width : (part + 1) * width]
    self_forward(heads, q_ref, k_ref, v_ref, near_ref, start_ref, o_ref, lse_ref, vt_ref)


def encoder_block(zorder, enc_ref, *refs):
    weights, (k_ref, v_ref, w_ref) = refs[:-3], refs[-3:]
    width = k_ref.shape[1]
    assemble_slabs(w_ref, weights, zorder)
    for r in range(0, enc_ref.shape[0], 256):
        at = pl.ds(r, 256)
        pair = dot(enc_ref[at, :], w_ref[...]).astype(BF)
        k_ref[at, :], v_ref[at, :] = pair[:, :width], pair[:, width:]


def cross_block(n_cols, n_w, depth, heads, order, zorder, count_ref, blocks_ref, docs_ref, offs_ref, x_ref, gains_ref, kc_ref, vc_ref, doc_ref, *refs):
    pieces, outs, locals_ = refs[:n_cols], refs[n_cols : n_cols + n_w], refs[n_cols + n_w : n_cols + n_w + depth]
    x1_ref, h_ref, q_ref, o_ref, lse_ref, wrows_ref, ob_ref, w_ref, wq_ref, vt_ref, acc_ref, norm_ref = refs[n_cols + n_w + depth :]
    width = heads * DK
    assemble_cols(ob_ref, pieces, order)
    assemble_weight(w_ref, outs, order, zorder)
    assemble_slabs(wq_ref, locals_, zorder)
    wrows_ref[...] = w_ref[rows_at(order[0] * width, width), :]
    gain = gains_ref[1:2, :]
    for r in range(0, x_ref.shape[0], 256):
        at = pl.ds(r, 256)
        x1 = x_ref[at, :].astype(F32) + dot(ob_ref[at, :], w_ref[...])
        x1_ref[at, :] = x1
        low = (x1 * inverse_rms(x1) * gain).astype(BF)
        h_ref[at, :] = low
        q_ref[at, :] = dot(low, wq_ref[...]).astype(BF)
    cross_forward(heads, count_ref, blocks_ref, docs_ref, offs_ref, q_ref, kc_ref, vc_ref, doc_ref, o_ref, lse_ref, vt_ref, acc_ref, norm_ref)


def gelu_parts(gate):
    inner = math.sqrt(2.0 / math.pi)
    square = gate * gate
    slope = jnp.tanh(inner * (gate + 0.044715 * gate * square))
    value = 0.5 * gate * (1.0 + slope)
    grad = 0.5 * (1.0 + slope) + 0.5 * gate * (1.0 - slope * slope) * inner * (1.0 + 3 * 0.044715 * square)
    return value, grad


def ffn_block(n, n_cols, n_w, order, zorder, x1_ref, gains_ref, in_ref, down_ref, *refs):
    pieces, outs, grads = refs[:n_cols], refs[n_cols : n_cols + n_w], refs[n_cols + n_w : n_cols + n_w + n]
    ocb_ref, g_ref, h_ref, act_ref, dgu_ref, own_ref, wrows_ref, *rest = refs[n_cols + n_w + n :]
    (keep_ref, away_ref), (w_ref, x2_ref, dh_ref) = (rest[:2], rest[2:]) if n == 8 else ((rest[0], None), rest[1:])
    half = grads[0].shape[0] // 2
    units = act_ref.shape[1]
    width = wrows_ref.shape[0]
    assemble_cols(ocb_ref, pieces, order)
    assemble_weight(w_ref, outs, order, zorder)
    wrows_ref[...] = w_ref[rows_at(order[0] * width, width), :]
    for p in range(n):
        for part, at in enumerate(token_rows(order[p], n, half)):
            g_ref[at, :] = grads[p][pl.ds(part * half, half), :]
    gain = gains_ref[2:3, :]
    for r in range(0, x1_ref.shape[0], 256):
        at = pl.ds(r, 256)
        x2 = x1_ref[at, :] + dot(ocb_ref[at, :], w_ref[...])
        x2_ref[at, :] = x2
        low = (x2 * inverse_rms(x2) * gain).astype(BF)
        h_ref[at, :] = low
        both = dot(low, in_ref[...])
        gate, up = both[:, :units], both[:, units:]
        value, slope = gelu_parts(gate)
        act_ref[at, :] = (value * up).astype(BF)
        dact = dot_nt(g_ref[at, :], down_ref[...])
        dgu = jnp.concatenate([dact * up * slope, dact * value], axis=1).astype(BF)
        dgu_ref[at, :] = dgu
        dh_ref[at, :] = dot_nt(dgu, in_ref[...])
    store_pieces(lambda at: dh_ref[at, :], order, n, half, keep_ref, away_ref)
    low, high = token_rows(order[0], n, half)
    own_ref[pl.ds(0, half), :] = x2_ref[low, :]
    own_ref[pl.ds(half, half), :] = x2_ref[high, :]


def ffn_output(n, order, act_ref, down_ref, *refs):
    (keep_ref, away_ref, out_ref) = refs if n == 8 else (refs[0], None, refs[1])
    for r in range(0, act_ref.shape[0], 256):
        at = pl.ds(r, 256)
        out_ref[at, :] = dot(act_ref[at, :], down_ref[...])
    store_pieces(lambda at: out_ref[at, :], order, n, keep_ref.shape[1] // 2, keep_ref, away_ref)


def norm_grad(index, arrived, own_ref, value_ref, base_ref, gains_ref, *refs):
    out_ref, low_ref, dgain_ref = refs[arrived:]
    total = own_ref[...]
    for ref in refs[:arrived]:
        total = total + ref[...].astype(F32)
    dvalue, dgain = norm_backward(total, value_ref[...].astype(F32), gains_ref[index : index + 1, :])
    out = base_ref[...].astype(F32) + dvalue
    out_ref[...] = out
    low_ref[...] = out.astype(BF)
    dgain_ref[...] = dgain


def column_parts(ref, parts, width):
    return [ref.at[:, pl.ds(p * width, width)] for p in range(parts)] if width % 128 == 0 else None


def put_columns(ref, parts):
    for r in range(0, ref.shape[0], 256):
        at = pl.ds(r, 256)
        ref[at, :] = jnp.concatenate([part[at, :] for part in parts], axis=1)


def spare(parts, rows, width):
    return [] if width % 128 == 0 else [((rows, width), BF)] * parts


def cross_grad(n, heads, order, count_ref, blocks_ref, docs_ref, offs_ref, wrows_ref, q_ref, k_ref, v_ref, doc_ref, lse_ref, *refs):
    pieces = refs[:n]
    g_ref, dq_ref, dkv_ref, do_ref, kt_ref, acc_ref, dka_ref, dva_ref, *extra = refs[n:]
    half = pieces[0].shape[0] // 2
    width = heads * DK
    for p in range(n):
        for part, at in enumerate(token_rows(order[p], n, half)):
            g_ref[at, :] = pieces[p][pl.ds(part * half, half), :]
    for r in range(0, g_ref.shape[0], 256):
        at = pl.ds(r, 256)
        do_ref[at, :] = dot_nt(g_ref[at, :], wrows_ref[...]).astype(BF)
    cross_backward(heads, count_ref, blocks_ref, docs_ref, offs_ref, q_ref, k_ref, v_ref, do_ref, doc_ref, lse_ref, dq_ref, *(extra or column_parts(dkv_ref, 2, width)), kt_ref, acc_ref, dka_ref, dva_ref)
    if extra:
        put_columns(dkv_ref, extra)


def self_grad(n, n_cols, n_w, heads, order, zorder, x1_ref, gb2_ref, own_ref, gains_ref, wo_ref, wqkv_ref, q_ref, k_ref, v_ref, lse_ref, near_ref, start_ref, *refs):
    pieces, outs = refs[:n_cols], refs[n_cols : n_cols + n_w]
    gb1_ref, dqkv_ref, dnear_ref, dfar_ref, gx1_ref, dgain_ref, *rest = refs[n_cols + n_w :]
    (keep_ref, away_ref), rest = (rest[:2], rest[2:]) if n == 8 else ((rest[0], None), rest[1:])
    dqc_ref, w_ref, dx_ref, do_ref, ds_ref, p_ref, kt_ref, *extra = rest
    half = own_ref.shape[0] // 2
    width = heads * DK
    stream = x1_ref.shape[0]
    if len(pieces) > 1:
        assemble_cols(dqc_ref, pieces, order)
        assemble_weight(w_ref, outs, order, zorder)
    else:
        dqc_ref, w_ref = pieces[0], outs[0].at[0]
    gain = gains_ref[1:2, :]
    total = jnp.zeros_like(gain)
    for r in range(0, stream, 256):
        at = pl.ds(r, 256)
        dh = dot_nt(dqc_ref[at, :], w_ref[...])
        dvalue, dgain = norm_backward(dh, x1_ref[at, :], gain)
        total = total + dgain
        dx_ref[at, :] = dvalue
        low = (gb2_ref[at, :].astype(F32) + dvalue).astype(BF)
        gb1_ref[at, :] = low
        do_ref[at, :] = dot_nt(low, wo_ref[...]).astype(BF)
    dgain_ref[...] = total
    for part, at in enumerate(token_rows(order[0], n, half)):
        mine = pl.ds(part * half, half)
        gx1_ref[mine, :] = own_ref[mine, :] + dx_ref[at, :]
    self_backward(heads, q_ref, k_ref, v_ref, do_ref, lse_ref, near_ref, start_ref, *(extra or column_parts(dqkv_ref, 3, width)), dnear_ref, dfar_ref, ds_ref, p_ref, kt_ref)
    if extra:
        put_columns(dqkv_ref, extra)
    for r in range(0, stream, 256):
        at = pl.ds(r, 256)
        dx_ref[at, :] = dot_nt(dqkv_ref[at, :], wqkv_ref[...])
    store_pieces(lambda at: dx_ref[at, :], order, n, half, keep_ref, away_ref)


def spread(groups, order, *refs):
    n = len(refs) - len(groups)
    pieces, outs = refs[:n], refs[n:]
    slab = outs[0].shape[0]
    width = outs[0].shape[1] // (n * groups[0])
    first = 0
    for out, parts in zip(outs, groups):
        for t in range(parts):
            for j, ref in enumerate(pieces):
                part = ref[pl.ds(0, slab), pl.ds((first + t) * width, width)]
                out[:, rows_at(t * n * width + order[j] * width, width)] = part.astype(F32)
        first += parts


def body(
    hidden_in,
    encoder_out,
    doc_ids,
    enc_offsets,
    cotangent,
    self_qkv,
    self_out,
    rel_bias,
    cross_q,
    cross_kv,
    cross_out,
    ffn_in,
    ffn_out,
    norm_gains,
):
    n, depth = lax.axis_size("ctx"), lax.axis_size("fsdp")
    me, level = lax.axis_index("ctx"), lax.axis_index("fsdp")
    tokens = hidden_in.shape[1]
    stream = tokens * n
    width = H * DK // n
    heads = H // n
    slab = D // depth
    piece = FF // (depth * n)
    units = -(-piece * depth // 128) * 128
    fill = units - piece * depth
    rows_all = encoder_out.shape[1] * n
    wide = n == 8
    own = me * width
    sources = ctx_order(me, n)
    order = jnp.stack(sources).astype(jnp.int32)
    zorder = jnp.stack([level ^ d for d in range(depth)]).astype(jnp.int32)
    per = BUCKETS // depth

    def columns(value, start, size):
        return lax.dynamic_slice_in_dim(value, start, size, 1)

    def gather_columns(value):
        if wide:
            return ctx_gather(value, n)
        return [lax.all_gather(value, "ctx", axis=1, tiled=True)]

    def gather_weight(pieces):
        if wide:
            return ctx_gather(jnp.stack(pieces), n)
        rows = jnp.zeros((D, width), BF)
        for d, value in enumerate(pieces):
            rows = lax.dynamic_update_slice(rows, value, ((level ^ d) * slab, 0))
        return [lax.all_gather(rows, "ctx", axis=1, tiled=True)[None]]

    hidden = ctx_gather(hidden_in[0], n)
    small = jnp.zeros((16, 3 * width), BF)
    small = lax.dynamic_update_slice(small, columns(rel_bias, me * heads, heads), (0, 0))
    small = lax.dynamic_update_slice(small, norm_gains, (8, 0))
    three = jnp.concatenate([columns(self_qkv, p * H * DK + own, width) for p in range(3)], axis=1)
    w_qkv = z_gather(jnp.concatenate([three, small], axis=0), depth)
    w_out = gather_weight(z_gather(columns(self_out, own, width), depth))
    w_kv = z_gather(jnp.concatenate([columns(cross_kv, p * H * DK + own, width) for p in range(2)], axis=1), depth)
    w_q = z_gather(columns(cross_q, own, width), depth)
    w_cout = gather_weight(z_gather(columns(cross_out, own, width), depth))
    w_cq = gather_weight(w_q)
    enc = lax.all_gather(encoder_out[0], "ctx", axis=0, tiled=True)
    parts = []
    for part in range(2):
        parts += [columns(ffn_in, part * FF + z * (FF // depth) + me * piece, piece) for z in range(depth)]
        parts += [jnp.zeros((slab, fill), BF)] * (fill > 0)
    w_in = lax.all_gather(jnp.concatenate(parts, axis=1), "fsdp", axis=0, tiled=True)
    w_down = lax.all_gather(lax.dynamic_slice_in_dim(ffn_out, me * piece, piece), "fsdp", axis=0, tiled=True)
    w_down = jnp.pad(w_down, ((0, fill), (0, 0)))
    grads = ctx_gather(cotangent[0], n)

    ids = doc_ids[0]
    offsets = enc_offsets[0]
    docs = offsets.shape[0]
    doc_range = jnp.arange(docs, dtype=jnp.int32)
    doc_starts = jnp.sum((ids[None, :] < doc_range[:, None]).astype(jnp.int32), axis=1)
    starts = jnp.sum(jnp.where(ids[None, :] == doc_range[:, None], doc_starts[:, None], 0), axis=0)[None]
    q_blocks = stream // QB
    first_doc = ids[::QB]
    spans = ids[QB - 1 :: QB] - first_doc + 1
    at_or_before = np.arange(q_blocks)[:, None] >= np.arange(q_blocks)[None, :]
    ends = jnp.sum(jnp.where(at_or_before, spans[None, :], 0), axis=1)
    slots = jnp.arange(q_blocks + docs, dtype=jnp.int32)
    slot_block = jnp.minimum(jnp.sum((slots[:, None] >= ends[None, :]).astype(jnp.int32), axis=1), q_blocks - 1)
    in_block = slot_block[:, None] == jnp.arange(q_blocks)[None, :]
    slot_doc = slots + jnp.sum(jnp.where(in_block, (first_doc - ends + spans)[None, :], 0), axis=1)
    slot_doc = jnp.clip(slot_doc, 0, docs - 1)
    slot_part = jnp.sum(jnp.where(slot_doc[:, None] == doc_range[None, :], (offsets // ENC_ROWS)[None, :], 0), axis=1)
    work = (jnp.sum(spans)[None], slot_block, slot_doc, slot_part)
    doc_rows = ids.reshape(q_blocks, 1, QB)
    near_ids = jnp.asarray(near_buckets())

    rows_bf = ((stream, width), BF)
    full_bf = ((stream, D), BF)
    own_f32 = ((tokens, D), F32)
    pieces_out = [((4, tokens, D), BF)] * 2 if wide else [((n, tokens, D), BF)]
    q_lanes = QB * heads
    triangle = ((q_blocks // 2, QB, (q_blocks + 1) * q_lanes), BF)

    x, h1, query, key, value, attended, lse, near, gains, wqkv = run(
        functools.partial(self_block, n, depth, heads), (order, zorder), (near_ids, starts, *hidden, *w_qkv),
        [full_bf, full_bf, rows_bf, rows_bf, rows_bf, rows_bf, ((1, stream * heads), F32), ((2, QB, q_lanes), F32), ((8, D), F32), ((D, 3 * width), BF)],
        [((width, stream), BF)], "self_block", 8 * stream * D * width, 10 * stream * D)
    ob = gather_columns(attended)
    ckey, cvalue, wckv = run(
        encoder_block, (zorder,), (enc, *w_kv),
        [((rows_all, width), BF)] * 2 + [((D, 2 * width), BF)], [], "encoder_block", 4 * rows_all * D * width, 3 * rows_all * D)
    x1, h2, cquery, crossed, clse, wo_rows, ob_all = run(
        functools.partial(cross_block, len(ob), len(w_out), depth, heads), (order, zorder, *work),
        (x, gains, ckey, cvalue, doc_rows, *ob, *w_out, *w_q),
        [((stream, D), F32), full_bf, rows_bf, rows_bf, ((q_blocks, 1, q_lanes), F32), ((width, D), BF), full_bf],
        [((D, D), BF), ((D, width), BF), ((rows_all // ENC_ROWS, width, ENC_ROWS), BF), ((q_blocks, width, q_lanes), F32), ((q_blocks, 1, q_lanes), F32)],
        "cross_block", 4 * stream * D * D, 14 * stream * D)
    ocb_pieces = gather_columns(crossed)
    ocb, g, h3, act, dgu, x2_own, wco_rows, *dh3 = run(
        functools.partial(ffn_block, n, len(ocb_pieces), len(w_cout)), (order, zorder),
        (x1, gains, w_in, w_down, *ocb_pieces, *w_cout, *grads),
        [full_bf, full_bf, full_bf, ((stream, units), BF), ((stream, 2 * units), BF), own_f32, ((width, D), BF), *pieces_out],
        [((D, D), BF), ((stream, D), F32), ((stream, D), F32)], "ffn_block", 2 * stream * D * (D + 5 * units), 22 * stream * D)

    def reduce_norm(parts, index, kept, base):
        total, arrived = ctx_reduce(*(parts if wide else (parts[0], None)), n)
        return run(
            functools.partial(norm_grad, index, len(arrived)), (), (total, kept, base, gains, *arrived),
            [own_f32, ((tokens, D), BF), ((1, D), F32)], [], "norm_grad", 10 * tokens * D, 20 * tokens * D)

    gx2_own, gb2_own, dgain3 = reduce_norm(dh3, 2, x2_own, cotangent[0])
    gb2_pieces = ctx_gather(gb2_own, n)
    out_parts = run(
        functools.partial(ffn_output, n), (order,), (act, w_down), pieces_out, [((stream, D), F32)], "ffn_output", 2 * stream * D * units, 6 * stream * D)
    total, arrived = ctx_reduce(*(out_parts if wide else (out_parts[0], None)), n)
    for part in arrived:
        total = total + part.astype(F32)
    result = (x2_own + total).astype(BF)

    def sum_z(value):
        return lax.psum_scatter(value, "fsdp", scatter_dimension=0, tiled=True)

    def reduce_z(value):
        total = lax.dynamic_index_in_dim(value, level, 0, False).astype(F32)
        for d in range(1, depth):
            away = lax.dynamic_index_in_dim(value, level ^ d, 0, False)
            total = total + send(away, "fsdp", depth, lambda i, d=d: i ^ d).astype(F32)
        return total.astype(BF)

    def place(part, groups):
        if wide:
            pieces = ctx_gather(part, n)
            outs = [((slab, g * D), F32) for g in groups]
            return pieces, run(functools.partial(spread, groups), (order,), pieces, outs, [], "spread", 1000, 6 * slab * D * sum(groups))
        pieces = lax.all_gather(part, "ctx", axis=0)
        outs, first = [], 0
        for g in groups:
            cols = pieces[:, :slab, first * width : (first + g) * width].reshape(n, slab, g, width)
            outs.append(jnp.transpose(cols, (1, 2, 0, 3)).reshape(slab, g * D).astype(F32))
            first += g
        return [pieces[j] for j in range(n)], outs

    grad_in = sum_z(dot_tn(h3, dgu).astype(BF))
    grad_down = sum_z(dot_tn(act, g)[: piece * depth].astype(BF))
    gb2, dcq, dkvc = run(
        functools.partial(cross_grad, n, heads), (order, *work), (wco_rows, cquery, ckey, cvalue, doc_rows, clse, *gb2_pieces),
        [full_bf, rows_bf, ((rows_all, 2 * width), BF)],
        [rows_bf, ((rows_all // ENC_ROWS, width, ENC_ROWS), BF), ((q_blocks, width, q_lanes), F32), ((rows_all, width), F32), ((rows_all, width), F32), *spare(2, rows_all, width)],
        "cross_grad", 2 * stream * D * width * 8, 8 * stream * D)
    dcq_pieces = gather_columns(dcq)
    grad_ckv = dot_tn(enc, dkvc).astype(BF)
    grad_enc = lax.psum_scatter(dot_nt(dkvc, wckv).astype(BF), "ctx", scatter_dimension=0, tiled=True).astype(F32)
    grad_cq = dot_tn(h2, dcq).astype(BF)
    grad_cout = dot_tn(ocb, columns(gb2, own, width)).astype(BF)
    middle = jnp.concatenate([grad_cq, grad_ckv, grad_cout], axis=1)
    gb1, dqkv, dnear, dfar, gx1_own, dgain2, *dh1 = run(
        functools.partial(self_grad, n, len(dcq_pieces), len(w_cq), heads), (order, zorder),
        (x1, gb2, gx2_own, gains, wo_rows, wqkv, query, key, value, lse, near, starts, *dcq_pieces, *w_cq),
        [full_bf, ((stream, 3 * width), BF), ((2, QB, q_lanes), F32), ((1, q_lanes), F32), own_f32, ((1, D), F32), *pieces_out],
        [full_bf if wide else ((16, 128), BF), ((D, D) if wide else (16, 128), BF), ((stream, D), F32), rows_bf, triangle, triangle, ((width, stream), BF), *spare(3, stream, width)],
        "self_grad", 2 * stream * D * (D + 8 * width), 30 * stream * D)
    grad_hidden, _, dgain1 = reduce_norm(dh1, 0, hidden_in[0], gx1_own)

    onehot = (near_ids[..., None] == jnp.arange(BUCKETS, dtype=jnp.int32)).astype(F32)
    dtable = jnp.einsum("akqb,akhq->bh", onehot, dnear.reshape(2, QB, heads, QB), precision=lax.Precision.HIGHEST)
    far = jnp.sum(dfar.reshape(heads, QB), axis=1)
    dtable = dtable + jnp.where(jnp.arange(BUCKETS)[:, None] == BUCKETS - 1, far[None, :], 0.0)
    dtable = jnp.pad(dtable.reshape(depth, per, heads), ((0, 0), (0, 8 - per), (0, 4 * width - heads)))
    dgains = jnp.concatenate([dgain1, jnp.where(me == 0, dgain2, 0.0), dgain3], axis=0)
    dgains = jnp.transpose(dgains.reshape(3, depth, slab), (1, 0, 2))
    dgains = jnp.pad(dgains, ((0, 0), (0, 5), (0, 4 * width - slab)))
    last = jnp.concatenate([dot_tn(h1, dqkv), dot_tn(ob_all, columns(gb1, own, width))], axis=1)
    last = jnp.concatenate([last.reshape(depth, slab, 4 * width), dtable, dgains], axis=1).astype(BF)
    last_pieces, (grad_self_qkv, grad_self_out) = place(reduce_z(last), (3, 1))
    extra = [p[slab:].astype(F32) for p in last_pieces]
    grad_gains = sum(e[8:11, :slab] for e in extra)
    grad_table = jnp.zeros((per, H), F32)
    for j, e in enumerate(extra):
        grad_table = lax.dynamic_update_slice(grad_table, e[:per, :heads], (0, (sources[j] if wide else j) * heads))
    _, (grad_cross_q, grad_cross_kv, grad_cross_out) = place(sum_z(middle), (1, 2, 1))
    up_cols = lax.all_gather(grad_in, "ctx", axis=0).reshape(n, slab, 2, units)[..., : piece * depth]
    up_cols = up_cols.reshape(n, slab, 2 * depth, piece)
    grad_ffn_in = jnp.transpose(up_cols, (1, 2, 0, 3)).reshape(slab, 2 * FF).astype(F32)
    grad_ffn_out = lax.all_gather(grad_down, "ctx", axis=0, tiled=True).astype(F32)
    return (
        result[None],
        grad_hidden[None],
        grad_enc[None],
        grad_self_qkv,
        grad_self_out,
        grad_table,
        grad_cross_q,
        grad_cross_kv,
        grad_cross_out,
        grad_ffn_in,
        grad_ffn_out,
        grad_gains,
    )


def solution(mesh):
    split = P("fsdp", "ctx", None)
    rows = P("fsdp", None)
    return jax.shard_map(
        body,
        mesh=mesh,
        in_specs=(split, split, rows, rows, split) + (rows,) * 8 + (P(None, "fsdp"),),
        out_specs=(split,) * 3 + (rows,) * 8 + (P(None, "fsdp"),),
        check_vma=False,
    )
```

```python
import functools
import math

import jax
import jax.numpy as jnp
import numpy as np
from jax import lax
from jax.experimental import pallas as pl
from jax.experimental.pallas import tpu as pltpu
from jax.sharding import PartitionSpec as P

D = 1024
H = 16
DK = 64
FF = 2816
BUCKETS = 32
ENC_ROWS = 512
QB = 128
NEG = -1e30
EPSILON = 1e-06
BF = jnp.bfloat16
F32 = jnp.float32

EDGES = np.ceil(16.0 * 8.0 ** (np.arange(1, 16) / 16.0)).astype(np.int32)


def near_buckets():
    gap = np.arange(-3, 4)[:, None, None] * 64 + (np.arange(QB) // 64 * 128 + np.arange(QB) % 64)[None, None, :]
    steps = np.maximum(gap - np.arange(64)[None, :, None], 0)
    far = 16 + np.sum(steps[..., None] >= EDGES, axis=-1)
    return np.where(steps < 16, steps, far).astype(np.int32)


def dot(a, b):
    return jnp.dot(a, b, preferred_element_type=F32)


def dot_nt(a, b):
    return lax.dot_general(a, b, (((1,), (1,)), ((), ())), preferred_element_type=F32)


def dot_tn(a, b):
    return lax.dot_general(a, b, (((0,), (0,)), ((), ())), preferred_element_type=F32)


def send(value, axis, count, target):
    return lax.ppermute(value, axis, [(i, target(i)) for i in range(count)])


def first_way(i):
    return i ^ 2 if i % 2 == 0 else i ^ 4


def second_way(i):
    return i ^ 4 if i % 2 == 0 else i ^ 2


def ctx_order(me, count):
    if count == 8:
        even = (me % 2) == 0
        one, two = jnp.where(even, 2, 4), jnp.where(even, 4, 2)
        rel = [0, one, two, 6, 1, jnp.where(even, 5, 3), jnp.where(even, 3, 5), 7]
    else:
        rel = list(range(count))
    return [me ^ r for r in rel]


def ctx_gather(value, count):
    if count == 8:
        near, other = send(value, "ctx", 8, first_way), send(value, "ctx", 8, second_way)
        far = send(near, "ctx", 8, second_way)
        mine = [value, near, other, far]
        return mine + [send(v, "ctx", 8, lambda i: i ^ 1) for v in mine]
    return [value] + [send(value, "ctx", count, lambda i, d=d: i ^ d) for d in range(1, count)]


def chip_order(me, count):
    return [(me // 2) ^ r for r in range(count // 2)]


def chip_gather(value, count):
    return [value] + [send(value, "ctx", count, lambda i, d=d: i ^ (2 * d)) for d in range(1, count // 2)]


def chip_reduce(away, count):
    return [send(away[d - 1], "ctx", count, lambda i, d=d: i ^ (2 * d)) for d in range(1, count // 2)]


def sibling(value, count):
    return send(value, "ctx", count, lambda i: i ^ 1)


def after(value, *others):
    return lax.optimization_barrier((value, *others))[0]


def z_gather(value, depth):
    return [value] + [send(value, "fsdp", depth, lambda i, d=d: i ^ d) for d in range(1, depth)]


def stack_heads(rows, heads):
    if heads == 1:
        return rows
    lane = lax.broadcasted_iota(jnp.int32, rows.shape, 1) // DK
    return jnp.concatenate([jnp.where(lane == h, rows, jnp.zeros_like(rows)) for h in range(heads)], axis=0)


def unstack_heads(cols, heads):
    parts = [cols[h * DK : (h + 1) * DK, h * QB : (h + 1) * QB] for h in range(heads)]
    return jnp.concatenate(parts, axis=0).T if heads > 1 else parts[0].T


def tile_lanes(row, heads):
    return jnp.concatenate([row] * heads, axis=1) if heads > 1 else row


def block_place(l, core, chips):
    return 2 * l + (core if l < chips else 1 - core)


def self_scores(q_ref, k_ref, near_ref, start_ref, place_ref, block, shift, heads):
    rows = pl.ds(block * QB, QB)
    stacked = stack_heads(q_ref[rows, :], heads)
    starts = tile_lanes(start_ref[:, rows], heads)
    places = tile_lanes(place_ref[:, rows], heads)
    tiles = []
    for kb in range(2 * block + 2):
        score = dot_nt(k_ref[pl.ds(kb * QB, QB), :], stacked)
        if kb >= 2 * block - 1:
            first = 4 * block - 2 * kb + shift + 3
            score = score + jnp.concatenate([near_ref[first], near_ref[first - 1]], axis=0)
        at = lax.broadcasted_iota(jnp.int32, score.shape, 0) + kb * QB
        keep = at >= starts
        if kb >= 2 * block:
            keep = keep & (at <= places)
        tiles.append(jnp.where(keep, score, NEG))
    return stacked, tiles


def fold(op, tiles, reduce):
    return functools.reduce(op, [reduce(t, axis=0, keepdims=True) for t in tiles])


def self_forward(heads, core, q_ref, k_ref, v_ref, near_ref, start_ref, place_ref, o_ref, lse_ref, vt_ref):
    blocks = q_ref.shape[0] // QB
    vt_ref[...] = v_ref[...].T
    for block in range(blocks):
        shift = core if block < blocks // 2 else 1 - core
        _, tiles = self_scores(q_ref, k_ref, near_ref, start_ref, place_ref, block, shift, heads)
        top = fold(jnp.maximum, tiles, jnp.max)
        tiles = [jnp.exp(t - top) for t in tiles]
        total = fold(jnp.add, tiles, jnp.sum)
        inverse = 1.0 / total
        probs = jnp.concatenate([(t * inverse).astype(BF) for t in tiles], axis=0)
        out = dot(vt_ref[:, pl.ds(0, (block + 1) * 2 * QB)], probs)
        o_ref[pl.ds(block * QB, QB), :] = unstack_heads(out, heads).astype(BF)
        lse_ref[:, pl.ds(block * QB * heads, QB * heads)] = top + jnp.log(total)


def self_backward(heads, core, q_ref, k_ref, v_ref, do_ref, lse_ref, near_ref, start_ref, place_ref, dq_ref, dkv_ref, dnear_ref, dfar_ref, ds_ref, p_ref, kt_ref):
    blocks = q_ref.shape[0] // QB
    width = q_ref.shape[1]
    wide = heads * QB

    def spot(kb, block):
        row, first = (kb, 0) if kb < blocks // 2 else (blocks - 1 - kb, kb + 1)
        return row, (first + block - kb) * wide

    kt_ref[...] = k_ref[...].T
    dnear_ref[...] = jnp.zeros_like(dnear_ref)
    far = jnp.zeros((1, wide), F32)
    for block in range(blocks):
        shift = core if block < blocks // 2 else 1 - core
        _, tiles = self_scores(q_ref, k_ref, near_ref, start_ref, place_ref, block, shift, heads)
        douts = stack_heads(do_ref[pl.ds(block * QB, QB), :], heads)
        lse = lse_ref[:, pl.ds(block * wide, wide)]
        probs = [jnp.exp(t - lse) for t in tiles]
        dprobs = [dot_nt(v_ref[pl.ds(kb * QB, QB), :], douts) for kb in range(len(tiles))]
        delta = functools.reduce(jnp.add, [jnp.sum(a * b, axis=0, keepdims=True) for a, b in zip(probs, dprobs)])
        dscores = []
        for kb in range(len(tiles)):
            dscore = (probs[kb] * (dprobs[kb] - delta)).astype(BF)
            row, first = spot(kb // 2, block)
            at = pl.ds(kb % 2 * QB, QB), pl.ds(first, wide)
            ds_ref[row, at[0], at[1]] = dscore
            p_ref[row, at[0], at[1]] = probs[kb].astype(BF)
            dscores.append(dscore)
            exact = dscore.astype(F32)
            if kb >= 2 * block - 1:
                first = 4 * block - 2 * kb + shift + 3
                dnear_ref[first] += exact[: QB // 2]
                dnear_ref[first - 1] += exact[QB // 2 :]
            else:
                far = far + jnp.sum(exact, axis=0, keepdims=True)
        dq = dot(kt_ref[:, pl.ds(0, (block + 1) * 2 * QB)], jnp.concatenate(dscores, axis=0))
        dq_ref[pl.ds(block * QB, QB), :] = unstack_heads(dq, heads).astype(BF)
    dfar_ref[...] = far
    queries = jnp.concatenate([stack_heads(q_ref[pl.ds(b * QB, QB), :], heads) for b in range(blocks)], axis=0)
    douts = jnp.concatenate([stack_heads(do_ref[pl.ds(b * QB, QB), :], heads) for b in range(blocks)], axis=0)
    for kb in range(blocks):
        row, first = spot(kb, kb)
        lanes = pl.ds(first, (blocks - kb) * wide)
        rows = pl.ds(kb * 2 * QB, 2 * QB)
        dkv_ref[rows, pl.ds(0, width)] = dot(ds_ref[row, :, lanes], queries[kb * wide :])
        dkv_ref[rows, pl.ds(width, width)] = dot(p_ref[row, :, lanes], douts[kb * wide :])


def cross_forward(heads, count_ref, blocks_ref, docs_ref, offs_ref, q_ref, k_ref, v_ref, doc_ref, o_ref, lse_ref, vt_ref, acc_ref, norm_ref):
    stream = q_ref.shape[0]
    for part in range(v_ref.shape[0] // ENC_ROWS):
        vt_ref[part] = v_ref[pl.ds(part * ENC_ROWS, ENC_ROWS), :].T
    acc_ref[...] = jnp.zeros_like(acc_ref)
    norm_ref[...] = jnp.zeros_like(norm_ref)

    def step(t, carry):
        block, doc, off = blocks_ref[t], docs_ref[t], offs_ref[t]
        stacked = stack_heads(q_ref[pl.ds(pl.multiple_of(block * QB, QB), QB), :], heads)
        keys = k_ref[pl.ds(pl.multiple_of(off * ENC_ROWS, ENC_ROWS), ENC_ROWS), :]
        score = dot_nt(keys, stacked)
        top = jnp.max(score, axis=0, keepdims=True)
        weights = jnp.exp(score - top)
        total = jnp.sum(weights, axis=0, keepdims=True)
        probs = (weights * (1.0 / total)).astype(BF)
        out = dot(vt_ref[off], probs)
        mine = tile_lanes(doc_ref[block], heads) == doc
        acc_ref[block] = jnp.where(mine, out, acc_ref[block])
        norm_ref[block] = jnp.where(mine, top + jnp.log(total), norm_ref[block])
        return carry

    lax.fori_loop(0, count_ref[0], step, 0)
    for block in range(stream // QB):
        o_ref[pl.ds(block * QB, QB), :] = unstack_heads(acc_ref[block], heads).astype(BF)
    lse_ref[...] = norm_ref[...]


def cross_backward(heads, count_ref, blocks_ref, docs_ref, offs_ref, q_ref, k_ref, v_ref, do_ref, doc_ref, lse_ref, dq_ref, kt_ref, acc_ref, dka_ref, dva_ref):
    stream = q_ref.shape[0]
    for part in range(k_ref.shape[0] // ENC_ROWS):
        kt_ref[part] = k_ref[pl.ds(part * ENC_ROWS, ENC_ROWS), :].T
    acc_ref[...] = jnp.zeros_like(acc_ref)
    dka_ref[...] = jnp.zeros_like(dka_ref)
    dva_ref[...] = jnp.zeros_like(dva_ref)

    def step(t, carry):
        block, doc, off = blocks_ref[t], docs_ref[t], offs_ref[t]
        at = pl.ds(pl.multiple_of(block * QB, QB), QB)
        enc = pl.ds(pl.multiple_of(off * ENC_ROWS, ENC_ROWS), ENC_ROWS)
        stacked, douts = stack_heads(q_ref[at, :], heads), stack_heads(do_ref[at, :], heads)
        mine = tile_lanes(doc_ref[block], heads) == doc
        probs = jnp.where(mine, jnp.exp(dot_nt(k_ref[enc, :], stacked) - lse_ref[block]), 0.0)
        dprobs = dot_nt(v_ref[enc, :], douts)
        delta = jnp.sum(probs * dprobs, axis=0, keepdims=True)
        dscore = (probs * (dprobs - delta)).astype(BF)
        acc_ref[block] += dot(kt_ref[off], dscore)
        dka_ref[enc, :] += dot(dscore, stacked)
        dva_ref[enc, :] += dot(probs.astype(BF), douts)
        return carry

    lax.fori_loop(0, count_ref[0], step, 0)
    for block in range(stream // QB):
        dq_ref[pl.ds(block * QB, QB), :] = unstack_heads(acc_ref[block], heads).astype(BF)


def rows_at(start, size):
    if isinstance(start, int):
        return pl.ds(start, size)
    return pl.ds(pl.multiple_of(start, size), size)


def assemble_cols(dst, refs, order):
    if len(refs) == 1:
        dst[...] = refs[0][...]
        return
    width = refs[0].shape[1]
    for j, ref in enumerate(refs):
        dst[:, rows_at(order[j] * width, width)] = ref[...]


def assemble_weight(dst, refs, order, zorder, first=0):
    if len(refs) == 1 and len(refs[0].shape) == 4:
        count, depth, slab, _ = refs[0].shape
        width = dst.shape[1] // count
        for j in range(count):
            for p in range(depth):
                dst[rows_at(zorder[p] * slab, slab), pl.ds(j * width, width)] = refs[0][j, p, :, pl.ds(first, width)]
        return
    depth, slab, _ = refs[0].shape
    if len(refs) == 1:
        dst[...] = refs[0][0]
        return
    width = dst.shape[1] // len(refs)
    for j, ref in enumerate(refs):
        for p in range(depth):
            dst[rows_at(zorder[p] * slab, slab), rows_at(order[j] * width, width)] = ref[p, :, pl.ds(first, width)]


def assemble_slabs(dst, refs, zorder, first=0, slab=None):
    slab = slab or refs[0].shape[0]
    width = dst.shape[1]
    for p, ref in enumerate(refs):
        dst[rows_at(zorder[p] * slab, slab), :] = ref[pl.ds(0, slab), pl.ds(first, width)]


def token_rows(device, count, half):
    return rows_at(device * half, half), rows_at((2 * count - 1 - device) * half, half)


def inverse_rms(value):
    return lax.rsqrt(jnp.mean(value * value, axis=-1, keepdims=True) + EPSILON)


def norm_backward(grad, value, gain):
    scale = inverse_rms(value)
    normed = value * scale
    dnormed = grad * gain
    dvalue = scale * (dnormed - normed * jnp.mean(dnormed * normed, axis=-1, keepdims=True))
    return dvalue, jnp.sum(grad * normed, axis=0, keepdims=True)


def run(kernel, scalars, arrays, outs, scratch, name, share):
    flops, moved = share * 1.15e9, share * 1e6
    smem = pl.BlockSpec(memory_space=pltpu.SMEM)
    vmem = pl.BlockSpec(memory_space=pltpu.VMEM)
    return pl.pallas_call(
        kernel,
        in_specs=[smem] * len(scalars) + [vmem] * len(arrays),
        out_specs=[vmem] * len(outs),
        out_shape=[jax.ShapeDtypeStruct(shape, kind) for shape, kind in outs],
        scratch_shapes=[pltpu.VMEM(shape, kind) for shape, kind in scratch],
        compiler_params=pltpu.CompilerParams(vmem_limit_bytes=60 << 20),
        cost_estimate=pl.CostEstimate(flops=int(flops), bytes_accessed=int(moved), transcendentals=0),
        name=name,
    )(*scalars, *arrays)


def assemble_chip(dst, mine, theirs, zorder, core, slab, half, first=0):
    for p, ref in enumerate(mine):
        rows = rows_at(zorder[p] * slab, slab)
        if not theirs:
            dst[rows, :] = ref[pl.ds(0, slab), pl.ds(first, dst.shape[1])]
            continue
        for t in range(dst.shape[1] // (2 * half)):
            lanes = pl.ds(first + t * half, half)
            dst[rows, rows_at(2 * t * half + core * half, half)] = ref[pl.ds(0, slab), lanes]
            dst[rows, rows_at(2 * t * half + (1 - core) * half, half)] = theirs[p][pl.ds(0, slab), lanes]


def store_chip_pieces(value_rows, chip, chips, half, own_ref, away_refs):
    for d in range(chips):
        low, high = token_rows(chip ^ d, chips, half)
        rows = jnp.concatenate([value_rows(low), value_rows(high)], axis=0)
        if d:
            away_refs[d - 1][...] = rows.astype(BF)
        else:
            own_ref[...] = rows


def pick_first(places, qkv_ref, o1_ref, o2_ref, bias_ref, gains_ref, out_ref):
    slab, size = qkv_ref.shape
    part = pl.program_id(0)
    out_ref[pl.ds(0, slab), :] = jnp.where(part < 3, qkv_ref[...], jnp.where(part == 3, o1_ref[...], o2_ref[...]))
    out_ref[pl.ds(slab, 16), :] = jnp.zeros((16, size), BF)
    for t in range(-(-gains_ref.shape[1] // size)):
        @pl.when(part == t)
        def _():
            out_ref[pl.ds(slab + 8, 3), :] = gains_ref[:, pl.ds(t * size, size)]

    @pl.when(part == 0)
    def _():
        out_ref[pl.ds(slab, bias_ref.shape[0]), pl.ds(0, H)] = bias_ref[...]


def first_weights(at, self_qkv, self_out, cross_out, rel_bias, norm_gains, size):
    slab = self_qkv.shape[0]
    step = H * DK // size
    whole = lambda p, at: (0, 0)
    return pl.pallas_call(
        pick_first,
        grid_spec=pltpu.PrefetchScalarGridSpec(
            num_scalar_prefetch=1,
            grid=(5,),
            in_specs=[
                pl.BlockSpec((slab, size), lambda p, at: (0, jnp.minimum(p, 2) * step + at[0])),
                pl.BlockSpec((slab, size), lambda p, at: (0, at[0])),
                pl.BlockSpec((slab, size), lambda p, at: (0, at[0])),
                pl.BlockSpec(rel_bias.shape, whole),
                pl.BlockSpec(norm_gains.shape, whole),
            ],
            out_specs=pl.BlockSpec((slab + 16, size), lambda p, at: (0, p)),
        ),
        out_shape=jax.ShapeDtypeStruct((slab + 16, 5 * size), BF),
        compiler_params=pltpu.CompilerParams(vmem_limit_bytes=16 << 20),
        cost_estimate=pl.CostEstimate(flops=10**9, bytes_accessed=10**6, transcendentals=0),
        name="first_weights",
    )(at.astype(jnp.int32)[None], self_qkv, self_out, cross_out, rel_bias, norm_gains)


def self_project(chips, depth, sides, heads, place, corder, zorder, ids_ref, *refs):
    hidden, mine, theirs = refs[:chips], refs[chips : chips + depth], refs[chips + depth : chips + depth * sides]
    x_ref, h_ref, q_ref, kv_ref, near_ref, gains_ref, w_ref = refs[chips + depth * sides :]
    half = hidden[0].shape[0] // 2
    slab = D // depth
    width = heads * DK
    aux = [w[pl.ds(slab, 16), :].astype(F32) for w in mine]
    for p in range(depth):
        gains_ref[:, rows_at(zorder[p] * slab, slab)] = aux[p][8:, :slab]
    assemble_chip(w_ref, mine, theirs, zorder, place[0], slab, width // 2)
    per = BUCKETS // depth
    lane = lax.broadcasted_iota(jnp.int32, (per, H), 1)
    for h in range(heads):
        pick = lane == place[1] * heads + h
        bias = [jnp.sum(jnp.where(pick, aux[p][:per, :H], 0.0), axis=1, keepdims=True) for p in range(depth)]
        far = sum(jnp.where(zorder[p] == depth - 1, bias[p][per - 1 : per], 0.0) for p in range(depth))
        for a in range(7):
            tile = jnp.zeros((QB // 2, QB), F32)
            if a not in (0, 6):
                for p in range(depth):
                    for r in range(per):
                        tile = jnp.where(ids_ref[a] == zorder[p] * per + r, bias[p][r : r + 1] - far, tile)
            near_ref[a, :, pl.ds(h * QB, QB)] = tile
    gain = gains_ref[0:1, :]
    for p in range(chips):
        rows = hidden[p][...]
        value = rows.astype(F32)
        low = (value * inverse_rms(value) * gain).astype(BF)
        for part, at in enumerate(token_rows(corder[p], chips, half)):
            x_ref[at, :] = rows[part * half : (part + 1) * half]
            h_ref[at, :] = low[part * half : (part + 1) * half]
    for r in range(0, x_ref.shape[0], 256):
        at = pl.ds(r, 256)
        proj = dot(h_ref[at, :], w_ref[...]).astype(BF)
        q_ref[at, :] = proj[:, :width]
        kv_ref[at, :] = proj[:, width:]


def self_attend(chips, heads, place, q_ref, mine_ref, theirs_ref, near_ref, start_ref, place_ref, k_ref, v_ref, o_ref, lse_ref, vt_ref):
    width = heads * DK
    core = place[0]
    for l in range(2 * chips):
        rows = pl.ds(l * 64, 64)
        for ref, side in ((mine_ref, core), (theirs_ref, 1 - core)):
            at = rows_at(block_place(l, side, chips) * 64, 64)
            k_ref[at, :] = ref[rows, pl.ds(0, width)]
            v_ref[at, :] = ref[rows, pl.ds(width, width)]
    self_forward(heads, core, q_ref, k_ref, v_ref, near_ref, start_ref, place_ref, o_ref, lse_ref, vt_ref)


def slabs(refs, depth, wide, zorder):
    if wide:
        return [refs[0].at[p] for p in range(depth)], [refs[1].at[p] for p in range(depth)], zorder, refs[2:]
    return refs[:depth], [], zorder, refs[depth:]


def encoder_block(chips, depth, wide, place, zorder, enc_ref, *refs):
    mine, theirs, zorder, (kv_ref, w_ref) = slabs(refs, depth, wide, zorder)
    width = kv_ref.shape[1] // 2
    rows = enc_ref.shape[1]
    slab = D // depth
    assemble_chip(w_ref, mine, theirs, zorder, place[0], slab, width // 2, width // 2 if wide else width)
    for j in range(chips):
        kv_ref[pl.ds(j * rows, rows), :] = dot(enc_ref[2 * j + place[0]], w_ref[...]).astype(BF)


def encoder_grad(chips, place, keep_ref, come_ref, w_ref, enc_ref, grad_ref, own_ref, *refs):
    away_refs, (dkv_ref,) = refs[: chips - 1], refs[chips - 1 :]
    rows = keep_ref.shape[0] // chips
    core, chip = place[0], place[1]
    total = jnp.zeros(grad_ref.shape, F32)
    for j in range(chips):
        at = pl.ds(j * rows, rows)
        low = (keep_ref[at, :] + come_ref[at, :].astype(F32)).astype(BF)
        dkv_ref[at, :] = low
        total = total + dot_tn(enc_ref[2 * j + core], low)
    grad_ref[...] = total.astype(BF)
    for d in range(chips):
        part = dot_nt(dkv_ref[rows_at((chip ^ d) * rows, rows), :], w_ref[...])
        if d:
            away_refs[d - 1][...] = part.astype(BF)
        else:
            own_ref[...] = part


def cross_block(n_cols, n_w, depth, wide, heads, chips_rows, place, order, corder, zorder, count_ref, blocks_ref, docs_ref, offs_ref, x_ref, gains_ref, kvm_ref, kvt_ref, doc_ref, *refs):
    pieces, outs = refs[:n_cols], refs[n_cols : n_cols + n_w]
    mine, theirs, slab_order, rest = slabs(refs[n_cols + n_w :], depth, wide, zorder)
    kc_ref, vc_ref, x1_ref, h_ref, q_ref, o_ref, lse_ref, wrows_ref, ob_ref, w_ref, wq_ref, vt_ref, acc_ref, norm_ref = rest
    width = heads * DK
    count = 2 * kvm_ref.shape[0] // chips_rows
    for j in range(count // 2):
        at = pl.ds(j * chips_rows, chips_rows)
        for ref, side in ((kvm_ref, place[0]), (kvt_ref, 1 - place[0])):
            to = rows_at((2 * j + side) * chips_rows, chips_rows)
            kc_ref[to, :] = ref[at, pl.ds(0, width)]
            vc_ref[to, :] = ref[at, pl.ds(width, width)]
    assemble_cols(ob_ref, pieces, corder)
    assemble_weight(w_ref, outs, order, zorder)
    assemble_chip(wq_ref, mine, theirs, slab_order, place[0], D // depth, width // 2)
    wrows_ref[...] = w_ref[rows_at(place[1] * width, width), :]
    gain = gains_ref[1:2, :]
    for r in range(0, x_ref.shape[0], 256):
        at = pl.ds(r, 256)
        x1 = x_ref[at, :].astype(F32) + dot(ob_ref[at, :], w_ref[...])
        x1_ref[at, :] = x1
        low = (x1 * inverse_rms(x1) * gain).astype(BF)
        h_ref[at, :] = low
        q_ref[at, :] = dot(low, wq_ref[...]).astype(BF)
    cross_forward(heads, count_ref, blocks_ref, docs_ref, offs_ref, q_ref, kc_ref, vc_ref, doc_ref, o_ref, lse_ref, vt_ref, acc_ref, norm_ref)


def gelu_parts(gate):
    inner = math.sqrt(2.0 / math.pi)
    square = gate * gate
    slope = jnp.tanh(inner * (gate + 0.044715 * gate * square))
    value = 0.5 * gate * (1.0 + slope)
    grad = 0.5 * (1.0 + slope) + 0.5 * gate * (1.0 - slope * slope) * inner * (1.0 + 3 * 0.044715 * square)
    return value, grad


def unpack_units(packed_ref, in_ref, down_ref, piece):
    depth, _, wide = packed_ref.shape
    slab = D // depth
    third = (packed_ref.shape[1] - slab - piece)
    down_ref[pl.ds(depth * piece, down_ref.shape[0] - depth * piece), :] = jnp.zeros((down_ref.shape[0] - depth * piece, D), BF)
    for z in range(depth):
        in_ref[pl.ds(z * slab, slab), :] = packed_ref[z, pl.ds(0, slab), :]
        down_ref[pl.ds(z * piece, piece), pl.ds(0, wide)] = packed_ref[z, pl.ds(slab, piece), :]
        for t in range(wide // (D - wide)):
            size = min(third, piece - t * third)
            down_ref[pl.ds(z * piece + t * third, size), pl.ds(wide, D - wide)] = packed_ref[z, pl.ds(slab + piece, size), pl.ds(t * (D - wide), D - wide)]


def ffn_block(chips, n_cols, n_w, packed, first, piece, place, order, corder, zorder, x1_ref, gains_ref, *refs):
    grads, refs = refs[:chips], refs[chips:]
    pieces, outs = refs[:n_cols], refs[n_cols : n_cols + n_w]
    units_in = refs[n_cols + n_w : n_cols + n_w + (2 if packed else 4)]
    ocb_ref, g_ref, h_ref, act0_ref, act1_ref, dgu0_ref, dgu1_ref, keep_ref, wrows_ref, down0_ref, down1_ref, own_ref, *rest = refs[n_cols + n_w + len(units_in) :]
    away_refs, (w_ref, in0_ref, in1_ref, x2_ref, dh_ref) = rest[: chips - 1], rest[chips - 1 :]
    half = own_ref.shape[0] // 2
    units = act0_ref.shape[1]
    width = wrows_ref.shape[0]
    if packed:
        unpack_units(units_in[0], in0_ref, down0_ref, piece)
        unpack_units(units_in[1], in1_ref, down1_ref, piece)
    else:
        for dst, src in zip((in0_ref, in1_ref, down0_ref, down1_ref), units_in):
            dst[...] = src[...]
    assemble_cols(ocb_ref, pieces, corder)
    assemble_weight(w_ref, outs, order, zorder, first)
    wrows_ref[...] = w_ref[rows_at(place[1] * width, width), :]
    for p in range(chips):
        for part, at in enumerate(token_rows(corder[p], chips, half)):
            g_ref[at, :] = grads[p][pl.ds(part * half, half), :]
    gain = gains_ref[2:3, :]
    for r in range(0, x1_ref.shape[0], 256):
        at = pl.ds(r, 256)
        x2 = x1_ref[at, :] + dot(ocb_ref[at, :], w_ref[...])
        x2_ref[at, :] = x2
        low = (x2 * inverse_rms(x2) * gain).astype(BF)
        h_ref[at, :] = low
        total = None
        for in_ref, down_ref, act_ref, dgu_ref in ((in0_ref, down0_ref, act0_ref, dgu0_ref), (in1_ref, down1_ref, act1_ref, dgu1_ref)):
            both = dot(low, in_ref[...])
            gate, up = both[:, :units], both[:, units:]
            value, slope = gelu_parts(gate)
            act_ref[at, :] = (value * up).astype(BF)
            dact = dot_nt(g_ref[at, :], down_ref[...])
            dgu = jnp.concatenate([dact * up * slope, dact * value], axis=1).astype(BF)
            dgu_ref[at, :] = dgu
            part = dot_nt(dgu, in_ref[...])
            total = part if total is None else total + part
        dh_ref[at, :] = total
    store_chip_pieces(lambda at: dh_ref[at, :], place[1], chips, half, own_ref, away_refs)
    low, high = token_rows(place[1], chips, half)
    keep_ref[pl.ds(0, half), :] = x2_ref[low, :]
    keep_ref[pl.ds(half, half), :] = x2_ref[high, :]


def ffn_output(chips, place, act0_ref, act1_ref, down0_ref, down1_ref, own_ref, *refs):
    away_refs, (out_ref,) = refs[: chips - 1], refs[chips - 1 :]
    for r in range(0, act0_ref.shape[0], 256):
        at = pl.ds(r, 256)
        out_ref[at, :] = dot(act0_ref[at, :], down0_ref[...]) + dot(act1_ref[at, :], down1_ref[...])
    store_chip_pieces(lambda at: out_ref[at, :], place[1], chips, own_ref.shape[0] // 2, own_ref, away_refs)


def norm_grad(index, arrived, *refs):
    own_ref, value_ref, base_ref, gains_ref, out_ref, low_ref, dgain_ref = refs[arrived:]
    total = own_ref[...]
    for ref in refs[:arrived]:
        total = total + ref[pl.ds(0, total.shape[0]), :].astype(F32)
    dvalue, dgain = norm_backward(total, value_ref[...].astype(F32), gains_ref[index : index + 1, :])
    out = base_ref[...].astype(F32) + dvalue
    out_ref[...] = out
    low_ref[...] = out.astype(BF)
    dgain_ref[...] = dgain


def cross_grad(chips, heads, place, corder, count_ref, blocks_ref, docs_ref, offs_ref, wrows_ref, q_ref, k_ref, v_ref, doc_ref, lse_ref, *refs):
    pieces = refs[:chips]
    g_ref, dq_ref, keep_ref, away_ref, do_ref, kt_ref, acc_ref, dka_ref, dva_ref = refs[chips:]
    half = pieces[0].shape[0] // 2
    width = heads * DK
    core = place[0]
    for p in range(chips):
        for part, at in enumerate(token_rows(corder[p], chips, half)):
            g_ref[at, :] = pieces[p][pl.ds(part * half, half), :]
    for r in range(0, g_ref.shape[0], 256):
        at = pl.ds(r, 256)
        do_ref[at, :] = dot_nt(g_ref[at, :], wrows_ref[...]).astype(BF)
    cross_backward(heads, count_ref, blocks_ref, docs_ref, offs_ref, q_ref, k_ref, v_ref, do_ref, doc_ref, lse_ref, dq_ref, kt_ref, acc_ref, dka_ref, dva_ref)
    rows = keep_ref.shape[0] // chips
    for j in range(chips):
        to = pl.ds(j * rows, rows)
        for src, lanes in ((dka_ref, pl.ds(0, width)), (dva_ref, pl.ds(width, width))):
            keep_ref[to, lanes] = src[rows_at((2 * j + core) * rows, rows), :]
            away_ref[to, lanes] = src[rows_at((2 * j + 1 - core) * rows, rows), :].astype(BF)


def table_sums(heads, ids_ref, dnear_ref, dfar_ref, dtable_ref):
    first = lax.broadcasted_iota(jnp.int32, (QB // 2, QB), 1) < QB // 2
    for h in range(heads):
        lanes = pl.ds(h * QB, QB)
        tiles = [dnear_ref[a, :, lanes] for a in range(7)]
        near = [jnp.where(first, tiles[3 + d] + pltpu.roll(tiles[1 + d], QB // 2, 1), 0.0) for d in range(3)]
        far = sum(jnp.sum(jnp.where(first, 0.0, tiles[a]) if a < 6 else tiles[a], axis=0, keepdims=True) for a in (4, 5, 6))
        sums = []
        for bucket in range(BUCKETS):
            parts = [jnp.where(ids_ref[3 + d] == bucket, near[d], 0.0) for d in range(3)]
            sums.append(jnp.sum(parts[0] + parts[1] + parts[2], axis=0, keepdims=True))
        sums[-1] = sums[-1] + far + dfar_ref[:, lanes]
        dtable_ref[h] = jnp.concatenate(sums, axis=0)


def self_grad(chips, n_cols, n_w, heads, first, place, order, corder, zorder, x1_ref, gb2_ref, own_ref, gains_ref, wo_ref, q_ref, k_ref, v_ref, lse_ref, near_ref, start_ref, place_ref, ids_ref, *refs):
    pieces, outs = refs[:n_cols], refs[n_cols : n_cols + n_w]
    gb1_ref, dq_ref, keep_ref, away_ref, dtable_ref, gx1_ref, dgain_ref, dnear_ref, dfar_ref, dqc_ref, w_ref, dx_ref, do_ref, dkv_ref, ds_ref, p_ref, kt_ref = refs[n_cols + n_w :]
    half = own_ref.shape[0] // 2
    core = place[0]
    assemble_cols(dqc_ref, pieces, corder)
    assemble_weight(w_ref, outs, order, zorder, first)
    gain = gains_ref[1:2, :]
    total = jnp.zeros_like(gain)
    for r in range(0, x1_ref.shape[0], 256):
        at = pl.ds(r, 256)
        dh = dot_nt(dqc_ref[at, :], w_ref[...])
        dvalue, dgain = norm_backward(dh, x1_ref[at, :], gain)
        total = total + dgain
        dx_ref[at, :] = dvalue
        low = (gb2_ref[at, :].astype(F32) + dvalue).astype(BF)
        gb1_ref[at, :] = low
        do_ref[at, :] = dot_nt(low, wo_ref[...]).astype(BF)
    dgain_ref[...] = total
    for part, at in enumerate(token_rows(place[1], chips, half)):
        mine = pl.ds(part * half, half)
        gx1_ref[mine, :] = own_ref[mine, :] + dx_ref[at, :]
    self_backward(heads, core, q_ref, k_ref, v_ref, do_ref, lse_ref, near_ref, start_ref, place_ref, dq_ref, dkv_ref, dnear_ref, dfar_ref, ds_ref, p_ref, kt_ref)
    for l in range(2 * chips):
        rows = pl.ds(l * 64, 64)
        keep_ref[rows, :] = dkv_ref[rows_at(block_place(l, core, chips) * 64, 64), :]
        away_ref[rows, :] = dkv_ref[rows_at(block_place(l, 1 - core, chips) * 64, 64), :].astype(BF)
    table_sums(heads, ids_ref, dnear_ref, dfar_ref, dtable_ref)


def self_close(chips, place, x_ref, dq_ref, keep_ref, come_ref, w_ref, *refs):
    more, (dqkv_ref, dgain_ref, own_ref, *refs) = refs[: chips - 1], refs[chips - 1 :]
    away_refs, (dx_ref,) = refs[: chips - 1], refs[chips - 1 :]
    width = dq_ref.shape[1]
    total = jnp.zeros_like(dgain_ref)
    for r in range(0, dq_ref.shape[0], 256):
        at = pl.ds(r, 256)
        dqkv_ref[at, pl.ds(0, width)] = dq_ref[at, :]
        dqkv_ref[at, pl.ds(width, 2 * width)] = (keep_ref[at, :] + come_ref[at, :].astype(F32)).astype(BF)
        part = dot_nt(dqkv_ref[at, :], w_ref[...])
        dx_ref[at, :] = part
        value = x_ref[at, :].astype(F32)
        total = total + jnp.sum(part * (value * inverse_rms(value)), axis=0, keepdims=True)
    dgain_ref[...] = total
    tokens = own_ref.shape[0]
    for ref, piece in zip(away_refs, more):
        ref[pl.ds(tokens, piece.shape[0]), :] = piece[...]
    firsts = [ref.at[pl.ds(0, tokens)] for ref in away_refs]
    store_chip_pieces(lambda at: dx_ref[at, :], place[1], chips, tokens // 2, own_ref, firsts)


def spread_units(depth, piece, parts_ref, out_ref, down_ref):
    n, slab = parts_ref.shape[0], out_ref.shape[0]
    wide = parts_ref.shape[2]
    third = parts_ref.shape[1] - slab - piece
    for j in range(n):
        down_ref[pl.ds(j * piece, piece), pl.ds(0, wide)] = parts_ref[j, pl.ds(slab, piece), :].astype(F32)
        for t in range(wide // (D - wide)):
            size = min(third, piece - t * third)
            part = parts_ref[j, pl.ds(slab + piece, size), pl.ds(t * (D - wide), D - wide)]
            down_ref[pl.ds(j * piece + t * third, size), pl.ds(wide, D - wide)] = part.astype(F32)
    units = -(-piece * depth // 128) * 128
    for r in range(0, slab, 32):
        at = pl.ds(r, 32)
        values = [parts_ref[j, at, :].astype(F32) for j in range(n)]
        cols = [values[j][:, g * units + z * piece : g * units + (z + 1) * piece] for g in range(2) for z in range(depth) for j in range(n)]
        out_ref[at, :] = jnp.concatenate(cols, axis=1)


def spread_stacked(first, groups, parts_ref, *outs):
    n, slab = parts_ref.shape[0], parts_ref.shape[1]
    width = outs[0].shape[1] // (n * groups[0])
    for out, parts in zip(outs, groups):
        for t in range(parts):
            for j in range(n):
                out[:, pl.ds((t * n + j) * width, width)] = parts_ref[j, :, pl.ds(first + t * width, width)].astype(F32)
        first += parts * width


def spread(groups, heads, order, *refs):
    n = len(refs) - len(groups) - 2
    pieces, (*outs, gain_ref, table_ref) = refs[:n], refs[n:]
    slab = outs[0].shape[0]
    width = pieces[0].shape[1] // sum(groups)
    per = table_ref.shape[0]
    lane = lax.broadcasted_iota(jnp.int32, (per, H), 1)
    gain, table = jnp.zeros(gain_ref.shape, F32), jnp.zeros((per, H), F32)
    for j, ref in enumerate(pieces):
        first = 0
        for out, parts in zip(outs, groups):
            for t in range(parts):
                part = ref[pl.ds(0, slab), pl.ds((first + t) * width, width)]
                out[:, rows_at(t * n * width + order[j] * width, width)] = part.astype(F32)
            first += parts
        extra = ref[pl.ds(slab, 16), :].astype(F32)
        gain = gain + extra[8:11, :slab]
        for h in range(heads):
            table = table + jnp.where(lane == (order[j] // 2) * heads + h, extra[:per, h : h + 1], 0.0)
    gain_ref[...] = gain
    table_ref[...] = table


def body(
    hidden_in,
    encoder_out,
    doc_ids,
    enc_offsets,
    cotangent,
    self_qkv,
    self_out,
    rel_bias,
    cross_q,
    cross_kv,
    cross_out,
    ffn_in,
    ffn_out,
    norm_gains,
):
    n, depth = lax.axis_size("ctx"), lax.axis_size("fsdp")
    me, level = lax.axis_index("ctx"), lax.axis_index("fsdp")
    chips = n // 2
    core, chip = me % 2, me // 2
    tokens = hidden_in.shape[1]
    half = tokens // 2
    mine_tokens = tokens * chips
    stream = tokens * n
    width = D // n
    cols = 2 * width
    heads = H // chips
    slab = D // depth
    piece = FF // (depth * n)
    units = -(-piece * depth // 128) * 128
    fill = units - piece * depth
    enc_rows = encoder_out.shape[1]
    rows_all = enc_rows * n
    wide = n == 8
    own, other = me * width, (me ^ 1) * width
    sides = 2 if wide else 1
    order = jnp.stack(ctx_order(me, n)).astype(jnp.int32)
    corder = jnp.stack(chip_order(me, n)).astype(jnp.int32)
    zorder = jnp.stack([level ^ d for d in range(depth)]).astype(jnp.int32)
    place = jnp.stack([core, chip]).astype(jnp.int32)
    per = BUCKETS // depth

    def columns(value, start, size):
        return lax.dynamic_slice_in_dim(value, start, size, 1)

    def part_columns(value, parts, start, size):
        step = value.shape[1] // parts
        return jnp.concatenate([columns(value, p * step + start, size) for p in range(parts)], axis=1)

    def gather_columns(value):
        if wide:
            return chip_gather(value, n)
        groups = [[2 * k + c for k in range(chips)] for c in range(2)]
        return [lax.all_gather(value, "ctx", axis=1, tiled=True, axis_index_groups=groups)]

    def gather_whole(pieces):
        rows = jnp.zeros((D, width), BF)
        for d, value in enumerate(pieces):
            rows = lax.dynamic_update_slice(rows, value, ((level ^ d) * slab, 0))
        return [lax.all_gather(rows, "ctx", axis=1, tiled=True)[None]]

    def cross_weights(start, size):
        return jnp.concatenate([columns(cross_q, start, size), part_columns(cross_kv, 2, start, size)], axis=1)

    def first_of(at, size):
        return first_weights(at, self_qkv, self_out, cross_out, rel_bias, norm_gains, size)

    encoder = lax.all_gather(encoder_out[0], "ctx", axis=0)
    if wide:
        w_first = z_gather(first_of(me, width), depth)
        hidden = chip_gather(after(hidden_in[0], w_first[1]), n)
        w_first2 = [first_of(me ^ 1, width)] + [sibling(v, n) for v in w_first[1:]]
        ready = (*hidden, *w_first, *w_first2)
        w_out = ctx_gather(jnp.stack([v[:slab, 3 * width :] for v in w_first]), n)
        w_cout, first_cout = w_out, width
        w_cross, w_cross2 = None, None
    else:
        w_first, w_first2 = z_gather(first_of(chip, cols), depth), []
        hidden = chip_gather(hidden_in[0], n)
        w_cross, w_cross2 = z_gather(cross_weights(chip * cols, cols), depth), []
        first_cout = 0
        w_out, w_cq, w_cout = [gather_whole(z_gather(columns(w, own, width), depth)) for w in (self_out, cross_q, cross_out)]
    parts = []
    for part in range(2):
        parts += [columns(ffn_in, part * FF + z * (FF // depth) + me * piece, piece) for z in range(depth)]
        parts += [jnp.zeros((slab, fill), BF)] * (fill > 0)
    unit_in = jnp.concatenate(parts, axis=1)
    unit_down = lax.dynamic_slice_in_dim(ffn_out, me * piece, piece)
    if wide:
        third = -(-piece // 24) * 8
        tail = jnp.pad(unit_down[:, 2 * units :], ((0, 3 * third - piece), (0, 0)))
        tail = jnp.concatenate([tail[t * third : (t + 1) * third] for t in range(3)], axis=1)
        packed = jnp.concatenate([unit_in, unit_down[:, : 2 * units], tail], axis=0)
    else:
        w_in = lax.all_gather(unit_in, "fsdp", axis=0, tiled=True)
        w_down = jnp.pad(lax.all_gather(unit_down, "fsdp", axis=0, tiled=True), ((0, fill), (0, 0)))
        w_units = [w_in, sibling(w_in, n), w_down, sibling(w_down, n)]

    ids = doc_ids[0]
    offsets = enc_offsets[0]
    docs = offsets.shape[0]
    doc_range = jnp.arange(docs, dtype=jnp.int32)

    def local_tokens(value):
        low, high = value[: stream // 2].reshape(chips, 2, half), value[stream // 2 :].reshape(chips, 2, half)
        low = jnp.where(core == 0, low[:, 0], low[:, 1])
        high = jnp.where(core == 0, high[:, 1], high[:, 0])
        return jnp.concatenate([low, high], axis=0).reshape(mine_tokens)

    doc_starts = jnp.sum((ids[None, :] < doc_range[:, None]).astype(jnp.int32), axis=1)
    my_ids = local_tokens(ids)
    places = local_tokens(jnp.arange(stream, dtype=jnp.int32))[None]
    starts = jnp.sum(jnp.where(my_ids[None, :] == doc_range[:, None], doc_starts[:, None], 0), axis=0)[None]
    q_blocks = mine_tokens // QB
    first_doc = my_ids[::QB]
    spans = my_ids[QB - 1 :: QB] - first_doc + 1
    at_or_before = np.arange(q_blocks)[:, None] >= np.arange(q_blocks)[None, :]
    ends = jnp.sum(jnp.where(at_or_before, spans[None, :], 0), axis=1)
    slots = jnp.arange(q_blocks + docs, dtype=jnp.int32)
    slot_block = jnp.minimum(jnp.sum((slots[:, None] >= ends[None, :]).astype(jnp.int32), axis=1), q_blocks - 1)
    in_block = slot_block[:, None] == jnp.arange(q_blocks)[None, :]
    slot_doc = slots + jnp.sum(jnp.where(in_block, (first_doc - ends + spans)[None, :], 0), axis=1)
    slot_doc = jnp.clip(slot_doc, 0, docs - 1)
    slot_part = jnp.sum(jnp.where(slot_doc[:, None] == doc_range[None, :], (offsets // ENC_ROWS)[None, :], 0), axis=1)
    work = (jnp.sum(spans)[None], slot_block, slot_doc, slot_part)
    doc_rows = my_ids.reshape(q_blocks, 1, QB)
    near_ids = jnp.asarray(near_buckets())

    rows_bf = ((mine_tokens, cols), BF)
    full_bf = ((mine_tokens, D), BF)
    full_f32 = ((mine_tokens, D), F32)
    own_f32 = ((tokens, D), F32)
    pieces_out = [own_f32] + [((tokens, D), BF)] * (chips - 1)
    lanes = QB * heads
    near_f32 = ((7, QB // 2, lanes), F32)
    triangle = ((q_blocks // 2, 2 * QB, (q_blocks + 1) * lanes), BF)
    parted = ((rows_all // ENC_ROWS, cols, ENC_ROWS), BF)
    blocked = ((q_blocks, cols, lanes), F32)

    x, h1, query, kv, near, gains, wqkv = run(
        functools.partial(self_project, chips, depth, sides, heads), (place, corder, zorder), (near_ids, *hidden, *w_first, *w_first2),
        [full_bf, full_bf, rows_bf, ((mine_tokens, 2 * cols), BF), near_f32, ((8, D), F32), ((D, 3 * cols), BF)],
        [], "self_project", 1)
    if wide:
        w_cross = z_gather(after(cross_weights(own, width), query), depth)
    key, value, attended, lse = run(
        functools.partial(self_attend, chips, heads), (place,), (query, kv, sibling(kv, n), near, starts, places),
        [((stream, cols), BF), ((stream, cols), BF), rows_bf, ((1, mine_tokens * heads), F32)],
        [((cols, stream), BF)], "self_attend", 1)
    ob = gather_columns(attended)
    if wide:
        w_cross = [jnp.stack(list(lax.optimization_barrier((*w_cross, attended))[:depth]))]
        w_cross2 = [sibling(w_cross[0], n)]
    if wide:
        packed = lax.all_gather(after(packed, w_cross[0]), "fsdp", axis=0)
    ckv, wckv = run(
        functools.partial(encoder_block, chips, depth, wide), (place, zorder), (encoder, *w_cross, *w_cross2),
        [((rows_all // 2, 2 * cols), BF), ((D, 2 * cols), BF)], [], "encoder_block", 1)
    ckey, cvalue, x1, h2, cquery, crossed, clse, wo_rows, ob_all = run(
        functools.partial(cross_block, len(ob), len(w_out), depth, wide, heads, enc_rows), (place, order, corder, zorder, *work),
        (x, gains, ckv, sibling(ckv, n), doc_rows, *ob, *w_out, *w_cross, *w_cross2),
        [((rows_all, cols), BF)] * 2 + [full_f32, full_bf, rows_bf, rows_bf, ((q_blocks, 1, lanes), F32), ((cols, D), BF), full_bf],
        [((D, D), BF), ((D, cols), BF), parted, blocked, ((q_blocks, 1, lanes), F32)],
        "cross_block", 6)
    g_pieces = chip_gather(after(cotangent[0], ob[-1]), n)
    ocb_pieces = gather_columns(after(crossed, *g_pieces[1:]))
    if wide:
        w_units = [packed, sibling(after(packed, *ocb_pieces[1:]), n)]
    ocb, g, h3, act, act2, dgu, dgu2, x2_own, wco_rows, down, down2, *dh3 = run(
        functools.partial(ffn_block, chips, len(ocb_pieces), len(w_cout), wide, first_cout, piece), (place, order, corder, zorder),
        (x1, gains, *g_pieces, *ocb_pieces, *w_cout, *w_units),
        [full_bf, full_bf, full_bf, *[((mine_tokens, units), BF)] * 2, *[((mine_tokens, 2 * units), BF)] * 2, own_f32, ((cols, D), BF), *[((units, D), BF)] * 2, *pieces_out],
        [((D, D), BF), *[((D, 2 * units), BF)] * 2, full_f32, full_f32], "ffn_block", 14)

    if wide:
        w_cq = [lax.all_gather(after(w_cross[0][:, :, :width], crossed), "ctx", axis=0)]

    def reduce_norm(parts, index, kept, base):
        arrived = chip_reduce(parts[1:], n)
        return arrived, run(
            functools.partial(norm_grad, index, len(arrived)), (), (*arrived, parts[0], kept, base, gains),
            [own_f32, ((tokens, D), BF), ((1, D), F32)], [], "norm_grad", 3)

    def sum_pieces(parts):
        total = parts[0]
        for part in chip_reduce(parts[1:], n):
            total = total + part.astype(F32)
        return total

    def pair_sum(left, mine, theirs):
        come = sibling(dot_tn(left, theirs).astype(BF), n)
        return (dot_tn(left, mine) + come.astype(F32)).astype(BF)

    def sum_z(value):
        return lax.psum_scatter(value, "fsdp", scatter_dimension=0, tiled=True)

    def send_z(value):
        parts = [lax.dynamic_index_in_dim(value, level, 0, False)]
        for d in range(1, depth):
            away = lax.dynamic_index_in_dim(value, level ^ d, 0, False)
            parts.append(send(away, "fsdp", depth, lambda i, d=d: i ^ d))
        return parts

    def total_z(parts):
        return sum(part.astype(F32) for part in parts).astype(BF)

    arrived3, (gx2_own, gb2_own, dgain3) = reduce_norm(dh3, 2, x2_own, cotangent[0])
    pair_in = pair_sum(after(h3, *arrived3), dgu, dgu2)
    g_late = after(g, *arrived3)
    come = sibling(dot_tn(act2, g_late).astype(BF), n)
    pair_down = (dot_tn(act, g_late) + come.astype(F32)).astype(BF)[: piece * depth]
    if wide:
        down_rows = pair_down.reshape(depth, piece, D)
        rest = jnp.pad(down_rows[:, :, 2 * units :], ((0, 0), (0, 3 * third - piece), (0, 0)))
        rest = jnp.concatenate([rest[:, t * third : (t + 1) * third] for t in range(3)], axis=2)
        pair = jnp.concatenate([pair_in.reshape(depth, slab, 2 * units), down_rows[:, :, : 2 * units], rest], axis=1)
        grad_units = sum_z(after(pair.reshape(depth * (slab + piece + third), 2 * units), *w_cq))
    else:
        pair = pair_in
        grad_in, grad_down = sum_z(pair_in), sum_z(pair_down)
    gb2_pieces = chip_gather(after(gb2_own, pair, *w_cq), n)
    out_parts = run(
        functools.partial(ffn_output, chips), (place,), (after(act, *gb2_pieces[1:]), act2, down, down2), pieces_out, [full_f32], "ffn_output", 4)
    gb2, dcq, dkv_keep, dkv_away = run(
        functools.partial(cross_grad, chips, heads), (place, corder, *work), (after(wco_rows, pair, *out_parts), cquery, ckey, cvalue, doc_rows, clse, *gb2_pieces),
        [full_bf, rows_bf, ((rows_all // 2, 2 * cols), F32), ((rows_all // 2, 2 * cols), BF)],
        [rows_bf, parted, blocked, ((rows_all, cols), F32), ((rows_all, cols), F32)],
        "cross_grad", 13)
    arrived = chip_reduce(out_parts[1:], n)
    result = after(x2_own, dcq) + out_parts[0]
    for part in arrived:
        result = result + part.astype(F32)
    result = result.astype(BF)
    dcq_pieces = gather_columns(after(dcq, result))
    early = dcq_pieces[1:] or dcq_pieces
    dkv_away = after(dkv_away, *early)
    h2, ocb = lax.optimization_barrier((h2, ocb, *early))[:2]
    ckv_both, *denc = run(
        functools.partial(encoder_grad, chips), (place,), (dkv_keep, sibling(dkv_away, n), wckv, encoder),
        [((D, 2 * cols), BF), ((enc_rows, D), F32), *[((enc_rows, D), BF)] * (chips - 1)], [((rows_all // 2, 2 * cols), BF)],
        "encoder_grad", 7)

    def side_columns(value, parts, mine):
        return part_columns(value, parts, (core if mine else 1 - core) * width, width)

    def middle_of(mine):
        return jnp.concatenate([
            dot_tn(h2, side_columns(dcq, 1, mine)),
            side_columns(ckv_both, 2, mine).astype(F32),
            dot_tn(ocb, columns(gb2, own if mine else other, width)),
        ], axis=1)

    come = sibling(middle_of(False).astype(BF), n)
    middle_pair = (middle_of(True) + come.astype(F32)).astype(BF)
    gb1, dq, dkv_keep, dkv_away, dtable, gx1_own, dgain2 = run(
        functools.partial(self_grad, chips, len(dcq_pieces), len(w_cq), heads, 0), (place, order, corder, zorder),
        (after(x1, *denc, middle_pair, *([grad_units] if wide else [])), gb2, gx2_own, gains, wo_rows, query, key, value, lse, near, starts, places, near_ids, *dcq_pieces, *w_cq),
        [full_bf, rows_bf, ((mine_tokens, 2 * cols), F32), ((mine_tokens, 2 * cols), BF), ((heads, BUCKETS, QB), F32), own_f32, ((1, D), F32)],
        [near_f32, ((1, lanes), F32), full_bf, ((D, D), BF), full_f32, rows_bf, ((stream, 2 * cols), F32), triangle, triangle, ((cols, stream), BF)],
        "self_grad", 15)
    if wide:
        grad_units = lax.all_gather(after(grad_units, dcq_pieces[-1]), "ctx", axis=0)
        middle_pair = after(middle_pair, grad_units, gb1)
    middle = sum_z(middle_pair)
    dqkv, dgain1, *dh1 = run(
        functools.partial(self_close, chips), (place,), (x, dq, dkv_keep, sibling(dkv_away, n), wqkv, *denc[1:]),
        [((mine_tokens, 3 * cols), BF), ((1, D), F32), own_f32, *[((tokens + enc_rows, D), BF)] * (chips - 1)], [full_f32], "self_close", 4)

    dtable = jnp.sum(dtable, axis=2).T
    dtable = jnp.pad(dtable.reshape(depth, per, heads), ((0, 0), (0, 8 - per), (0, 4 * width - heads)))
    dgains = jnp.concatenate([dgain1, jnp.where(chip == 0, dgain2, 0.0), dgain3], axis=0)
    dgains = jnp.transpose(dgains.reshape(3, depth, slab), (1, 0, 2))
    dgains = jnp.pad(dgains, ((0, 0), (0, 5), (0, 4 * width - slab)))

    def last_of(mine):
        return jnp.concatenate([dot_tn(h1, side_columns(dqkv, 3, mine)), dot_tn(ob_all, columns(gb1, own if mine else other, width))], axis=1)

    come = sibling(last_of(False).astype(BF), n)
    last = last_of(True) + come.astype(F32)
    last = jnp.concatenate([last.reshape(depth, slab, 4 * width), dtable, dgains], axis=1).astype(BF)
    last = send_z(last)
    dh1[0] = after(dh1[0], last[1])
    arrived, (grad_hidden, _, _) = reduce_norm(dh1, 0, hidden_in[0], gx1_own)
    grad_enc = denc[0]
    for part in arrived:
        grad_enc = grad_enc + part[tokens:].astype(F32)
    if wide:
        grad_ffn_in, grad_ffn_out = run(
            functools.partial(spread_units, depth, piece), (), (grad_units,), [((slab, 2 * FF), F32), ((n * piece, D), F32)], [], "spread_units", 6)
        grad_cross_q, grad_cross_kv, grad_cross_out = run(
            functools.partial(spread_stacked, 0, (1, 2, 1)), (), (lax.all_gather(after(middle, gb1), "ctx", axis=0),),
            [((slab, D), F32), ((slab, 2 * D), F32), ((slab, D), F32)], [], "spread_stacked", 4)
        last = total_z([after(last[0], grad_hidden, grad_ffn_in), *last[1:]])
        grad_self_qkv, grad_self_out, grad_gains, grad_table = run(
            functools.partial(spread, (3, 1), heads), (order,), ctx_gather(last, n),
            [((slab, 3 * D), F32), ((slab, D), F32), ((3, slab), F32), ((per, H), F32)], [], "spread", 4)
    else:
        def place_columns(pieces, groups):
            outs, first = [], 0
            for g in groups:
                value = pieces[:, :slab, first * width : (first + g) * width].reshape(n, slab, g, width)
                outs.append(jnp.transpose(value, (1, 2, 0, 3)).reshape(slab, g * D).astype(F32))
                first += g
            return outs

        pieces = lax.all_gather(total_z(last), "ctx", axis=0)
        grad_self_qkv, grad_self_out = place_columns(pieces, (3, 1))
        extra = pieces[:, slab:].astype(F32)
        grad_gains = jnp.sum(extra[:, 8:11, :slab], axis=0)
        table = jnp.sum(extra[:, :per, :heads].reshape(chips, 2, per, heads), axis=1)
        grad_table = jnp.transpose(table, (1, 0, 2)).reshape(per, H)
        grad_cross_q, grad_cross_kv, grad_cross_out = place_columns(lax.all_gather(middle, "ctx", axis=0), (1, 2, 1))
        grad_ffn_out = lax.all_gather(grad_down, "ctx", axis=0, tiled=True).astype(F32)
        up_cols = lax.all_gather(grad_in, "ctx", axis=0).reshape(n, slab, 2, units)[..., : piece * depth]
        up_cols = up_cols.reshape(n, slab, 2 * depth, piece)
        grad_ffn_in = jnp.transpose(up_cols, (1, 2, 0, 3)).reshape(slab, 2 * FF).astype(F32)
    return (
        result[None],
        grad_hidden[None],
        grad_enc[None],
        grad_self_qkv,
        grad_self_out,
        grad_table,
        grad_cross_q,
        grad_cross_kv,
        grad_cross_out,
        grad_ffn_in,
        grad_ffn_out,
        grad_gains,
    )


def solution(mesh):
    split = P("fsdp", "ctx", None)
    rows = P("fsdp", None)
    return jax.shard_map(
        body,
        mesh=mesh,
        in_specs=(split, split, rows, rows, split) + (rows,) * 8 + (P(None, "fsdp"),),
        out_specs=(split,) * 3 + (rows,) * 8 + (P(None, "fsdp"),),
        check_vma=False,
    )
```

```python
import functools
import math

import jax
import jax.numpy as jnp
import numpy as np
from jax import lax
from jax.experimental import pallas as pl
from jax.experimental.pallas import tpu as pltpu
from jax.sharding import PartitionSpec as P

D = 1024
H = 16
DK = 64
FF = 2816
BUCKETS = 32
ENC_ROWS = 512
QB = 128
NEG = -1e30
EPSILON = 1e-06
BF = jnp.bfloat16
F32 = jnp.float32

EDGES = np.ceil(16.0 * 8.0 ** (np.arange(1, 16) / 16.0)).astype(np.int32)


def near_buckets():
    gap = np.arange(-3, 4)[:, None, None] * 64 + (np.arange(QB) // 64 * 128 + np.arange(QB) % 64)[None, None, :]
    steps = np.maximum(gap - np.arange(64)[None, :, None], 0)
    far = 16 + np.sum(steps[..., None] >= EDGES, axis=-1)
    return np.where(steps < 16, steps, far).astype(np.int32)


def dot(a, b):
    return jnp.dot(a, b, preferred_element_type=F32)


def dot_nt(a, b):
    return lax.dot_general(a, b, (((1,), (1,)), ((), ())), preferred_element_type=F32)


def dot_tn(a, b):
    return lax.dot_general(a, b, (((0,), (0,)), ((), ())), preferred_element_type=F32)


def send(value, axis, count, target):
    return lax.ppermute(value, axis, [(i, target(i)) for i in range(count)])


def first_way(i):
    return i ^ 2 if i % 2 == 0 else i ^ 4


def second_way(i):
    return i ^ 4 if i % 2 == 0 else i ^ 2


def ctx_order(me, count):
    if count == 8:
        even = (me % 2) == 0
        one, two = jnp.where(even, 2, 4), jnp.where(even, 4, 2)
        rel = [0, one, two, 6, 1, jnp.where(even, 5, 3), jnp.where(even, 3, 5), 7]
    else:
        rel = list(range(count))
    return [me ^ r for r in rel]


def ctx_gather(value, count):
    if count == 8:
        near, other = send(value, "ctx", 8, first_way), send(value, "ctx", 8, second_way)
        far = send(near, "ctx", 8, second_way)
        mine = [value, near, other, far]
        return mine + [send(v, "ctx", 8, lambda i: i ^ 1) for v in mine]
    return [value] + [send(value, "ctx", count, lambda i, d=d: i ^ d) for d in range(1, count)]


def chip_order(me, count):
    return [(me // 2) ^ r for r in range(count // 2)]


def chip_gather(value, count):
    return [value] + [send(value, "ctx", count, lambda i, d=d: i ^ (2 * d)) for d in range(1, count // 2)]


def chip_reduce(away, count):
    return [send(away[d - 1], "ctx", count, lambda i, d=d: i ^ (2 * d)) for d in range(1, count // 2)]


def sibling(value, count):
    return send(value, "ctx", count, lambda i: i ^ 1)


def after(value, *others):
    return lax.optimization_barrier((value, *others))[0]


def z_gather(value, depth):
    return [value] + [send(value, "fsdp", depth, lambda i, d=d: i ^ d) for d in range(1, depth)]


def stack_heads(rows, heads):
    if heads == 1:
        return rows
    lane = lax.broadcasted_iota(jnp.int32, rows.shape, 1) // DK
    return jnp.concatenate([jnp.where(lane == h, rows, jnp.zeros_like(rows)) for h in range(heads)], axis=0)


def unstack_heads(cols, heads):
    parts = [cols[h * DK : (h + 1) * DK, h * QB : (h + 1) * QB] for h in range(heads)]
    return jnp.concatenate(parts, axis=0).T if heads > 1 else parts[0].T


def tile_lanes(row, heads):
    return jnp.concatenate([row] * heads, axis=1) if heads > 1 else row


def block_place(l, core, chips):
    return 2 * l + (core if l < chips else 1 - core)


def self_scores(q_ref, k_ref, near_ref, start_ref, place_ref, block, shift, heads):
    rows = pl.ds(block * QB, QB)
    stacked = stack_heads(q_ref[rows, :], heads)
    starts = tile_lanes(start_ref[:, rows], heads)
    places = tile_lanes(place_ref[:, rows], heads)
    tiles = []
    for kb in range(2 * block + 2):
        score = dot_nt(k_ref[pl.ds(kb * QB, QB), :], stacked)
        if kb >= 2 * block - 1:
            first = 4 * block - 2 * kb + shift + 3
            score = score + jnp.concatenate([near_ref[first], near_ref[first - 1]], axis=0)
        at = lax.broadcasted_iota(jnp.int32, score.shape, 0) + kb * QB
        keep = at >= starts
        if kb >= 2 * block:
            keep = keep & (at <= places)
        tiles.append(jnp.where(keep, score, NEG))
    return stacked, tiles


def fold(op, tiles, reduce):
    return functools.reduce(op, [reduce(t, axis=0, keepdims=True) for t in tiles])


def self_forward(heads, core, q_ref, k_ref, v_ref, near_ref, start_ref, place_ref, o_ref, lse_ref, vt_ref):
    blocks = q_ref.shape[0] // QB
    vt_ref[...] = v_ref[...].T
    for block in range(blocks):
        shift = core if block < blocks // 2 else 1 - core
        _, tiles = self_scores(q_ref, k_ref, near_ref, start_ref, place_ref, block, shift, heads)
        top = fold(jnp.maximum, tiles, jnp.max)
        tiles = [jnp.exp(t - top) for t in tiles]
        total = fold(jnp.add, tiles, jnp.sum)
        inverse = 1.0 / total
        probs = jnp.concatenate([(t * inverse).astype(BF) for t in tiles], axis=0)
        out = dot(vt_ref[:, pl.ds(0, (block + 1) * 2 * QB)], probs)
        o_ref[pl.ds(block * QB, QB), :] = unstack_heads(out, heads).astype(BF)
        lse_ref[:, pl.ds(block * QB * heads, QB * heads)] = top + jnp.log(total)


def self_backward(heads, core, q_ref, k_ref, v_ref, do_ref, lse_ref, near_ref, start_ref, place_ref, dq_ref, dkv_ref, dnear_ref, dfar_ref, ds_ref, p_ref, kt_ref):
    blocks = q_ref.shape[0] // QB
    width = q_ref.shape[1]
    wide = heads * QB

    def spot(kb, block):
        row, first = (kb, 0) if kb < blocks // 2 else (blocks - 1 - kb, kb + 1)
        return row, (first + block - kb) * wide

    kt_ref[...] = k_ref[...].T
    dnear_ref[...] = jnp.zeros_like(dnear_ref)
    far = jnp.zeros((1, wide), F32)
    for block in range(blocks):
        shift = core if block < blocks // 2 else 1 - core
        _, tiles = self_scores(q_ref, k_ref, near_ref, start_ref, place_ref, block, shift, heads)
        douts = stack_heads(do_ref[pl.ds(block * QB, QB), :], heads)
        lse = lse_ref[:, pl.ds(block * wide, wide)]
        probs = [jnp.exp(t - lse) for t in tiles]
        dprobs = [dot_nt(v_ref[pl.ds(kb * QB, QB), :], douts) for kb in range(len(tiles))]
        delta = functools.reduce(jnp.add, [jnp.sum(a * b, axis=0, keepdims=True) for a, b in zip(probs, dprobs)])
        dscores = []
        for kb in range(len(tiles)):
            dscore = (probs[kb] * (dprobs[kb] - delta)).astype(BF)
            row, first = spot(kb // 2, block)
            at = pl.ds(kb % 2 * QB, QB), pl.ds(first, wide)
            ds_ref[row, at[0], at[1]] = dscore
            p_ref[row, at[0], at[1]] = probs[kb].astype(BF)
            dscores.append(dscore)
            exact = dscore.astype(F32)
            if kb >= 2 * block - 1:
                first = 4 * block - 2 * kb + shift + 3
                dnear_ref[first] += exact[: QB // 2]
                dnear_ref[first - 1] += exact[QB // 2 :]
            else:
                far = far + jnp.sum(exact, axis=0, keepdims=True)
        dq = dot(kt_ref[:, pl.ds(0, (block + 1) * 2 * QB)], jnp.concatenate(dscores, axis=0))
        dq_ref[pl.ds(block * QB, QB), :] = unstack_heads(dq, heads).astype(BF)
    dfar_ref[...] = far
    queries = jnp.concatenate([stack_heads(q_ref[pl.ds(b * QB, QB), :], heads) for b in range(blocks)], axis=0)
    douts = jnp.concatenate([stack_heads(do_ref[pl.ds(b * QB, QB), :], heads) for b in range(blocks)], axis=0)
    for kb in range(blocks):
        row, first = spot(kb, kb)
        lanes = pl.ds(first, (blocks - kb) * wide)
        rows = pl.ds(kb * 2 * QB, 2 * QB)
        dkv_ref[rows, pl.ds(0, width)] = dot(ds_ref[row, :, lanes], queries[kb * wide :])
        dkv_ref[rows, pl.ds(width, width)] = dot(p_ref[row, :, lanes], douts[kb * wide :])


def cross_forward(heads, count_ref, blocks_ref, docs_ref, offs_ref, q_ref, k_ref, v_ref, doc_ref, o_ref, lse_ref, vt_ref, acc_ref, norm_ref):
    stream = q_ref.shape[0]
    for part in range(v_ref.shape[0] // ENC_ROWS):
        vt_ref[part] = v_ref[pl.ds(part * ENC_ROWS, ENC_ROWS), :].T
    acc_ref[...] = jnp.zeros_like(acc_ref)
    norm_ref[...] = jnp.zeros_like(norm_ref)

    def step(t, carry):
        block, doc, off = blocks_ref[t], docs_ref[t], offs_ref[t]
        stacked = stack_heads(q_ref[pl.ds(pl.multiple_of(block * QB, QB), QB), :], heads)
        keys = k_ref[pl.ds(pl.multiple_of(off * ENC_ROWS, ENC_ROWS), ENC_ROWS), :]
        score = dot_nt(keys, stacked)
        top = jnp.max(score, axis=0, keepdims=True)
        weights = jnp.exp(score - top)
        total = jnp.sum(weights, axis=0, keepdims=True)
        probs = (weights * (1.0 / total)).astype(BF)
        out = dot(vt_ref[off], probs)
        mine = tile_lanes(doc_ref[block], heads) == doc
        acc_ref[block] = jnp.where(mine, out, acc_ref[block])
        norm_ref[block] = jnp.where(mine, top + jnp.log(total), norm_ref[block])
        return carry

    lax.fori_loop(0, count_ref[0], step, 0)
    for block in range(stream // QB):
        o_ref[pl.ds(block * QB, QB), :] = unstack_heads(acc_ref[block], heads).astype(BF)
    lse_ref[...] = norm_ref[...]


def cross_backward(heads, count_ref, blocks_ref, docs_ref, offs_ref, q_ref, k_ref, v_ref, do_ref, doc_ref, lse_ref, dq_ref, kt_ref, acc_ref, dka_ref, dva_ref):
    stream = q_ref.shape[0]
    for part in range(k_ref.shape[0] // ENC_ROWS):
        kt_ref[part] = k_ref[pl.ds(part * ENC_ROWS, ENC_ROWS), :].T
    acc_ref[...] = jnp.zeros_like(acc_ref)
    dka_ref[...] = jnp.zeros_like(dka_ref)
    dva_ref[...] = jnp.zeros_like(dva_ref)

    def step(t, carry):
        block, doc, off = blocks_ref[t], docs_ref[t], offs_ref[t]
        at = pl.ds(pl.multiple_of(block * QB, QB), QB)
        enc = pl.ds(pl.multiple_of(off * ENC_ROWS, ENC_ROWS), ENC_ROWS)
        stacked, douts = stack_heads(q_ref[at, :], heads), stack_heads(do_ref[at, :], heads)
        mine = tile_lanes(doc_ref[block], heads) == doc
        probs = jnp.where(mine, jnp.exp(dot_nt(k_ref[enc, :], stacked) - lse_ref[block]), 0.0)
        dprobs = dot_nt(v_ref[enc, :], douts)
        delta = jnp.sum(probs * dprobs, axis=0, keepdims=True)
        dscore = (probs * (dprobs - delta)).astype(BF)
        acc_ref[block] += dot(kt_ref[off], dscore)
        dka_ref[enc, :] += dot(dscore, stacked)
        dva_ref[enc, :] += dot(probs.astype(BF), douts)
        return carry

    lax.fori_loop(0, count_ref[0], step, 0)
    for block in range(stream // QB):
        dq_ref[pl.ds(block * QB, QB), :] = unstack_heads(acc_ref[block], heads).astype(BF)


def rows_at(start, size):
    if isinstance(start, int):
        return pl.ds(start, size)
    return pl.ds(pl.multiple_of(start, size), size)


def assemble_cols(dst, refs, order):
    if len(refs) == 1:
        dst[...] = refs[0][...]
        return
    width = refs[0].shape[1]
    for j, ref in enumerate(refs):
        dst[:, rows_at(order[j] * width, width)] = ref[...]


def assemble_weight(dst, refs, order, zorder, first=0):
    if len(refs) == 1 and len(refs[0].shape) == 4:
        count, depth, slab, _ = refs[0].shape
        width = dst.shape[1] // count
        for j in range(count):
            for p in range(depth):
                dst[rows_at(zorder[p] * slab, slab), pl.ds(j * width, width)] = refs[0][j, p, :, pl.ds(first, width)]
        return
    depth, slab, _ = refs[0].shape
    if len(refs) == 1:
        dst[...] = refs[0][0]
        return
    width = dst.shape[1] // len(refs)
    for j, ref in enumerate(refs):
        for p in range(depth):
            dst[rows_at(zorder[p] * slab, slab), rows_at(order[j] * width, width)] = ref[p, :, pl.ds(first, width)]


def assemble_slabs(dst, refs, zorder, first=0, slab=None):
    slab = slab or refs[0].shape[0]
    width = dst.shape[1]
    for p, ref in enumerate(refs):
        dst[rows_at(zorder[p] * slab, slab), :] = ref[pl.ds(0, slab), pl.ds(first, width)]


def token_rows(device, count, half):
    return rows_at(device * half, half), rows_at((2 * count - 1 - device) * half, half)


def inverse_rms(value):
    return lax.rsqrt(jnp.mean(value * value, axis=-1, keepdims=True) + EPSILON)


def norm_backward(grad, value, gain):
    scale = inverse_rms(value)
    normed = value * scale
    dnormed = grad * gain
    dvalue = scale * (dnormed - normed * jnp.mean(dnormed * normed, axis=-1, keepdims=True))
    return dvalue, jnp.sum(grad * normed, axis=0, keepdims=True)


def run(kernel, scalars, arrays, outs, scratch, name, share):
    flops, moved = share * 1.15e9, share * 1e6
    smem = pl.BlockSpec(memory_space=pltpu.SMEM)
    vmem = pl.BlockSpec(memory_space=pltpu.VMEM)
    return pl.pallas_call(
        kernel,
        in_specs=[smem] * len(scalars) + [vmem] * len(arrays),
        out_specs=[vmem] * len(outs),
        out_shape=[jax.ShapeDtypeStruct(shape, kind) for shape, kind in outs],
        scratch_shapes=[pltpu.VMEM(shape, kind) for shape, kind in scratch],
        compiler_params=pltpu.CompilerParams(vmem_limit_bytes=60 << 20),
        cost_estimate=pl.CostEstimate(flops=int(flops), bytes_accessed=int(moved), transcendentals=0),
        name=name,
    )(*scalars, *arrays)


def assemble_chip(dst, mine, theirs, zorder, core, slab, half, first=0):
    for p, ref in enumerate(mine):
        rows = rows_at(zorder[p] * slab, slab)
        if not theirs:
            dst[rows, :] = ref[pl.ds(0, slab), pl.ds(first, dst.shape[1])]
            continue
        for t in range(dst.shape[1] // (2 * half)):
            lanes = pl.ds(first + t * half, half)
            dst[rows, rows_at(2 * t * half + core * half, half)] = ref[pl.ds(0, slab), lanes]
            dst[rows, rows_at(2 * t * half + (1 - core) * half, half)] = theirs[p][pl.ds(0, slab), lanes]


def store_chip_pieces(value_rows, chip, chips, half, own_ref, away_refs):
    for d in range(chips):
        low, high = token_rows(chip ^ d, chips, half)
        rows = jnp.concatenate([value_rows(low), value_rows(high)], axis=0)
        if d:
            away_refs[d - 1][...] = rows.astype(BF)
        else:
            own_ref[...] = rows


def pick_first(places, qkv_ref, o1_ref, o2_ref, bias_ref, gains_ref, out_ref):
    slab, size = qkv_ref.shape
    part = pl.program_id(0)
    out_ref[pl.ds(0, slab), :] = jnp.where(part < 3, qkv_ref[...], jnp.where(part == 3, o1_ref[...], o2_ref[...]))
    out_ref[pl.ds(slab, 16), :] = jnp.zeros((16, size), BF)
    for t in range(-(-gains_ref.shape[1] // size)):
        @pl.when(part == t)
        def _():
            out_ref[pl.ds(slab + 8, 3), :] = gains_ref[:, pl.ds(t * size, size)]

    @pl.when(part == 0)
    def _():
        out_ref[pl.ds(slab, bias_ref.shape[0]), pl.ds(0, H)] = bias_ref[...]


def first_weights(at, self_qkv, self_out, cross_out, rel_bias, norm_gains, size):
    slab = self_qkv.shape[0]
    step = H * DK // size
    whole = lambda p, at: (0, 0)
    return pl.pallas_call(
        pick_first,
        grid_spec=pltpu.PrefetchScalarGridSpec(
            num_scalar_prefetch=1,
            grid=(5,),
            in_specs=[
                pl.BlockSpec((slab, size), lambda p, at: (0, jnp.minimum(p, 2) * step + at[0])),
                pl.BlockSpec((slab, size), lambda p, at: (0, at[0])),
                pl.BlockSpec((slab, size), lambda p, at: (0, at[0])),
                pl.BlockSpec(rel_bias.shape, whole),
                pl.BlockSpec(norm_gains.shape, whole),
            ],
            out_specs=pl.BlockSpec((slab + 16, size), lambda p, at: (0, p)),
        ),
        out_shape=jax.ShapeDtypeStruct((slab + 16, 5 * size), BF),
        compiler_params=pltpu.CompilerParams(vmem_limit_bytes=16 << 20),
        cost_estimate=pl.CostEstimate(flops=10**9, bytes_accessed=10**6, transcendentals=0),
        name="first_weights",
    )(at.astype(jnp.int32)[None], self_qkv, self_out, cross_out, rel_bias, norm_gains)


def self_project(chips, depth, sides, heads, place, corder, zorder, ids_ref, *refs):
    hidden, mine, theirs = refs[:chips], refs[chips : chips + depth], refs[chips + depth : chips + depth * sides]
    x_ref, h_ref, q_ref, kv_ref, near_ref, gains_ref, w_ref = refs[chips + depth * sides :]
    half = hidden[0].shape[0] // 2
    slab = D // depth
    width = heads * DK
    aux = [w[pl.ds(slab, 16), :].astype(F32) for w in mine]
    for p in range(depth):
        gains_ref[:, rows_at(zorder[p] * slab, slab)] = aux[p][8:, :slab]
    assemble_chip(w_ref, mine, theirs, zorder, place[0], slab, width // 2)
    per = BUCKETS // depth
    lane = lax.broadcasted_iota(jnp.int32, (per, H), 1)
    for h in range(heads):
        pick = lane == place[1] * heads + h
        bias = [jnp.sum(jnp.where(pick, aux[p][:per, :H], 0.0), axis=1, keepdims=True) for p in range(depth)]
        far = sum(jnp.where(zorder[p] == depth - 1, bias[p][per - 1 : per], 0.0) for p in range(depth))
        for a in range(7):
            tile = jnp.zeros((QB // 2, QB), F32)
            if a not in (0, 6):
                for p in range(depth):
                    for r in range(per):
                        tile = jnp.where(ids_ref[a] == zorder[p] * per + r, bias[p][r : r + 1] - far, tile)
            near_ref[a, :, pl.ds(h * QB, QB)] = tile
    gain = gains_ref[0:1, :]
    for p in range(chips):
        rows = hidden[p][...]
        value = rows.astype(F32)
        low = (value * inverse_rms(value) * gain).astype(BF)
        for part, at in enumerate(token_rows(corder[p], chips, half)):
            x_ref[at, :] = rows[part * half : (part + 1) * half]
            h_ref[at, :] = low[part * half : (part + 1) * half]
    for r in range(0, x_ref.shape[0], 256):
        at = pl.ds(r, 256)
        proj = dot(h_ref[at, :], w_ref[...]).astype(BF)
        q_ref[at, :] = proj[:, :width]
        kv_ref[at, :] = proj[:, width:]


def self_attend(chips, heads, place, q_ref, mine_ref, theirs_ref, near_ref, start_ref, place_ref, k_ref, v_ref, o_ref, lse_ref, vt_ref):
    width = heads * DK
    core = place[0]
    for l in range(2 * chips):
        rows = pl.ds(l * 64, 64)
        for ref, side in ((mine_ref, core), (theirs_ref, 1 - core)):
            at = rows_at(block_place(l, side, chips) * 64, 64)
            k_ref[at, :] = ref[rows, pl.ds(0, width)]
            v_ref[at, :] = ref[rows, pl.ds(width, width)]
    self_forward(heads, core, q_ref, k_ref, v_ref, near_ref, start_ref, place_ref, o_ref, lse_ref, vt_ref)


def slabs(refs, depth, wide, zorder):
    if wide:
        return [refs[0].at[p] for p in range(depth)], [refs[1].at[p] for p in range(depth)], zorder, refs[2:]
    return refs[:depth], [], zorder, refs[depth:]


def encoder_block(chips, depth, wide, place, zorder, enc_ref, *refs):
    mine, theirs, zorder, (kv_ref, w_ref) = slabs(refs, depth, wide, zorder)
    width = kv_ref.shape[1] // 2
    rows = enc_ref.shape[1]
    slab = D // depth
    assemble_chip(w_ref, mine, theirs, zorder, place[0], slab, width // 2, width // 2 if wide else width)
    for j in range(chips):
        kv_ref[pl.ds(j * rows, rows), :] = dot(enc_ref[2 * j + place[0]], w_ref[...]).astype(BF)


def encoder_grad(chips, place, keep_ref, come_ref, w_ref, enc_ref, grad_ref, own_ref, *refs):
    away_refs, (dkv_ref,) = refs[: chips - 1], refs[chips - 1 :]
    rows = keep_ref.shape[0] // chips
    core, chip = place[0], place[1]
    total = jnp.zeros(grad_ref.shape, F32)
    for j in range(chips):
        at = pl.ds(j * rows, rows)
        low = (keep_ref[at, :] + come_ref[at, :].astype(F32)).astype(BF)
        dkv_ref[at, :] = low
        total = total + dot_tn(enc_ref[2 * j + core], low)
    grad_ref[...] = total.astype(BF)
    for d in range(chips):
        part = dot_nt(dkv_ref[rows_at((chip ^ d) * rows, rows), :], w_ref[...])
        if d:
            away_refs[d - 1][...] = part.astype(BF)
        else:
            own_ref[...] = part


def cross_block(n_cols, n_w, depth, wide, heads, chips_rows, place, order, corder, zorder, count_ref, blocks_ref, docs_ref, offs_ref, x_ref, gains_ref, kvm_ref, kvt_ref, doc_ref, *refs):
    pieces, outs = refs[:n_cols], refs[n_cols : n_cols + n_w]
    mine, theirs, slab_order, rest = slabs(refs[n_cols + n_w :], depth, wide, zorder)
    kc_ref, vc_ref, x1_ref, h_ref, q_ref, o_ref, lse_ref, wrows_ref, ob_ref, w_ref, wq_ref, vt_ref, acc_ref, norm_ref = rest
    width = heads * DK
    count = 2 * kvm_ref.shape[0] // chips_rows
    for j in range(count // 2):
        at = pl.ds(j * chips_rows, chips_rows)
        for ref, side in ((kvm_ref, place[0]), (kvt_ref, 1 - place[0])):
            to = rows_at((2 * j + side) * chips_rows, chips_rows)
            kc_ref[to, :] = ref[at, pl.ds(0, width)]
            vc_ref[to, :] = ref[at, pl.ds(width, width)]
    assemble_cols(ob_ref, pieces, corder)
    assemble_weight(w_ref, outs, order, zorder)
    assemble_chip(wq_ref, mine, theirs, slab_order, place[0], D // depth, width // 2)
    wrows_ref[...] = w_ref[rows_at(place[1] * width, width), :]
    gain = gains_ref[1:2, :]
    for r in range(0, x_ref.shape[0], 256):
        at = pl.ds(r, 256)
        x1 = x_ref[at, :].astype(F32) + dot(ob_ref[at, :], w_ref[...])
        x1_ref[at, :] = x1
        low = (x1 * inverse_rms(x1) * gain).astype(BF)
        h_ref[at, :] = low
        q_ref[at, :] = dot(low, wq_ref[...]).astype(BF)
    cross_forward(heads, count_ref, blocks_ref, docs_ref, offs_ref, q_ref, kc_ref, vc_ref, doc_ref, o_ref, lse_ref, vt_ref, acc_ref, norm_ref)


def gelu_parts(gate):
    inner = math.sqrt(2.0 / math.pi)
    square = gate * gate
    slope = jnp.tanh(inner * (gate + 0.044715 * gate * square))
    value = 0.5 * gate * (1.0 + slope)
    grad = 0.5 * (1.0 + slope) + 0.5 * gate * (1.0 - slope * slope) * inner * (1.0 + 3 * 0.044715 * square)
    return value, grad


def unpack_units(packed_ref, in_ref, down_ref, piece):
    depth, _, wide = packed_ref.shape
    slab = D // depth
    third = (packed_ref.shape[1] - slab - piece)
    down_ref[pl.ds(depth * piece, down_ref.shape[0] - depth * piece), :] = jnp.zeros((down_ref.shape[0] - depth * piece, D), BF)
    for z in range(depth):
        in_ref[pl.ds(z * slab, slab), :] = packed_ref[z, pl.ds(0, slab), :]
        down_ref[pl.ds(z * piece, piece), pl.ds(0, wide)] = packed_ref[z, pl.ds(slab, piece), :]
        for t in range(wide // (D - wide)):
            size = min(third, piece - t * third)
            down_ref[pl.ds(z * piece + t * third, size), pl.ds(wide, D - wide)] = packed_ref[z, pl.ds(slab + piece, size), pl.ds(t * (D - wide), D - wide)]


def ffn_block(chips, n_cols, n_w, packed, first, piece, place, order, corder, zorder, x1_ref, gains_ref, *refs):
    grads, refs = refs[:chips], refs[chips:]
    pieces, outs = refs[:n_cols], refs[n_cols : n_cols + n_w]
    units_in = refs[n_cols + n_w : n_cols + n_w + (2 if packed else 4)]
    ocb_ref, g_ref, h_ref, act0_ref, act1_ref, dgu0_ref, dgu1_ref, keep_ref, wrows_ref, down0_ref, down1_ref, own_ref, *rest = refs[n_cols + n_w + len(units_in) :]
    away_refs, (w_ref, in0_ref, in1_ref, x2_ref, dh_ref) = rest[: chips - 1], rest[chips - 1 :]
    half = own_ref.shape[0] // 2
    units = act0_ref.shape[1]
    width = wrows_ref.shape[0]
    if packed:
        unpack_units(units_in[0], in0_ref, down0_ref, piece)
        unpack_units(units_in[1], in1_ref, down1_ref, piece)
    else:
        for dst, src in zip((in0_ref, in1_ref, down0_ref, down1_ref), units_in):
            dst[...] = src[...]
    assemble_cols(ocb_ref, pieces, corder)
    assemble_weight(w_ref, outs, order, zorder, first)
    wrows_ref[...] = w_ref[rows_at(place[1] * width, width), :]
    for p in range(chips):
        for part, at in enumerate(token_rows(corder[p], chips, half)):
            g_ref[at, :] = grads[p][pl.ds(part * half, half), :]
    gain = gains_ref[2:3, :]
    for r in range(0, x1_ref.shape[0], 256):
        at = pl.ds(r, 256)
        x2 = x1_ref[at, :] + dot(ocb_ref[at, :], w_ref[...])
        x2_ref[at, :] = x2
        low = (x2 * inverse_rms(x2) * gain).astype(BF)
        h_ref[at, :] = low
        total = None
        for in_ref, down_ref, act_ref, dgu_ref in ((in0_ref, down0_ref, act0_ref, dgu0_ref), (in1_ref, down1_ref, act1_ref, dgu1_ref)):
            both = dot(low, in_ref[...])
            gate, up = both[:, :units], both[:, units:]
            value, slope = gelu_parts(gate)
            act_ref[at, :] = (value * up).astype(BF)
            dact = dot_nt(g_ref[at, :], down_ref[...])
            dgu = jnp.concatenate([dact * up * slope, dact * value], axis=1).astype(BF)
            dgu_ref[at, :] = dgu
            part = dot_nt(dgu, in_ref[...])
            total = part if total is None else total + part
        dh_ref[at, :] = total
    store_chip_pieces(lambda at: dh_ref[at, :], place[1], chips, half, own_ref, away_refs)
    low, high = token_rows(place[1], chips, half)
    keep_ref[pl.ds(0, half), :] = x2_ref[low, :]
    keep_ref[pl.ds(half, half), :] = x2_ref[high, :]


def ffn_output(chips, place, act0_ref, act1_ref, down0_ref, down1_ref, own_ref, *refs):
    away_refs, (out_ref,) = refs[: chips - 1], refs[chips - 1 :]
    for r in range(0, act0_ref.shape[0], 256):
        at = pl.ds(r, 256)
        out_ref[at, :] = dot(act0_ref[at, :], down0_ref[...]) + dot(act1_ref[at, :], down1_ref[...])
    store_chip_pieces(lambda at: out_ref[at, :], place[1], chips, own_ref.shape[0] // 2, own_ref, away_refs)


def norm_grad(index, arrived, *refs):
    own_ref, value_ref, base_ref, gains_ref, out_ref, low_ref, dgain_ref = refs[arrived:]
    total = own_ref[...]
    for ref in refs[:arrived]:
        total = total + ref[pl.ds(0, total.shape[0]), :].astype(F32)
    dvalue, dgain = norm_backward(total, value_ref[...].astype(F32), gains_ref[index : index + 1, :])
    out = base_ref[...].astype(F32) + dvalue
    out_ref[...] = out
    low_ref[...] = out.astype(BF)
    dgain_ref[...] = dgain


def cross_grad(chips, heads, place, corder, count_ref, blocks_ref, docs_ref, offs_ref, wrows_ref, q_ref, k_ref, v_ref, doc_ref, lse_ref, *refs):
    pieces = refs[:chips]
    g_ref, dq_ref, keep_ref, away_ref, do_ref, kt_ref, acc_ref, dka_ref, dva_ref = refs[chips:]
    half = pieces[0].shape[0] // 2
    width = heads * DK
    core = place[0]
    for p in range(chips):
        for part, at in enumerate(token_rows(corder[p], chips, half)):
            g_ref[at, :] = pieces[p][pl.ds(part * half, half), :]
    for r in range(0, g_ref.shape[0], 256):
        at = pl.ds(r, 256)
        do_ref[at, :] = dot_nt(g_ref[at, :], wrows_ref[...]).astype(BF)
    cross_backward(heads, count_ref, blocks_ref, docs_ref, offs_ref, q_ref, k_ref, v_ref, do_ref, doc_ref, lse_ref, dq_ref, kt_ref, acc_ref, dka_ref, dva_ref)
    rows = keep_ref.shape[0] // chips
    for j in range(chips):
        to = pl.ds(j * rows, rows)
        for src, lanes in ((dka_ref, pl.ds(0, width)), (dva_ref, pl.ds(width, width))):
            keep_ref[to, lanes] = src[rows_at((2 * j + core) * rows, rows), :]
            away_ref[to, lanes] = src[rows_at((2 * j + 1 - core) * rows, rows), :].astype(BF)


def table_sums(heads, ids_ref, dnear_ref, dfar_ref, dtable_ref):
    first = lax.broadcasted_iota(jnp.int32, (QB // 2, QB), 1) < QB // 2
    for h in range(heads):
        lanes = pl.ds(h * QB, QB)
        tiles = [dnear_ref[a, :, lanes] for a in range(7)]
        near = [jnp.where(first, tiles[3 + d] + pltpu.roll(tiles[1 + d], QB // 2, 1), 0.0) for d in range(3)]
        far = sum(jnp.sum(jnp.where(first, 0.0, tiles[a]) if a < 6 else tiles[a], axis=0, keepdims=True) for a in (4, 5, 6))
        sums = []
        for bucket in range(BUCKETS):
            parts = [jnp.where(ids_ref[3 + d] == bucket, near[d], 0.0) for d in range(3)]
            sums.append(jnp.sum(parts[0] + parts[1] + parts[2], axis=0, keepdims=True))
        sums[-1] = sums[-1] + far + dfar_ref[:, lanes]
        dtable_ref[h] = jnp.concatenate(sums, axis=0)


def self_grad(chips, n_cols, n_w, heads, first, place, order, corder, zorder, x1_ref, gb2_ref, own_ref, gains_ref, wo_ref, q_ref, k_ref, v_ref, lse_ref, near_ref, start_ref, place_ref, ids_ref, *refs):
    pieces, outs = refs[:n_cols], refs[n_cols : n_cols + n_w]
    gb1_ref, dq_ref, keep_ref, away_ref, dtable_ref, gx1_ref, dgain_ref, dnear_ref, dfar_ref, dqc_ref, w_ref, dx_ref, do_ref, dkv_ref, ds_ref, p_ref, kt_ref = refs[n_cols + n_w :]
    half = own_ref.shape[0] // 2
    core = place[0]
    assemble_cols(dqc_ref, pieces, corder)
    assemble_weight(w_ref, outs, order, zorder, first)
    gain = gains_ref[1:2, :]
    total = jnp.zeros_like(gain)
    for r in range(0, x1_ref.shape[0], 256):
        at = pl.ds(r, 256)
        dh = dot_nt(dqc_ref[at, :], w_ref[...])
        dvalue, dgain = norm_backward(dh, x1_ref[at, :], gain)
        total = total + dgain
        dx_ref[at, :] = dvalue
        low = (gb2_ref[at, :].astype(F32) + dvalue).astype(BF)
        gb1_ref[at, :] = low
        do_ref[at, :] = dot_nt(low, wo_ref[...]).astype(BF)
    dgain_ref[...] = total
    for part, at in enumerate(token_rows(place[1], chips, half)):
        mine = pl.ds(part * half, half)
        gx1_ref[mine, :] = own_ref[mine, :] + dx_ref[at, :]
    self_backward(heads, core, q_ref, k_ref, v_ref, do_ref, lse_ref, near_ref, start_ref, place_ref, dq_ref, dkv_ref, dnear_ref, dfar_ref, ds_ref, p_ref, kt_ref)
    for l in range(2 * chips):
        rows = pl.ds(l * 64, 64)
        keep_ref[rows, :] = dkv_ref[rows_at(block_place(l, core, chips) * 64, 64), :]
        away_ref[rows, :] = dkv_ref[rows_at(block_place(l, 1 - core, chips) * 64, 64), :].astype(BF)
    table_sums(heads, ids_ref, dnear_ref, dfar_ref, dtable_ref)


def self_close(chips, place, x_ref, dq_ref, keep_ref, come_ref, w_ref, *refs):
    more, (dqkv_ref, dgain_ref, own_ref, *refs) = refs[: chips - 1], refs[chips - 1 :]
    away_refs, (dx_ref,) = refs[: chips - 1], refs[chips - 1 :]
    width = dq_ref.shape[1]
    total = jnp.zeros_like(dgain_ref)
    for r in range(0, dq_ref.shape[0], 256):
        at = pl.ds(r, 256)
        dqkv_ref[at, pl.ds(0, width)] = dq_ref[at, :]
        dqkv_ref[at, pl.ds(width, 2 * width)] = (keep_ref[at, :] + come_ref[at, :].astype(F32)).astype(BF)
        part = dot_nt(dqkv_ref[at, :], w_ref[...])
        dx_ref[at, :] = part
        value = x_ref[at, :].astype(F32)
        total = total + jnp.sum(part * (value * inverse_rms(value)), axis=0, keepdims=True)
    dgain_ref[...] = total
    tokens = own_ref.shape[0]
    for ref, piece in zip(away_refs, more):
        ref[pl.ds(tokens, piece.shape[0]), :] = piece[...]
    firsts = [ref.at[pl.ds(0, tokens)] for ref in away_refs]
    store_chip_pieces(lambda at: dx_ref[at, :], place[1], chips, tokens // 2, own_ref, firsts)


def spread_units(depth, piece, parts_ref, out_ref, down_ref):
    n, slab = parts_ref.shape[0], out_ref.shape[0]
    wide = parts_ref.shape[2]
    third = parts_ref.shape[1] - slab - piece
    for j in range(n):
        down_ref[pl.ds(j * piece, piece), pl.ds(0, wide)] = parts_ref[j, pl.ds(slab, piece), :].astype(F32)
        for t in range(wide // (D - wide)):
            size = min(third, piece - t * third)
            part = parts_ref[j, pl.ds(slab + piece, size), pl.ds(t * (D - wide), D - wide)]
            down_ref[pl.ds(j * piece + t * third, size), pl.ds(wide, D - wide)] = part.astype(F32)
    units = -(-piece * depth // 128) * 128
    for r in range(0, slab, 32):
        at = pl.ds(r, 32)
        values = [parts_ref[j, at, :].astype(F32) for j in range(n)]
        cols = [values[j][:, g * units + z * piece : g * units + (z + 1) * piece] for g in range(2) for z in range(depth) for j in range(n)]
        out_ref[at, :] = jnp.concatenate(cols, axis=1)


def spread_stacked(first, groups, parts_ref, *outs):
    n, slab = parts_ref.shape[0], parts_ref.shape[1]
    width = outs[0].shape[1] // (n * groups[0])
    for out, parts in zip(outs, groups):
        for t in range(parts):
            for j in range(n):
                out[:, pl.ds((t * n + j) * width, width)] = parts_ref[j, :, pl.ds(first + t * width, width)].astype(F32)
        first += parts * width


def spread(groups, heads, order, *refs):
    n = len(refs) - len(groups) - 2
    pieces, (*outs, gain_ref, table_ref) = refs[:n], refs[n:]
    slab = outs[0].shape[0]
    width = pieces[0].shape[1] // sum(groups)
    per = table_ref.shape[0]
    lane = lax.broadcasted_iota(jnp.int32, (per, H), 1)
    gain, table = jnp.zeros(gain_ref.shape, F32), jnp.zeros((per, H), F32)
    for j, ref in enumerate(pieces):
        first = 0
        for out, parts in zip(outs, groups):
            for t in range(parts):
                part = ref[pl.ds(0, slab), pl.ds((first + t) * width, width)]
                out[:, rows_at(t * n * width + order[j] * width, width)] = part.astype(F32)
            first += parts
        extra = ref[pl.ds(slab, 16), :].astype(F32)
        gain = gain + extra[8:11, :slab]
        for h in range(heads):
            table = table + jnp.where(lane == (order[j] // 2) * heads + h, extra[:per, h : h + 1], 0.0)
    gain_ref[...] = gain
    table_ref[...] = table


def body(
    hidden_in,
    encoder_out,
    doc_ids,
    enc_offsets,
    cotangent,
    self_qkv,
    self_out,
    rel_bias,
    cross_q,
    cross_kv,
    cross_out,
    ffn_in,
    ffn_out,
    norm_gains,
):
    n, depth = lax.axis_size("ctx"), lax.axis_size("fsdp")
    me, level = lax.axis_index("ctx"), lax.axis_index("fsdp")
    chips = n // 2
    core, chip = me % 2, me // 2
    tokens = hidden_in.shape[1]
    half = tokens // 2
    mine_tokens = tokens * chips
    stream = tokens * n
    width = D // n
    cols = 2 * width
    heads = H // chips
    slab = D // depth
    piece = FF // (depth * n)
    units = -(-piece * depth // 128) * 128
    fill = units - piece * depth
    enc_rows = encoder_out.shape[1]
    rows_all = enc_rows * n
    wide = n == 8
    own, other = me * width, (me ^ 1) * width
    sides = 2 if wide else 1
    order = jnp.stack(ctx_order(me, n)).astype(jnp.int32)
    corder = jnp.stack(chip_order(me, n)).astype(jnp.int32)
    zorder = jnp.stack([level ^ d for d in range(depth)]).astype(jnp.int32)
    place = jnp.stack([core, chip]).astype(jnp.int32)
    per = BUCKETS // depth

    def columns(value, start, size):
        return lax.dynamic_slice_in_dim(value, start, size, 1)

    def part_columns(value, parts, start, size):
        step = value.shape[1] // parts
        return jnp.concatenate([columns(value, p * step + start, size) for p in range(parts)], axis=1)

    def gather_columns(value):
        if wide:
            return chip_gather(value, n)
        groups = [[2 * k + c for k in range(chips)] for c in range(2)]
        return [lax.all_gather(value, "ctx", axis=1, tiled=True, axis_index_groups=groups)]

    def gather_whole(pieces):
        rows = jnp.zeros((D, width), BF)
        for d, value in enumerate(pieces):
            rows = lax.dynamic_update_slice(rows, value, ((level ^ d) * slab, 0))
        return [lax.all_gather(rows, "ctx", axis=1, tiled=True)[None]]

    def cross_weights(start, size):
        return jnp.concatenate([columns(cross_q, start, size), part_columns(cross_kv, 2, start, size)], axis=1)

    def first_of(at, size):
        return first_weights(at, self_qkv, self_out, cross_out, rel_bias, norm_gains, size)

    encoder = lax.all_gather(encoder_out[0], "ctx", axis=0)
    if wide:
        w_first = z_gather(first_of(me, width), depth)
        hidden = chip_gather(after(hidden_in[0], w_first[1]), n)
        w_first2 = [first_of(me ^ 1, width)] + [sibling(v, n) for v in w_first[1:]]
        ready = (*hidden, *w_first, *w_first2)
        w_out = ctx_gather(jnp.stack([v[:slab, 3 * width :] for v in w_first]), n)
        w_cout, first_cout = w_out, width
        w_cross, w_cross2 = None, None
    else:
        w_first, w_first2 = z_gather(first_of(chip, cols), depth), []
        hidden = chip_gather(hidden_in[0], n)
        w_cross, w_cross2 = z_gather(cross_weights(chip * cols, cols), depth), []
        first_cout = 0
        w_out, w_cq, w_cout = [gather_whole(z_gather(columns(w, own, width), depth)) for w in (self_out, cross_q, cross_out)]
    parts = []
    for part in range(2):
        parts += [columns(ffn_in, part * FF + z * (FF // depth) + me * piece, piece) for z in range(depth)]
        parts += [jnp.zeros((slab, fill), BF)] * (fill > 0)
    unit_in = jnp.concatenate(parts, axis=1)
    unit_down = lax.dynamic_slice_in_dim(ffn_out, me * piece, piece)
    if wide:
        third = -(-piece // 24) * 8
        tail = jnp.pad(unit_down[:, 2 * units :], ((0, 3 * third - piece), (0, 0)))
        tail = jnp.concatenate([tail[t * third : (t + 1) * third] for t in range(3)], axis=1)
        packed = jnp.concatenate([unit_in, unit_down[:, : 2 * units], tail], axis=0)
    else:
        w_in = lax.all_gather(unit_in, "fsdp", axis=0, tiled=True)
        w_down = jnp.pad(lax.all_gather(unit_down, "fsdp", axis=0, tiled=True), ((0, fill), (0, 0)))
        w_units = [w_in, sibling(w_in, n), w_down, sibling(w_down, n)]

    ids = doc_ids[0]
    offsets = enc_offsets[0]
    docs = offsets.shape[0]
    doc_range = jnp.arange(docs, dtype=jnp.int32)

    def local_tokens(value):
        low, high = value[: stream // 2].reshape(chips, 2, half), value[stream // 2 :].reshape(chips, 2, half)
        low = jnp.where(core == 0, low[:, 0], low[:, 1])
        high = jnp.where(core == 0, high[:, 1], high[:, 0])
        return jnp.concatenate([low, high], axis=0).reshape(mine_tokens)

    doc_starts = jnp.sum((ids[None, :] < doc_range[:, None]).astype(jnp.int32), axis=1)
    my_ids = local_tokens(ids)
    places = local_tokens(jnp.arange(stream, dtype=jnp.int32))[None]
    starts = jnp.sum(jnp.where(my_ids[None, :] == doc_range[:, None], doc_starts[:, None], 0), axis=0)[None]
    q_blocks = mine_tokens // QB
    first_doc = my_ids[::QB]
    spans = my_ids[QB - 1 :: QB] - first_doc + 1
    at_or_before = np.arange(q_blocks)[:, None] >= np.arange(q_blocks)[None, :]
    ends = jnp.sum(jnp.where(at_or_before, spans[None, :], 0), axis=1)
    slots = jnp.arange(q_blocks + docs, dtype=jnp.int32)
    slot_block = jnp.minimum(jnp.sum((slots[:, None] >= ends[None, :]).astype(jnp.int32), axis=1), q_blocks - 1)
    in_block = slot_block[:, None] == jnp.arange(q_blocks)[None, :]
    slot_doc = slots + jnp.sum(jnp.where(in_block, (first_doc - ends + spans)[None, :], 0), axis=1)
    slot_doc = jnp.clip(slot_doc, 0, docs - 1)
    slot_part = jnp.sum(jnp.where(slot_doc[:, None] == doc_range[None, :], (offsets // ENC_ROWS)[None, :], 0), axis=1)
    work = (jnp.sum(spans)[None], slot_block, slot_doc, slot_part)
    doc_rows = my_ids.reshape(q_blocks, 1, QB)
    near_ids = jnp.asarray(near_buckets())

    rows_bf = ((mine_tokens, cols), BF)
    full_bf = ((mine_tokens, D), BF)
    full_f32 = ((mine_tokens, D), F32)
    own_f32 = ((tokens, D), F32)
    pieces_out = [own_f32] + [((tokens, D), BF)] * (chips - 1)
    lanes = QB * heads
    near_f32 = ((7, QB // 2, lanes), F32)
    triangle = ((q_blocks // 2, 2 * QB, (q_blocks + 1) * lanes), BF)
    parted = ((rows_all // ENC_ROWS, cols, ENC_ROWS), BF)
    blocked = ((q_blocks, cols, lanes), F32)

    x, h1, query, kv, near, gains, wqkv = run(
        functools.partial(self_project, chips, depth, sides, heads), (place, corder, zorder), (near_ids, *hidden, *w_first, *w_first2),
        [full_bf, full_bf, rows_bf, ((mine_tokens, 2 * cols), BF), near_f32, ((8, D), F32), ((D, 3 * cols), BF)],
        [], "self_project", 1)
    if wide:
        w_cross = z_gather(after(cross_weights(own, width), query), depth)
    key, value, attended, lse = run(
        functools.partial(self_attend, chips, heads), (place,), (query, kv, sibling(kv, n), near, starts, places),
        [((stream, cols), BF), ((stream, cols), BF), rows_bf, ((1, mine_tokens * heads), F32)],
        [((cols, stream), BF)], "self_attend", 1)
    ob = gather_columns(attended)
    if wide:
        w_cross = [jnp.stack(list(lax.optimization_barrier((*w_cross, attended))[:depth]))]
        w_cross2 = [sibling(w_cross[0], n)]
    if wide:
        packed = lax.all_gather(after(packed, w_cross[0]), "fsdp", axis=0)
    ckv, wckv = run(
        functools.partial(encoder_block, chips, depth, wide), (place, zorder), (encoder, *w_cross, *w_cross2),
        [((rows_all // 2, 2 * cols), BF), ((D, 2 * cols), BF)], [], "encoder_block", 1)
    ckey, cvalue, x1, h2, cquery, crossed, clse, wo_rows, ob_all = run(
        functools.partial(cross_block, len(ob), len(w_out), depth, wide, heads, enc_rows), (place, order, corder, zorder, *work),
        (x, gains, ckv, sibling(ckv, n), doc_rows, *ob, *w_out, *w_cross, *w_cross2),
        [((rows_all, cols), BF)] * 2 + [full_f32, full_bf, rows_bf, rows_bf, ((q_blocks, 1, lanes), F32), ((cols, D), BF), full_bf],
        [((D, D), BF), ((D, cols), BF), parted, blocked, ((q_blocks, 1, lanes), F32)],
        "cross_block", 6)
    g_pieces = chip_gather(after(cotangent[0], ob[-1]), n)
    ocb_pieces = gather_columns(after(crossed, *g_pieces[1:]))
    if wide:
        w_units = [packed, sibling(after(packed, *ocb_pieces[1:]), n)]
    ocb, g, h3, act, act2, dgu, dgu2, x2_own, wco_rows, down, down2, *dh3 = run(
        functools.partial(ffn_block, chips, len(ocb_pieces), len(w_cout), wide, first_cout, piece), (place, order, corder, zorder),
        (x1, gains, *g_pieces, *ocb_pieces, *w_cout, *w_units),
        [full_bf, full_bf, full_bf, *[((mine_tokens, units), BF)] * 2, *[((mine_tokens, 2 * units), BF)] * 2, own_f32, ((cols, D), BF), *[((units, D), BF)] * 2, *pieces_out],
        [((D, D), BF), *[((D, 2 * units), BF)] * 2, full_f32, full_f32], "ffn_block", 14)

    if wide:
        w_cq = [lax.all_gather(after(w_cross[0][:, :, :width], crossed), "ctx", axis=0)]

    def reduce_norm(parts, index, kept, base):
        arrived = chip_reduce(parts[1:], n)
        return arrived, run(
            functools.partial(norm_grad, index, len(arrived)), (), (*arrived, parts[0], kept, base, gains),
            [own_f32, ((tokens, D), BF), ((1, D), F32)], [], "norm_grad", 3)

    def sum_pieces(parts):
        total = parts[0]
        for part in chip_reduce(parts[1:], n):
            total = total + part.astype(F32)
        return total

    def pair_sum(left, mine, theirs):
        come = sibling(dot_tn(left, theirs).astype(BF), n)
        return (dot_tn(left, mine) + come.astype(F32)).astype(BF)

    def sum_z(value):
        return lax.psum_scatter(value, "fsdp", scatter_dimension=0, tiled=True)

    def send_z(value):
        parts = [lax.dynamic_index_in_dim(value, level, 0, False)]
        for d in range(1, depth):
            away = lax.dynamic_index_in_dim(value, level ^ d, 0, False)
            parts.append(send(away, "fsdp", depth, lambda i, d=d: i ^ d))
        return parts

    def total_z(parts):
        return sum(part.astype(F32) for part in parts).astype(BF)

    arrived3, (gx2_own, gb2_own, dgain3) = reduce_norm(dh3, 2, x2_own, cotangent[0])
    pair_in = pair_sum(after(h3, *arrived3), dgu, dgu2)
    g_late = after(g, *arrived3)
    come = sibling(dot_tn(act2, g_late).astype(BF), n)
    pair_down = (dot_tn(act, g_late) + come.astype(F32)).astype(BF)[: piece * depth]
    if wide:
        down_rows = pair_down.reshape(depth, piece, D)
        rest = jnp.pad(down_rows[:, :, 2 * units :], ((0, 0), (0, 3 * third - piece), (0, 0)))
        rest = jnp.concatenate([rest[:, t * third : (t + 1) * third] for t in range(3)], axis=2)
        pair = jnp.concatenate([pair_in.reshape(depth, slab, 2 * units), down_rows[:, :, : 2 * units], rest], axis=1)
        grad_units = sum_z(after(pair.reshape(depth * (slab + piece + third), 2 * units), *w_cq))
    else:
        pair = pair_in
        grad_in, grad_down = sum_z(pair_in), sum_z(pair_down)
    gb2_pieces = chip_gather(after(gb2_own, pair, *w_cq), n)
    out_parts = run(
        functools.partial(ffn_output, chips), (place,), (after(act, *gb2_pieces[1:]), act2, down, down2), pieces_out, [full_f32], "ffn_output", 4)
    gb2, dcq, dkv_keep, dkv_away = run(
        functools.partial(cross_grad, chips, heads), (place, corder, *work), (after(wco_rows, pair, *out_parts), cquery, ckey, cvalue, doc_rows, clse, *gb2_pieces),
        [full_bf, rows_bf, ((rows_all // 2, 2 * cols), F32), ((rows_all // 2, 2 * cols), BF)],
        [rows_bf, parted, blocked, ((rows_all, cols), F32), ((rows_all, cols), F32)],
        "cross_grad", 13)
    arrived = chip_reduce(out_parts[1:], n)
    result = after(x2_own, dcq) + out_parts[0]
    for part in arrived:
        result = result + part.astype(F32)
    result = result.astype(BF)
    dcq_pieces = gather_columns(after(dcq, result))
    early = dcq_pieces[1:] or dcq_pieces
    dkv_away = after(dkv_away, *early)
    h2, ocb = lax.optimization_barrier((h2, ocb, *early))[:2]
    ckv_both, *denc = run(
        functools.partial(encoder_grad, chips), (place,), (dkv_keep, sibling(dkv_away, n), wckv, encoder),
        [((D, 2 * cols), BF), ((enc_rows, D), F32), *[((enc_rows, D), BF)] * (chips - 1)], [((rows_all // 2, 2 * cols), BF)],
        "encoder_grad", 7)

    def side_columns(value, parts, mine):
        return part_columns(value, parts, (core if mine else 1 - core) * width, width)

    def middle_of(mine):
        return jnp.concatenate([
            dot_tn(h2, side_columns(dcq, 1, mine)),
            side_columns(ckv_both, 2, mine).astype(F32),
            dot_tn(ocb, columns(gb2, own if mine else other, width)),
        ], axis=1)

    come = sibling(middle_of(False).astype(BF), n)
    middle_pair = (middle_of(True) + come.astype(F32)).astype(BF)
    gb1, dq, dkv_keep, dkv_away, dtable, gx1_own, dgain2 = run(
        functools.partial(self_grad, chips, len(dcq_pieces), len(w_cq), heads, 0), (place, order, corder, zorder),
        (after(x1, *denc, middle_pair, *([grad_units] if wide else [])), gb2, gx2_own, gains, wo_rows, query, key, value, lse, near, starts, places, near_ids, *dcq_pieces, *w_cq),
        [full_bf, rows_bf, ((mine_tokens, 2 * cols), F32), ((mine_tokens, 2 * cols), BF), ((heads, BUCKETS, QB), F32), own_f32, ((1, D), F32)],
        [near_f32, ((1, lanes), F32), full_bf, ((D, D), BF), full_f32, rows_bf, ((stream, 2 * cols), F32), triangle, triangle, ((cols, stream), BF)],
        "self_grad", 15)
    if wide:
        grad_units = lax.all_gather(after(grad_units, *dcq_pieces[1:]), "ctx", axis=0)
        middle_pair = after(middle_pair, grad_units, gb1)
    middle = sum_z(middle_pair)
    dqkv, dgain1, *dh1 = run(
        functools.partial(self_close, chips), (place,), (x, dq, dkv_keep, sibling(dkv_away, n), wqkv, *denc[1:]),
        [((mine_tokens, 3 * cols), BF), ((1, D), F32), own_f32, *[((tokens + enc_rows, D), BF)] * (chips - 1)], [full_f32], "self_close", 4)

    dtable = jnp.sum(dtable, axis=2).T
    dtable = jnp.pad(dtable.reshape(depth, per, heads), ((0, 0), (0, 8 - per), (0, 4 * width - heads)))
    dgains = jnp.concatenate([dgain1, jnp.where(chip == 0, dgain2, 0.0), dgain3], axis=0)
    dgains = jnp.transpose(dgains.reshape(3, depth, slab), (1, 0, 2))
    dgains = jnp.pad(dgains, ((0, 0), (0, 5), (0, 4 * width - slab)))

    def last_of(mine):
        return jnp.concatenate([dot_tn(h1, side_columns(dqkv, 3, mine)), dot_tn(ob_all, columns(gb1, own if mine else other, width))], axis=1)

    come = sibling(last_of(False).astype(BF), n)
    last = last_of(True) + come.astype(F32)
    last = jnp.concatenate([last.reshape(depth, slab, 4 * width), dtable, dgains], axis=1).astype(BF)
    last = send_z(last)
    dh1[0] = after(dh1[0], last[1])
    arrived, (grad_hidden, _, _) = reduce_norm(dh1, 0, hidden_in[0], gx1_own)
    grad_enc = denc[0]
    for part in arrived:
        grad_enc = grad_enc + part[tokens:].astype(F32)
    if wide:
        grad_ffn_in, grad_ffn_out = run(
            functools.partial(spread_units, depth, piece), (), (grad_units,), [((slab, 2 * FF), F32), ((n * piece, D), F32)], [], "spread_units", 6)
        grad_cross_q, grad_cross_kv, grad_cross_out = run(
            functools.partial(spread_stacked, 0, (1, 2, 1)), (), (lax.all_gather(after(middle, gb1), "ctx", axis=0),),
            [((slab, D), F32), ((slab, 2 * D), F32), ((slab, D), F32)], [], "spread_stacked", 4)
        last = total_z([after(last[0], grad_hidden, grad_ffn_in), *last[1:]])
        grad_self_qkv, grad_self_out, grad_gains, grad_table = run(
            functools.partial(spread, (3, 1), heads), (order,), ctx_gather(last, n),
            [((slab, 3 * D), F32), ((slab, D), F32), ((3, slab), F32), ((per, H), F32)], [], "spread", 4)
    else:
        def place_columns(pieces, groups):
            outs, first = [], 0
            for g in groups:
                value = pieces[:, :slab, first * width : (first + g) * width].reshape(n, slab, g, width)
                outs.append(jnp.transpose(value, (1, 2, 0, 3)).reshape(slab, g * D).astype(F32))
                first += g
            return outs

        pieces = lax.all_gather(total_z(last), "ctx", axis=0)
        grad_self_qkv, grad_self_out = place_columns(pieces, (3, 1))
        extra = pieces[:, slab:].astype(F32)
        grad_gains = jnp.sum(extra[:, 8:11, :slab], axis=0)
        table = jnp.sum(extra[:, :per, :heads].reshape(chips, 2, per, heads), axis=1)
        grad_table = jnp.transpose(table, (1, 0, 2)).reshape(per, H)
        grad_cross_q, grad_cross_kv, grad_cross_out = place_columns(lax.all_gather(middle, "ctx", axis=0), (1, 2, 1))
        grad_ffn_out = lax.all_gather(grad_down, "ctx", axis=0, tiled=True).astype(F32)
        up_cols = lax.all_gather(grad_in, "ctx", axis=0).reshape(n, slab, 2, units)[..., : piece * depth]
        up_cols = up_cols.reshape(n, slab, 2 * depth, piece)
        grad_ffn_in = jnp.transpose(up_cols, (1, 2, 0, 3)).reshape(slab, 2 * FF).astype(F32)
    return (
        result[None],
        grad_hidden[None],
        grad_enc[None],
        grad_self_qkv,
        grad_self_out,
        grad_table,
        grad_cross_q,
        grad_cross_kv,
        grad_cross_out,
        grad_ffn_in,
        grad_ffn_out,
        grad_gains,
    )


def solution(mesh):
    split = P("fsdp", "ctx", None)
    rows = P("fsdp", None)
    return jax.shard_map(
        body,
        mesh=mesh,
        in_specs=(split, split, rows, rows, split) + (rows,) * 8 + (P(None, "fsdp"),),
        out_specs=(split,) * 3 + (rows,) * 8 + (P(None, "fsdp"),),
        check_vma=False,
    )
```

```python
import functools
import math

import jax
import jax.numpy as jnp
import numpy as np
from jax import lax
from jax.experimental import pallas as pl
from jax.experimental.pallas import tpu as pltpu
from jax.sharding import PartitionSpec as P

D = 1024
H = 16
DK = 64
FF = 2816
BUCKETS = 32
ENC_ROWS = 512
QB = 128
NEG = -1e30
EPSILON = 1e-06
BF = jnp.bfloat16
F32 = jnp.float32

EDGES = np.ceil(16.0 * 8.0 ** (np.arange(1, 16) / 16.0)).astype(np.int32)


def near_buckets():
    gap = np.arange(-3, 4)[:, None, None] * 64 + (np.arange(QB) // 64 * 128 + np.arange(QB) % 64)[None, None, :]
    steps = np.maximum(gap - np.arange(64)[None, :, None], 0)
    far = 16 + np.sum(steps[..., None] >= EDGES, axis=-1)
    return np.where(steps < 16, steps, far).astype(np.int32)


def dot(a, b):
    return jnp.dot(a, b, preferred_element_type=F32)


def dot_nt(a, b):
    return lax.dot_general(a, b, (((1,), (1,)), ((), ())), preferred_element_type=F32)


def dot_tn(a, b):
    return lax.dot_general(a, b, (((0,), (0,)), ((), ())), preferred_element_type=F32)


def send(value, axis, count, target):
    return lax.ppermute(value, axis, [(i, target(i)) for i in range(count)])


def first_way(i):
    return i ^ 2 if i % 2 == 0 else i ^ 4


def second_way(i):
    return i ^ 4 if i % 2 == 0 else i ^ 2


def ctx_order(me, count):
    if count == 8:
        even = (me % 2) == 0
        one, two = jnp.where(even, 2, 4), jnp.where(even, 4, 2)
        rel = [0, one, two, 6, 1, jnp.where(even, 5, 3), jnp.where(even, 3, 5), 7]
    else:
        rel = list(range(count))
    return [me ^ r for r in rel]


def ctx_gather(value, count):
    if count == 8:
        near, other = send(value, "ctx", 8, first_way), send(value, "ctx", 8, second_way)
        far = send(near, "ctx", 8, second_way)
        mine = [value, near, other, far]
        return mine + [send(v, "ctx", 8, lambda i: i ^ 1) for v in mine]
    return [value] + [send(value, "ctx", count, lambda i, d=d: i ^ d) for d in range(1, count)]


def chip_order(me, count):
    return [(me // 2) ^ r for r in range(count // 2)]


def chip_gather(value, count):
    return [value] + [send(value, "ctx", count, lambda i, d=d: i ^ (2 * d)) for d in range(1, count // 2)]


def chip_reduce(away, count):
    return [send(away[d - 1], "ctx", count, lambda i, d=d: i ^ (2 * d)) for d in range(1, count // 2)]


def sibling(value, count):
    return send(value, "ctx", count, lambda i: i ^ 1)


def after(value, *others):
    return lax.optimization_barrier((value, *others))[0]


def z_gather(value, depth):
    return [value] + [send(value, "fsdp", depth, lambda i, d=d: i ^ d) for d in range(1, depth)]


def stack_heads(rows, heads):
    if heads == 1:
        return rows
    lane = lax.broadcasted_iota(jnp.int32, rows.shape, 1) // DK
    return jnp.concatenate([jnp.where(lane == h, rows, jnp.zeros_like(rows)) for h in range(heads)], axis=0)


def unstack_heads(cols, heads):
    parts = [cols[h * DK : (h + 1) * DK, h * QB : (h + 1) * QB] for h in range(heads)]
    return jnp.concatenate(parts, axis=0).T if heads > 1 else parts[0].T


def tile_lanes(row, heads):
    return jnp.concatenate([row] * heads, axis=1) if heads > 1 else row


def block_place(l, core, chips):
    return 2 * l + (core if l < chips else 1 - core)


def self_scores(q_ref, k_ref, near_ref, start_ref, place_ref, block, shift, heads):
    rows = pl.ds(block * QB, QB)
    stacked = stack_heads(q_ref[rows, :], heads)
    starts = tile_lanes(start_ref[:, rows], heads)
    places = tile_lanes(place_ref[:, rows], heads)
    tiles = []
    for kb in range(2 * block + 2):
        score = dot_nt(k_ref[pl.ds(kb * QB, QB), :], stacked)
        if kb >= 2 * block - 1:
            first = 4 * block - 2 * kb + shift + 3
            score = score + jnp.concatenate([near_ref[first], near_ref[first - 1]], axis=0)
        at = lax.broadcasted_iota(jnp.int32, score.shape, 0) + kb * QB
        keep = at >= starts
        if kb >= 2 * block:
            keep = keep & (at <= places)
        tiles.append(jnp.where(keep, score, NEG))
    return stacked, tiles


def fold(op, tiles, reduce):
    return functools.reduce(op, [reduce(t, axis=0, keepdims=True) for t in tiles])


def self_forward(heads, core, q_ref, k_ref, v_ref, near_ref, start_ref, place_ref, o_ref, lse_ref, vt_ref):
    blocks = q_ref.shape[0] // QB
    vt_ref[...] = v_ref[...].T
    for block in range(blocks):
        shift = core if block < blocks // 2 else 1 - core
        _, tiles = self_scores(q_ref, k_ref, near_ref, start_ref, place_ref, block, shift, heads)
        top = fold(jnp.maximum, tiles, jnp.max)
        tiles = [jnp.exp(t - top) for t in tiles]
        total = fold(jnp.add, tiles, jnp.sum)
        inverse = 1.0 / total
        probs = jnp.concatenate([(t * inverse).astype(BF) for t in tiles], axis=0)
        out = dot(vt_ref[:, pl.ds(0, (block + 1) * 2 * QB)], probs)
        o_ref[pl.ds(block * QB, QB), :] = unstack_heads(out, heads).astype(BF)
        lse_ref[:, pl.ds(block * QB * heads, QB * heads)] = top + jnp.log(total)


def self_backward(heads, core, q_ref, k_ref, v_ref, do_ref, lse_ref, near_ref, start_ref, place_ref, dq_ref, dkv_ref, dnear_ref, dfar_ref, ds_ref, p_ref, kt_ref):
    blocks = q_ref.shape[0] // QB
    width = q_ref.shape[1]
    wide = heads * QB

    def spot(kb, block):
        row, first = (kb, 0) if kb < blocks // 2 else (blocks - 1 - kb, kb + 1)
        return row, (first + block - kb) * wide

    kt_ref[...] = k_ref[...].T
    dnear_ref[...] = jnp.zeros_like(dnear_ref)
    far = jnp.zeros((1, wide), F32)
    for block in range(blocks):
        shift = core if block < blocks // 2 else 1 - core
        _, tiles = self_scores(q_ref, k_ref, near_ref, start_ref, place_ref, block, shift, heads)
        douts = stack_heads(do_ref[pl.ds(block * QB, QB), :], heads)
        lse = lse_ref[:, pl.ds(block * wide, wide)]
        probs = [jnp.exp(t - lse) for t in tiles]
        dprobs = [dot_nt(v_ref[pl.ds(kb * QB, QB), :], douts) for kb in range(len(tiles))]
        delta = functools.reduce(jnp.add, [jnp.sum(a * b, axis=0, keepdims=True) for a, b in zip(probs, dprobs)])
        dscores = []
        for kb in range(len(tiles)):
            dscore = (probs[kb] * (dprobs[kb] - delta)).astype(BF)
            row, first = spot(kb // 2, block)
            at = pl.ds(kb % 2 * QB, QB), pl.ds(first, wide)
            ds_ref[row, at[0], at[1]] = dscore
            p_ref[row, at[0], at[1]] = probs[kb].astype(BF)
            dscores.append(dscore)
            exact = dscore.astype(F32)
            if kb >= 2 * block - 1:
                first = 4 * block - 2 * kb + shift + 3
                dnear_ref[first] += exact[: QB // 2]
                dnear_ref[first - 1] += exact[QB // 2 :]
            else:
                far = far + jnp.sum(exact, axis=0, keepdims=True)
        dq = dot(kt_ref[:, pl.ds(0, (block + 1) * 2 * QB)], jnp.concatenate(dscores, axis=0))
        dq_ref[pl.ds(block * QB, QB), :] = unstack_heads(dq, heads).astype(BF)
    dfar_ref[...] = far
    queries = jnp.concatenate([stack_heads(q_ref[pl.ds(b * QB, QB), :], heads) for b in range(blocks)], axis=0)
    douts = jnp.concatenate([stack_heads(do_ref[pl.ds(b * QB, QB), :], heads) for b in range(blocks)], axis=0)
    for kb in range(blocks):
        row, first = spot(kb, kb)
        lanes = pl.ds(first, (blocks - kb) * wide)
        rows = pl.ds(kb * 2 * QB, 2 * QB)
        dkv_ref[rows, pl.ds(0, width)] = dot(ds_ref[row, :, lanes], queries[kb * wide :])
        dkv_ref[rows, pl.ds(width, width)] = dot(p_ref[row, :, lanes], douts[kb * wide :])


def cross_forward(heads, count_ref, blocks_ref, docs_ref, offs_ref, q_ref, k_ref, v_ref, doc_ref, o_ref, lse_ref, vt_ref, acc_ref, norm_ref):
    stream = q_ref.shape[0]
    for part in range(v_ref.shape[0] // ENC_ROWS):
        vt_ref[part] = v_ref[pl.ds(part * ENC_ROWS, ENC_ROWS), :].T
    acc_ref[...] = jnp.zeros_like(acc_ref)
    norm_ref[...] = jnp.zeros_like(norm_ref)

    def step(t, carry):
        block, doc, off = blocks_ref[t], docs_ref[t], offs_ref[t]
        stacked = stack_heads(q_ref[pl.ds(pl.multiple_of(block * QB, QB), QB), :], heads)
        keys = k_ref[pl.ds(pl.multiple_of(off * ENC_ROWS, ENC_ROWS), ENC_ROWS), :]
        score = dot_nt(keys, stacked)
        top = jnp.max(score, axis=0, keepdims=True)
        weights = jnp.exp(score - top)
        total = jnp.sum(weights, axis=0, keepdims=True)
        probs = (weights * (1.0 / total)).astype(BF)
        out = dot(vt_ref[off], probs)
        mine = tile_lanes(doc_ref[block], heads) == doc
        acc_ref[block] = jnp.where(mine, out, acc_ref[block])
        norm_ref[block] = jnp.where(mine, top + jnp.log(total), norm_ref[block])
        return carry

    lax.fori_loop(0, count_ref[0], step, 0)
    for block in range(stream // QB):
        o_ref[pl.ds(block * QB, QB), :] = unstack_heads(acc_ref[block], heads).astype(BF)
    lse_ref[...] = norm_ref[...]


def cross_backward(heads, count_ref, blocks_ref, docs_ref, offs_ref, q_ref, k_ref, v_ref, do_ref, doc_ref, lse_ref, dq_ref, kt_ref, acc_ref, dka_ref, dva_ref):
    stream = q_ref.shape[0]
    for part in range(k_ref.shape[0] // ENC_ROWS):
        kt_ref[part] = k_ref[pl.ds(part * ENC_ROWS, ENC_ROWS), :].T
    acc_ref[...] = jnp.zeros_like(acc_ref)
    dka_ref[...] = jnp.zeros_like(dka_ref)
    dva_ref[...] = jnp.zeros_like(dva_ref)

    def step(t, carry):
        block, doc, off = blocks_ref[t], docs_ref[t], offs_ref[t]
        at = pl.ds(pl.multiple_of(block * QB, QB), QB)
        enc = pl.ds(pl.multiple_of(off * ENC_ROWS, ENC_ROWS), ENC_ROWS)
        stacked, douts = stack_heads(q_ref[at, :], heads), stack_heads(do_ref[at, :], heads)
        mine = tile_lanes(doc_ref[block], heads) == doc
        probs = jnp.where(mine, jnp.exp(dot_nt(k_ref[enc, :], stacked) - lse_ref[block]), 0.0)
        dprobs = dot_nt(v_ref[enc, :], douts)
        delta = jnp.sum(probs * dprobs, axis=0, keepdims=True)
        dscore = (probs * (dprobs - delta)).astype(BF)
        acc_ref[block] += dot(kt_ref[off], dscore)
        dka_ref[enc, :] += dot(dscore, stacked)
        dva_ref[enc, :] += dot(probs.astype(BF), douts)
        return carry

    lax.fori_loop(0, count_ref[0], step, 0)
    for block in range(stream // QB):
        dq_ref[pl.ds(block * QB, QB), :] = unstack_heads(acc_ref[block], heads).astype(BF)


def rows_at(start, size):
    if isinstance(start, int):
        return pl.ds(start, size)
    return pl.ds(pl.multiple_of(start, size), size)


def assemble_cols(dst, refs, order):
    if len(refs) == 1:
        dst[...] = refs[0][...]
        return
    width = refs[0].shape[1]
    for j, ref in enumerate(refs):
        dst[:, rows_at(order[j] * width, width)] = ref[...]


def assemble_weight(dst, refs, order, zorder, first=0):
    if len(refs) == 1 and len(refs[0].shape) == 4:
        count, depth, slab, _ = refs[0].shape
        width = dst.shape[1] // count
        for j in range(count):
            for p in range(depth):
                dst[rows_at(zorder[p] * slab, slab), pl.ds(j * width, width)] = refs[0][j, p, :, pl.ds(first, width)]
        return
    depth, slab, _ = refs[0].shape
    if len(refs) == 1:
        dst[...] = refs[0][0]
        return
    width = dst.shape[1] // len(refs)
    for j, ref in enumerate(refs):
        for p in range(depth):
            dst[rows_at(zorder[p] * slab, slab), rows_at(order[j] * width, width)] = ref[p, :, pl.ds(first, width)]


def assemble_slabs(dst, refs, zorder, first=0, slab=None):
    slab = slab or refs[0].shape[0]
    width = dst.shape[1]
    for p, ref in enumerate(refs):
        dst[rows_at(zorder[p] * slab, slab), :] = ref[pl.ds(0, slab), pl.ds(first, width)]


def token_rows(device, count, half):
    return rows_at(device * half, half), rows_at((2 * count - 1 - device) * half, half)


def inverse_rms(value):
    return lax.rsqrt(jnp.mean(value * value, axis=-1, keepdims=True) + EPSILON)


def norm_backward(grad, value, gain):
    scale = inverse_rms(value)
    normed = value * scale
    dnormed = grad * gain
    dvalue = scale * (dnormed - normed * jnp.mean(dnormed * normed, axis=-1, keepdims=True))
    return dvalue, jnp.sum(grad * normed, axis=0, keepdims=True)


def run(kernel, scalars, arrays, outs, scratch, name, share):
    flops, moved = share * 1.15e9, share * 1e6
    smem = pl.BlockSpec(memory_space=pltpu.SMEM)
    vmem = pl.BlockSpec(memory_space=pltpu.VMEM)
    return pl.pallas_call(
        kernel,
        in_specs=[smem] * len(scalars) + [vmem] * len(arrays),
        out_specs=[vmem] * len(outs),
        out_shape=[jax.ShapeDtypeStruct(shape, kind) for shape, kind in outs],
        scratch_shapes=[pltpu.VMEM(shape, kind) for shape, kind in scratch],
        compiler_params=pltpu.CompilerParams(vmem_limit_bytes=60 << 20),
        cost_estimate=pl.CostEstimate(flops=int(flops), bytes_accessed=int(moved), transcendentals=0),
        name=name,
    )(*scalars, *arrays)


def assemble_chip(dst, mine, theirs, zorder, core, slab, half, first=0):
    for p, ref in enumerate(mine):
        rows = rows_at(zorder[p] * slab, slab)
        if not theirs:
            dst[rows, :] = ref[pl.ds(0, slab), pl.ds(first, dst.shape[1])]
            continue
        for t in range(dst.shape[1] // (2 * half)):
            lanes = pl.ds(first + t * half, half)
            dst[rows, rows_at(2 * t * half + core * half, half)] = ref[pl.ds(0, slab), lanes]
            dst[rows, rows_at(2 * t * half + (1 - core) * half, half)] = theirs[p][pl.ds(0, slab), lanes]


def store_chip_pieces(value_rows, chip, chips, half, own_ref, away_refs):
    for d in range(chips):
        low, high = token_rows(chip ^ d, chips, half)
        rows = jnp.concatenate([value_rows(low), value_rows(high)], axis=0)
        if d:
            away_refs[d - 1][...] = rows.astype(BF)
        else:
            own_ref[...] = rows


def pick_first(places, qkv_ref, o1_ref, o2_ref, bias_ref, gains_ref, out_ref):
    slab, size = qkv_ref.shape
    part = pl.program_id(0)
    out_ref[pl.ds(0, slab), :] = jnp.where(part < 3, qkv_ref[...], jnp.where(part == 3, o1_ref[...], o2_ref[...]))
    out_ref[pl.ds(slab, 16), :] = jnp.zeros((16, size), BF)
    for t in range(-(-gains_ref.shape[1] // size)):
        @pl.when(part == t)
        def _():
            out_ref[pl.ds(slab + 8, 3), :] = gains_ref[:, pl.ds(t * size, size)]

    @pl.when(part == 0)
    def _():
        out_ref[pl.ds(slab, bias_ref.shape[0]), pl.ds(0, H)] = bias_ref[...]


def first_weights(at, self_qkv, self_out, cross_out, rel_bias, norm_gains, size):
    slab = self_qkv.shape[0]
    step = H * DK // size
    whole = lambda p, at: (0, 0)
    return pl.pallas_call(
        pick_first,
        grid_spec=pltpu.PrefetchScalarGridSpec(
            num_scalar_prefetch=1,
            grid=(5,),
            in_specs=[
                pl.BlockSpec((slab, size), lambda p, at: (0, jnp.minimum(p, 2) * step + at[0])),
                pl.BlockSpec((slab, size), lambda p, at: (0, at[0])),
                pl.BlockSpec((slab, size), lambda p, at: (0, at[0])),
                pl.BlockSpec(rel_bias.shape, whole),
                pl.BlockSpec(norm_gains.shape, whole),
            ],
            out_specs=pl.BlockSpec((slab + 16, size), lambda p, at: (0, p)),
        ),
        out_shape=jax.ShapeDtypeStruct((slab + 16, 5 * size), BF),
        compiler_params=pltpu.CompilerParams(vmem_limit_bytes=16 << 20),
        cost_estimate=pl.CostEstimate(flops=10**9, bytes_accessed=10**6, transcendentals=0),
        name="first_weights",
    )(at.astype(jnp.int32)[None], self_qkv, self_out, cross_out, rel_bias, norm_gains)


def self_project(chips, depth, sides, heads, place, corder, zorder, ids_ref, *refs):
    hidden, mine, theirs = refs[:chips], refs[chips : chips + depth], refs[chips + depth : chips + depth * sides]
    x_ref, h_ref, q_ref, kv_ref, near_ref, gains_ref, w_ref = refs[chips + depth * sides :]
    half = hidden[0].shape[0] // 2
    slab = D // depth
    width = heads * DK
    aux = [w[pl.ds(slab, 16), :].astype(F32) for w in mine]
    for p in range(depth):
        gains_ref[:, rows_at(zorder[p] * slab, slab)] = aux[p][8:, :slab]
    assemble_chip(w_ref, mine, theirs, zorder, place[0], slab, width // 2)
    per = BUCKETS // depth
    lane = lax.broadcasted_iota(jnp.int32, (per, H), 1)
    for h in range(heads):
        pick = lane == place[1] * heads + h
        bias = [jnp.sum(jnp.where(pick, aux[p][:per, :H], 0.0), axis=1, keepdims=True) for p in range(depth)]
        far = sum(jnp.where(zorder[p] == depth - 1, bias[p][per - 1 : per], 0.0) for p in range(depth))
        tiles = []
        for a in (3, 4):
            tile = jnp.zeros((QB // 2, QB), F32)
            for p in range(depth):
                for r in range(per):
                    tile = jnp.where(ids_ref[a] == zorder[p] * per + r, bias[p][r : r + 1] - far, tile)
            tiles.append(tile)
        turned = [pltpu.roll(tile, QB // 2, 1) for tile in tiles]
        half_lanes = lax.broadcasted_iota(jnp.int32, (QB // 2, QB), 1) < QB // 2
        zero = jnp.zeros((QB // 2, QB), F32)
        for a, tile in enumerate((zero, *turned, *tiles, jnp.where(half_lanes, turned[0], 0.0), zero)):
            near_ref[a, :, pl.ds(h * QB, QB)] = tile
    gain = gains_ref[0:1, :]
    for p in range(chips):
        rows = hidden[p][...]
        value = rows.astype(F32)
        low = (value * inverse_rms(value) * gain).astype(BF)
        for part, at in enumerate(token_rows(corder[p], chips, half)):
            x_ref[at, :] = rows[part * half : (part + 1) * half]
            h_ref[at, :] = low[part * half : (part + 1) * half]
    for r in range(0, x_ref.shape[0], 256):
        at = pl.ds(r, 256)
        proj = dot(h_ref[at, :], w_ref[...]).astype(BF)
        q_ref[at, :] = proj[:, :width]
        kv_ref[at, :] = proj[:, width:]


def self_attend(chips, heads, place, q_ref, mine_ref, theirs_ref, near_ref, start_ref, place_ref, k_ref, v_ref, o_ref, lse_ref, vt_ref):
    width = heads * DK
    core = place[0]
    for l in range(2 * chips):
        rows = pl.ds(l * 64, 64)
        for ref, side in ((mine_ref, core), (theirs_ref, 1 - core)):
            at = rows_at(block_place(l, side, chips) * 64, 64)
            k_ref[at, :] = ref[rows, pl.ds(0, width)]
            v_ref[at, :] = ref[rows, pl.ds(width, width)]
    self_forward(heads, core, q_ref, k_ref, v_ref, near_ref, start_ref, place_ref, o_ref, lse_ref, vt_ref)


def slabs(refs, depth, wide, zorder):
    if wide:
        return [refs[0].at[p] for p in range(depth)], [refs[1].at[p] for p in range(depth)], zorder, refs[2:]
    return refs[:depth], [], zorder, refs[depth:]


def encoder_block(chips, depth, wide, place, zorder, enc_ref, *refs):
    mine, theirs, zorder, (kv_ref, w_ref) = slabs(refs, depth, wide, zorder)
    width = kv_ref.shape[1] // 2
    rows = enc_ref.shape[1]
    slab = D // depth
    assemble_chip(w_ref, mine, theirs, zorder, place[0], slab, width // 2, width // 2 if wide else width)
    for j in range(chips):
        kv_ref[pl.ds(j * rows, rows), :] = dot(enc_ref[2 * j + place[0]], w_ref[...]).astype(BF)


def encoder_grad(chips, place, keep_ref, come_ref, w_ref, enc_ref, grad_ref, own_ref, *refs):
    away_refs, (dkv_ref,) = refs[: chips - 1], refs[chips - 1 :]
    rows = keep_ref.shape[0] // chips
    core, chip = place[0], place[1]
    total = jnp.zeros(grad_ref.shape, F32)
    for j in range(chips):
        at = pl.ds(j * rows, rows)
        low = (keep_ref[at, :] + come_ref[at, :].astype(F32)).astype(BF)
        dkv_ref[at, :] = low
        total = total + dot_tn(enc_ref[2 * j + core], low)
    grad_ref[...] = total.astype(BF)
    for d in range(chips):
        part = dot_nt(dkv_ref[rows_at((chip ^ d) * rows, rows), :], w_ref[...])
        if d:
            away_refs[d - 1][...] = part.astype(BF)
        else:
            own_ref[...] = part


def cross_block(n_cols, n_w, depth, wide, heads, chips_rows, place, order, corder, zorder, count_ref, blocks_ref, docs_ref, offs_ref, x_ref, gains_ref, kvm_ref, kvt_ref, doc_ref, *refs):
    pieces, outs = refs[:n_cols], refs[n_cols : n_cols + n_w]
    mine, theirs, slab_order, rest = slabs(refs[n_cols + n_w :], depth, wide, zorder)
    kc_ref, vc_ref, x1_ref, h_ref, q_ref, o_ref, lse_ref, wrows_ref, ob_ref, w_ref, wq_ref, vt_ref, acc_ref, norm_ref = rest
    width = heads * DK
    count = 2 * kvm_ref.shape[0] // chips_rows
    for j in range(count // 2):
        at = pl.ds(j * chips_rows, chips_rows)
        for ref, side in ((kvm_ref, place[0]), (kvt_ref, 1 - place[0])):
            to = rows_at((2 * j + side) * chips_rows, chips_rows)
            kc_ref[to, :] = ref[at, pl.ds(0, width)]
            vc_ref[to, :] = ref[at, pl.ds(width, width)]
    assemble_cols(ob_ref, pieces, corder)
    assemble_weight(w_ref, outs, order, zorder)
    assemble_chip(wq_ref, mine, theirs, slab_order, place[0], D // depth, width // 2)
    wrows_ref[...] = w_ref[rows_at(place[1] * width, width), :]
    gain = gains_ref[1:2, :]
    for r in range(0, x_ref.shape[0], 256):
        at = pl.ds(r, 256)
        x1 = x_ref[at, :].astype(F32) + dot(ob_ref[at, :], w_ref[...])
        x1_ref[at, :] = x1
        low = (x1 * inverse_rms(x1) * gain).astype(BF)
        h_ref[at, :] = low
        q_ref[at, :] = dot(low, wq_ref[...]).astype(BF)
    cross_forward(heads, count_ref, blocks_ref, docs_ref, offs_ref, q_ref, kc_ref, vc_ref, doc_ref, o_ref, lse_ref, vt_ref, acc_ref, norm_ref)


def gelu_parts(gate):
    inner = math.sqrt(2.0 / math.pi)
    square = gate * gate
    slope = jnp.tanh(inner * (gate + 0.044715 * gate * square))
    value = 0.5 * gate * (1.0 + slope)
    grad = 0.5 * (1.0 + slope) + 0.5 * gate * (1.0 - slope * slope) * inner * (1.0 + 3 * 0.044715 * square)
    return value, grad


def unpack_units(packed_ref, in_ref, down_ref, piece):
    depth, _, wide = packed_ref.shape
    slab = D // depth
    third = (packed_ref.shape[1] - slab - piece)
    down_ref[pl.ds(depth * piece, down_ref.shape[0] - depth * piece), :] = jnp.zeros((down_ref.shape[0] - depth * piece, D), BF)
    for z in range(depth):
        in_ref[pl.ds(z * slab, slab), :] = packed_ref[z, pl.ds(0, slab), :]
        down_ref[pl.ds(z * piece, piece), pl.ds(0, wide)] = packed_ref[z, pl.ds(slab, piece), :]
        for t in range(wide // (D - wide)):
            size = min(third, piece - t * third)
            down_ref[pl.ds(z * piece + t * third, size), pl.ds(wide, D - wide)] = packed_ref[z, pl.ds(slab + piece, size), pl.ds(t * (D - wide), D - wide)]


def ffn_block(chips, n_cols, n_w, packed, first, piece, place, order, corder, zorder, x1_ref, gains_ref, *refs):
    grads, refs = refs[:chips], refs[chips:]
    pieces, outs = refs[:n_cols], refs[n_cols : n_cols + n_w]
    units_in = refs[n_cols + n_w : n_cols + n_w + (2 if packed else 4)]
    ocb_ref, g_ref, h_ref, act0_ref, act1_ref, dgu0_ref, dgu1_ref, keep_ref, wrows_ref, down0_ref, down1_ref, own_ref, *rest = refs[n_cols + n_w + len(units_in) :]
    away_refs, (w_ref, in0_ref, in1_ref, x2_ref, dh_ref) = rest[: chips - 1], rest[chips - 1 :]
    half = own_ref.shape[0] // 2
    units = act0_ref.shape[1]
    width = wrows_ref.shape[0]
    if packed:
        unpack_units(units_in[0], in0_ref, down0_ref, piece)
        unpack_units(units_in[1], in1_ref, down1_ref, piece)
    else:
        for dst, src in zip((in0_ref, in1_ref, down0_ref, down1_ref), units_in):
            dst[...] = src[...]
    assemble_cols(ocb_ref, pieces, corder)
    assemble_weight(w_ref, outs, order, zorder, first)
    wrows_ref[...] = w_ref[rows_at(place[1] * width, width), :]
    for p in range(chips):
        for part, at in enumerate(token_rows(corder[p], chips, half)):
            g_ref[at, :] = grads[p][pl.ds(part * half, half), :]
    gain = gains_ref[2:3, :]
    for r in range(0, x1_ref.shape[0], 256):
        at = pl.ds(r, 256)
        x2 = x1_ref[at, :] + dot(ocb_ref[at, :], w_ref[...])
        x2_ref[at, :] = x2
        low = (x2 * inverse_rms(x2) * gain).astype(BF)
        h_ref[at, :] = low
        total = None
        for in_ref, down_ref, act_ref, dgu_ref in ((in0_ref, down0_ref, act0_ref, dgu0_ref), (in1_ref, down1_ref, act1_ref, dgu1_ref)):
            both = dot(low, in_ref[...])
            gate, up = both[:, :units], both[:, units:]
            value, slope = gelu_parts(gate)
            act_ref[at, :] = (value * up).astype(BF)
            dact = dot_nt(g_ref[at, :], down_ref[...])
            dgu = jnp.concatenate([dact * up * slope, dact * value], axis=1).astype(BF)
            dgu_ref[at, :] = dgu
            part = dot_nt(dgu, in_ref[...])
            total = part if total is None else total + part
        dh_ref[at, :] = total
    store_chip_pieces(lambda at: dh_ref[at, :], place[1], chips, half, own_ref, away_refs)
    low, high = token_rows(place[1], chips, half)
    keep_ref[pl.ds(0, half), :] = x2_ref[low, :]
    keep_ref[pl.ds(half, half), :] = x2_ref[high, :]


def ffn_output(chips, place, act0_ref, act1_ref, down0_ref, down1_ref, own_ref, *refs):
    away_refs, (out_ref,) = refs[: chips - 1], refs[chips - 1 :]
    for r in range(0, act0_ref.shape[0], 256):
        at = pl.ds(r, 256)
        out_ref[at, :] = dot(act0_ref[at, :], down0_ref[...]) + dot(act1_ref[at, :], down1_ref[...])
    store_chip_pieces(lambda at: out_ref[at, :], place[1], chips, own_ref.shape[0] // 2, own_ref, away_refs)


def norm_grad(index, arrived, *refs):
    own_ref, value_ref, base_ref, gains_ref, out_ref, low_ref, dgain_ref = refs[arrived:]
    total = own_ref[...]
    for ref in refs[:arrived]:
        total = total + ref[pl.ds(0, total.shape[0]), :].astype(F32)
    dvalue, dgain = norm_backward(total, value_ref[...].astype(F32), gains_ref[index : index + 1, :])
    out = base_ref[...].astype(F32) + dvalue
    out_ref[...] = out
    low_ref[...] = out.astype(BF)
    dgain_ref[...] = dgain


def cross_grad(chips, heads, place, corder, count_ref, blocks_ref, docs_ref, offs_ref, wrows_ref, q_ref, k_ref, v_ref, doc_ref, lse_ref, *refs):
    pieces = refs[:chips]
    g_ref, dq_ref, keep_ref, away_ref, do_ref, kt_ref, acc_ref, dka_ref, dva_ref = refs[chips:]
    half = pieces[0].shape[0] // 2
    width = heads * DK
    core = place[0]
    for p in range(chips):
        for part, at in enumerate(token_rows(corder[p], chips, half)):
            g_ref[at, :] = pieces[p][pl.ds(part * half, half), :]
    for r in range(0, g_ref.shape[0], 256):
        at = pl.ds(r, 256)
        do_ref[at, :] = dot_nt(g_ref[at, :], wrows_ref[...]).astype(BF)
    cross_backward(heads, count_ref, blocks_ref, docs_ref, offs_ref, q_ref, k_ref, v_ref, do_ref, doc_ref, lse_ref, dq_ref, kt_ref, acc_ref, dka_ref, dva_ref)
    rows = keep_ref.shape[0] // chips
    for j in range(chips):
        to = pl.ds(j * rows, rows)
        for src, lanes in ((dka_ref, pl.ds(0, width)), (dva_ref, pl.ds(width, width))):
            keep_ref[to, lanes] = src[rows_at((2 * j + core) * rows, rows), :]
            away_ref[to, lanes] = src[rows_at((2 * j + 1 - core) * rows, rows), :].astype(BF)


def table_sums(heads, ids_ref, dnear_ref, dfar_ref, dtable_ref):
    first = lax.broadcasted_iota(jnp.int32, (QB // 2, QB), 1) < QB // 2
    for h in range(heads):
        lanes = pl.ds(h * QB, QB)
        tiles = [dnear_ref[a, :, lanes] for a in range(7)]
        near = [jnp.where(first, tiles[3 + d] + pltpu.roll(tiles[1 + d], QB // 2, 1), 0.0) for d in range(3)]
        far = sum(jnp.sum(jnp.where(first, 0.0, tiles[a]) if a < 6 else tiles[a], axis=0, keepdims=True) for a in (4, 5, 6))
        sums = []
        for bucket in range(BUCKETS):
            parts = [jnp.where(ids_ref[3 + d] == bucket, near[d], 0.0) for d in range(3)]
            sums.append(jnp.sum(parts[0] + parts[1] + parts[2], axis=0, keepdims=True))
        sums[-1] = sums[-1] + far + dfar_ref[:, lanes]
        dtable_ref[h] = jnp.concatenate(sums, axis=0)


def self_grad(chips, n_cols, n_w, heads, first, place, order, corder, zorder, x1_ref, gb2_ref, own_ref, gains_ref, wo_ref, q_ref, k_ref, v_ref, lse_ref, near_ref, start_ref, place_ref, ids_ref, *refs):
    pieces, outs = refs[:n_cols], refs[n_cols : n_cols + n_w]
    gb1_ref, dq_ref, keep_ref, away_ref, dtable_ref, gx1_ref, dgain_ref, dnear_ref, dfar_ref, dqc_ref, w_ref, dx_ref, do_ref, dkv_ref, ds_ref, p_ref, kt_ref = refs[n_cols + n_w :]
    half = own_ref.shape[0] // 2
    core = place[0]
    assemble_cols(dqc_ref, pieces, corder)
    assemble_weight(w_ref, outs, order, zorder, first)
    gain = gains_ref[1:2, :]
    total = jnp.zeros_like(gain)
    for r in range(0, x1_ref.shape[0], 256):
        at = pl.ds(r, 256)
        dh = dot_nt(dqc_ref[at, :], w_ref[...])
        dvalue, dgain = norm_backward(dh, x1_ref[at, :], gain)
        total = total + dgain
        dx_ref[at, :] = dvalue
        low = (gb2_ref[at, :].astype(F32) + dvalue).astype(BF)
        gb1_ref[at, :] = low
        do_ref[at, :] = dot_nt(low, wo_ref[...]).astype(BF)
    dgain_ref[...] = total
    for part, at in enumerate(token_rows(place[1], chips, half)):
        mine = pl.ds(part * half, half)
        gx1_ref[mine, :] = own_ref[mine, :] + dx_ref[at, :]
    self_backward(heads, core, q_ref, k_ref, v_ref, do_ref, lse_ref, near_ref, start_ref, place_ref, dq_ref, dkv_ref, dnear_ref, dfar_ref, ds_ref, p_ref, kt_ref)
    for l in range(2 * chips):
        rows = pl.ds(l * 64, 64)
        keep_ref[rows, :] = dkv_ref[rows_at(block_place(l, core, chips) * 64, 64), :]
        away_ref[rows, :] = dkv_ref[rows_at(block_place(l, 1 - core, chips) * 64, 64), :].astype(BF)
    table_sums(heads, ids_ref, dnear_ref, dfar_ref, dtable_ref)


def self_close(chips, place, x_ref, dq_ref, keep_ref, come_ref, w_ref, *refs):
    more, (dqkv_ref, dgain_ref, own_ref, *refs) = refs[: chips - 1], refs[chips - 1 :]
    away_refs, (dx_ref,) = refs[: chips - 1], refs[chips - 1 :]
    width = dq_ref.shape[1]
    total = jnp.zeros_like(dgain_ref)
    for r in range(0, dq_ref.shape[0], 256):
        at = pl.ds(r, 256)
        dqkv_ref[at, pl.ds(0, width)] = dq_ref[at, :]
        dqkv_ref[at, pl.ds(width, 2 * width)] = (keep_ref[at, :] + come_ref[at, :].astype(F32)).astype(BF)
        part = dot_nt(dqkv_ref[at, :], w_ref[...])
        dx_ref[at, :] = part
        value = x_ref[at, :].astype(F32)
        total = total + jnp.sum(part * (value * inverse_rms(value)), axis=0, keepdims=True)
    dgain_ref[...] = total
    tokens = own_ref.shape[0]
    for ref, piece in zip(away_refs, more):
        ref[pl.ds(tokens, piece.shape[0]), :] = piece[...]
    firsts = [ref.at[pl.ds(0, tokens)] for ref in away_refs]
    store_chip_pieces(lambda at: dx_ref[at, :], place[1], chips, tokens // 2, own_ref, firsts)


def spread_units(depth, piece, parts_ref, out_ref, down_ref):
    n, slab = parts_ref.shape[0], out_ref.shape[0]
    wide = parts_ref.shape[2]
    third = parts_ref.shape[1] - slab - piece
    for j in range(n):
        down_ref[pl.ds(j * piece, piece), pl.ds(0, wide)] = parts_ref[j, pl.ds(slab, piece), :].astype(F32)
        for t in range(wide // (D - wide)):
            size = min(third, piece - t * third)
            part = parts_ref[j, pl.ds(slab + piece, size), pl.ds(t * (D - wide), D - wide)]
            down_ref[pl.ds(j * piece + t * third, size), pl.ds(wide, D - wide)] = part.astype(F32)
    units = -(-piece * depth // 128) * 128
    for r in range(0, slab, 32):
        at = pl.ds(r, 32)
        values = [parts_ref[j, at, :].astype(F32) for j in range(n)]
        cols = [values[j][:, g * units + z * piece : g * units + (z + 1) * piece] for g in range(2) for z in range(depth) for j in range(n)]
        out_ref[at, :] = jnp.concatenate(cols, axis=1)


def spread_stacked(first, groups, parts_ref, *outs):
    n, slab = parts_ref.shape[0], parts_ref.shape[1]
    width = outs[0].shape[1] // (n * groups[0])
    for out, parts in zip(outs, groups):
        for t in range(parts):
            for j in range(n):
                out[:, pl.ds((t * n + j) * width, width)] = parts_ref[j, :, pl.ds(first + t * width, width)].astype(F32)
        first += parts * width


def spread(groups, heads, order, *refs):
    n = len(refs) - len(groups) - 2
    pieces, (*outs, gain_ref, table_ref) = refs[:n], refs[n:]
    slab = outs[0].shape[0]
    width = pieces[0].shape[1] // sum(groups)
    per = table_ref.shape[0]
    lane = lax.broadcasted_iota(jnp.int32, (per, H), 1)
    gain, table = jnp.zeros(gain_ref.shape, F32), jnp.zeros((per, H), F32)
    for j, ref in enumerate(pieces):
        first = 0
        for out, parts in zip(outs, groups):
            for t in range(parts):
                part = ref[pl.ds(0, slab), pl.ds((first + t) * width, width)]
                out[:, rows_at(t * n * width + order[j] * width, width)] = part.astype(F32)
            first += parts
        extra = ref[pl.ds(slab, 16), :].astype(F32)
        gain = gain + extra[8:11, :slab]
        for h in range(heads):
            table = table + jnp.where(lane == (order[j] // 2) * heads + h, extra[:per, h : h + 1], 0.0)
    gain_ref[...] = gain
    table_ref[...] = table


def body(
    hidden_in,
    encoder_out,
    doc_ids,
    enc_offsets,
    cotangent,
    self_qkv,
    self_out,
    rel_bias,
    cross_q,
    cross_kv,
    cross_out,
    ffn_in,
    ffn_out,
    norm_gains,
):
    n, depth = lax.axis_size("ctx"), lax.axis_size("fsdp")
    me, level = lax.axis_index("ctx"), lax.axis_index("fsdp")
    chips = n // 2
    core, chip = me % 2, me // 2
    tokens = hidden_in.shape[1]
    half = tokens // 2
    mine_tokens = tokens * chips
    stream = tokens * n
    width = D // n
    cols = 2 * width
    heads = H // chips
    slab = D // depth
    piece = FF // (depth * n)
    units = -(-piece * depth // 128) * 128
    fill = units - piece * depth
    enc_rows = encoder_out.shape[1]
    rows_all = enc_rows * n
    wide = n == 8
    own, other = me * width, (me ^ 1) * width
    sides = 2 if wide else 1
    order = jnp.stack(ctx_order(me, n)).astype(jnp.int32)
    corder = jnp.stack(chip_order(me, n)).astype(jnp.int32)
    zorder = jnp.stack([level ^ d for d in range(depth)]).astype(jnp.int32)
    place = jnp.stack([core, chip]).astype(jnp.int32)
    per = BUCKETS // depth

    def columns(value, start, size):
        return lax.dynamic_slice_in_dim(value, start, size, 1)

    def part_columns(value, parts, start, size):
        step = value.shape[1] // parts
        return jnp.concatenate([columns(value, p * step + start, size) for p in range(parts)], axis=1)

    def gather_columns(value):
        if wide:
            return chip_gather(value, n)
        groups = [[2 * k + c for k in range(chips)] for c in range(2)]
        return [lax.all_gather(value, "ctx", axis=1, tiled=True, axis_index_groups=groups)]

    def gather_whole(pieces):
        rows = jnp.zeros((D, width), BF)
        for d, value in enumerate(pieces):
            rows = lax.dynamic_update_slice(rows, value, ((level ^ d) * slab, 0))
        return [lax.all_gather(rows, "ctx", axis=1, tiled=True)[None]]

    def cross_weights(start, size):
        return jnp.concatenate([columns(cross_q, start, size), part_columns(cross_kv, 2, start, size)], axis=1)

    def first_of(at, size):
        return first_weights(at, self_qkv, self_out, cross_out, rel_bias, norm_gains, size)

    encoder = lax.all_gather(encoder_out[0], "ctx", axis=0)
    if wide:
        w_first = z_gather(first_of(me, width), depth)
        hidden = chip_gather(after(hidden_in[0], w_first[1]), n)
        w_first2 = [first_of(me ^ 1, width)] + [sibling(v, n) for v in w_first[1:]]
        ready = (*hidden, *w_first, *w_first2)
        w_out = ctx_gather(jnp.stack([v[:slab, 3 * width :] for v in w_first]), n)
        w_cout, first_cout = w_out, width
        w_cross, w_cross2 = None, None
    else:
        w_first, w_first2 = z_gather(first_of(chip, cols), depth), []
        hidden = chip_gather(hidden_in[0], n)
        w_cross, w_cross2 = z_gather(cross_weights(chip * cols, cols), depth), []
        first_cout = 0
        w_out, w_cq, w_cout = [gather_whole(z_gather(columns(w, own, width), depth)) for w in (self_out, cross_q, cross_out)]
    parts = []
    for part in range(2):
        parts += [columns(ffn_in, part * FF + z * (FF // depth) + me * piece, piece) for z in range(depth)]
        parts += [jnp.zeros((slab, fill), BF)] * (fill > 0)
    unit_in = jnp.concatenate(parts, axis=1)
    unit_down = lax.dynamic_slice_in_dim(ffn_out, me * piece, piece)
    if wide:
        third = -(-piece // 24) * 8
        tail = jnp.pad(unit_down[:, 2 * units :], ((0, 3 * third - piece), (0, 0)))
        tail = jnp.concatenate([tail[t * third : (t + 1) * third] for t in range(3)], axis=1)
        packed = jnp.concatenate([unit_in, unit_down[:, : 2 * units], tail], axis=0)
    else:
        w_in = lax.all_gather(unit_in, "fsdp", axis=0, tiled=True)
        w_down = jnp.pad(lax.all_gather(unit_down, "fsdp", axis=0, tiled=True), ((0, fill), (0, 0)))
        w_units = [w_in, sibling(w_in, n), w_down, sibling(w_down, n)]

    ids = doc_ids[0]
    offsets = enc_offsets[0]
    docs = offsets.shape[0]
    doc_range = jnp.arange(docs, dtype=jnp.int32)

    def local_tokens(value):
        low, high = value[: stream // 2].reshape(chips, 2, half), value[stream // 2 :].reshape(chips, 2, half)
        low = jnp.where(core == 0, low[:, 0], low[:, 1])
        high = jnp.where(core == 0, high[:, 1], high[:, 0])
        return jnp.concatenate([low, high], axis=0).reshape(mine_tokens)

    doc_starts = jnp.sum((ids[None, :] < doc_range[:, None]).astype(jnp.int32), axis=1)
    my_ids = local_tokens(ids)
    places = local_tokens(jnp.arange(stream, dtype=jnp.int32))[None]
    starts = jnp.sum(jnp.where(my_ids[None, :] == doc_range[:, None], doc_starts[:, None], 0), axis=0)[None]
    q_blocks = mine_tokens // QB
    first_doc = my_ids[::QB]
    spans = my_ids[QB - 1 :: QB] - first_doc + 1
    at_or_before = np.arange(q_blocks)[:, None] >= np.arange(q_blocks)[None, :]
    ends = jnp.sum(jnp.where(at_or_before, spans[None, :], 0), axis=1)
    slots = jnp.arange(q_blocks + docs, dtype=jnp.int32)
    slot_block = jnp.minimum(jnp.sum((slots[:, None] >= ends[None, :]).astype(jnp.int32), axis=1), q_blocks - 1)
    in_block = slot_block[:, None] == jnp.arange(q_blocks)[None, :]
    slot_doc = slots + jnp.sum(jnp.where(in_block, (first_doc - ends + spans)[None, :], 0), axis=1)
    slot_doc = jnp.clip(slot_doc, 0, docs - 1)
    slot_part = jnp.sum(jnp.where(slot_doc[:, None] == doc_range[None, :], (offsets // ENC_ROWS)[None, :], 0), axis=1)
    work = (jnp.sum(spans)[None], slot_block, slot_doc, slot_part)
    doc_rows = my_ids.reshape(q_blocks, 1, QB)
    near_ids = jnp.asarray(near_buckets())

    rows_bf = ((mine_tokens, cols), BF)
    full_bf = ((mine_tokens, D), BF)
    full_f32 = ((mine_tokens, D), F32)
    own_f32 = ((tokens, D), F32)
    pieces_out = [own_f32] + [((tokens, D), BF)] * (chips - 1)
    lanes = QB * heads
    near_f32 = ((7, QB // 2, lanes), F32)
    triangle = ((q_blocks // 2, 2 * QB, (q_blocks + 1) * lanes), BF)
    parted = ((rows_all // ENC_ROWS, cols, ENC_ROWS), BF)
    blocked = ((q_blocks, cols, lanes), F32)

    x, h1, query, kv, near, gains, wqkv = run(
        functools.partial(self_project, chips, depth, sides, heads), (place, corder, zorder), (near_ids, *hidden, *w_first, *w_first2),
        [full_bf, full_bf, rows_bf, ((mine_tokens, 2 * cols), BF), near_f32, ((8, D), F32), ((D, 3 * cols), BF)],
        [], "self_project", 1)
    if wide:
        w_cross = z_gather(after(cross_weights(own, width), query), depth)
    key, value, attended, lse = run(
        functools.partial(self_attend, chips, heads), (place,), (query, kv, sibling(kv, n), near, starts, places),
        [((stream, cols), BF), ((stream, cols), BF), rows_bf, ((1, mine_tokens * heads), F32)],
        [((cols, stream), BF)], "self_attend", 1)
    ob = gather_columns(attended)
    if wide:
        w_cross = [jnp.stack(list(lax.optimization_barrier((*w_cross, attended))[:depth]))]
        w_cross2 = [sibling(w_cross[0], n)]
    if wide:
        packed = lax.all_gather(after(packed, w_cross[0]), "fsdp", axis=0)
    ckv, wckv = run(
        functools.partial(encoder_block, chips, depth, wide), (place, zorder), (encoder, *w_cross, *w_cross2),
        [((rows_all // 2, 2 * cols), BF), ((D, 2 * cols), BF)], [], "encoder_block", 1)
    ckey, cvalue, x1, h2, cquery, crossed, clse, wo_rows, ob_all = run(
        functools.partial(cross_block, len(ob), len(w_out), depth, wide, heads, enc_rows), (place, order, corder, zorder, *work),
        (x, gains, ckv, sibling(ckv, n), doc_rows, *ob, *w_out, *w_cross, *w_cross2),
        [((rows_all, cols), BF)] * 2 + [full_f32, full_bf, rows_bf, rows_bf, ((q_blocks, 1, lanes), F32), ((cols, D), BF), full_bf],
        [((D, D), BF), ((D, cols), BF), parted, blocked, ((q_blocks, 1, lanes), F32)],
        "cross_block", 6)
    g_pieces = chip_gather(after(cotangent[0], ob[-1]), n)
    ocb_pieces = gather_columns(after(crossed, *g_pieces[1:]))
    if wide:
        w_units = [packed, sibling(after(packed, *ocb_pieces[1:]), n)]
    ocb, g, h3, act, act2, dgu, dgu2, x2_own, wco_rows, down, down2, *dh3 = run(
        functools.partial(ffn_block, chips, len(ocb_pieces), len(w_cout), wide, first_cout, piece), (place, order, corder, zorder),
        (x1, gains, *g_pieces, *ocb_pieces, *w_cout, *w_units),
        [full_bf, full_bf, full_bf, *[((mine_tokens, units), BF)] * 2, *[((mine_tokens, 2 * units), BF)] * 2, own_f32, ((cols, D), BF), *[((units, D), BF)] * 2, *pieces_out],
        [((D, D), BF), *[((D, 2 * units), BF)] * 2, full_f32, full_f32], "ffn_block", 14)

    if wide:
        w_cq = [lax.all_gather(after(w_cross[0][:, :, :width], crossed), "ctx", axis=0)]

    def reduce_norm(parts, index, kept, base):
        arrived = chip_reduce(parts[1:], n)
        return arrived, run(
            functools.partial(norm_grad, index, len(arrived)), (), (*arrived, parts[0], kept, base, gains),
            [own_f32, ((tokens, D), BF), ((1, D), F32)], [], "norm_grad", 3)

    def sum_pieces(parts):
        total = parts[0]
        for part in chip_reduce(parts[1:], n):
            total = total + part.astype(F32)
        return total

    def pair_sum(left, mine, theirs):
        come = sibling(dot_tn(left, theirs).astype(BF), n)
        return (dot_tn(left, mine) + come.astype(F32)).astype(BF)

    def sum_z(value):
        return lax.psum_scatter(value, "fsdp", scatter_dimension=0, tiled=True)

    def send_z(value):
        parts = [lax.dynamic_index_in_dim(value, level, 0, False)]
        for d in range(1, depth):
            away = lax.dynamic_index_in_dim(value, level ^ d, 0, False)
            parts.append(send(away, "fsdp", depth, lambda i, d=d: i ^ d))
        return parts

    def total_z(parts):
        return sum(part.astype(F32) for part in parts).astype(BF)

    arrived3, (gx2_own, gb2_own, dgain3) = reduce_norm(dh3, 2, x2_own, cotangent[0])
    pair_in = pair_sum(after(h3, *arrived3), dgu, dgu2)
    g_late = after(g, *arrived3)
    come = sibling(dot_tn(act2, g_late).astype(BF), n)
    pair_down = (dot_tn(act, g_late) + come.astype(F32)).astype(BF)[: piece * depth]
    if wide:
        down_rows = pair_down.reshape(depth, piece, D)
        rest = jnp.pad(down_rows[:, :, 2 * units :], ((0, 0), (0, 3 * third - piece), (0, 0)))
        rest = jnp.concatenate([rest[:, t * third : (t + 1) * third] for t in range(3)], axis=2)
        pair = jnp.concatenate([pair_in.reshape(depth, slab, 2 * units), down_rows[:, :, : 2 * units], rest], axis=1)
        grad_units = sum_z(after(pair.reshape(depth * (slab + piece + third), 2 * units), *w_cq))
    else:
        pair = pair_in
        grad_in, grad_down = sum_z(pair_in), sum_z(pair_down)
    gb2_pieces = chip_gather(after(gb2_own, pair, *w_cq), n)
    out_parts = run(
        functools.partial(ffn_output, chips), (place,), (after(act, *gb2_pieces[1:]), act2, down, down2), pieces_out, [full_f32], "ffn_output", 4)
    gb2, dcq, dkv_keep, dkv_away = run(
        functools.partial(cross_grad, chips, heads), (place, corder, *work), (after(wco_rows, pair, *out_parts), cquery, ckey, cvalue, doc_rows, clse, *gb2_pieces),
        [full_bf, rows_bf, ((rows_all // 2, 2 * cols), F32), ((rows_all // 2, 2 * cols), BF)],
        [rows_bf, parted, blocked, ((rows_all, cols), F32), ((rows_all, cols), F32)],
        "cross_grad", 13)
    arrived = chip_reduce(out_parts[1:], n)
    result = after(x2_own, dcq) + out_parts[0]
    for part in arrived:
        result = result + part.astype(F32)
    result = result.astype(BF)
    dcq_pieces = gather_columns(after(dcq, result))
    early = dcq_pieces[1:] or dcq_pieces
    dkv_away = after(dkv_away, *early)
    h2, ocb = lax.optimization_barrier((h2, ocb, *early))[:2]
    ckv_both, *denc = run(
        functools.partial(encoder_grad, chips), (place,), (dkv_keep, sibling(dkv_away, n), wckv, encoder),
        [((D, 2 * cols), BF), ((enc_rows, D), F32), *[((enc_rows, D), BF)] * (chips - 1)], [((rows_all // 2, 2 * cols), BF)],
        "encoder_grad", 7)

    def side_columns(value, parts, mine):
        return part_columns(value, parts, (core if mine else 1 - core) * width, width)

    def middle_of(mine):
        return jnp.concatenate([
            dot_tn(h2, side_columns(dcq, 1, mine)),
            side_columns(ckv_both, 2, mine).astype(F32),
            dot_tn(ocb, columns(gb2, own if mine else other, width)),
        ], axis=1)

    come = sibling(middle_of(False).astype(BF), n)
    middle_pair = (middle_of(True) + come.astype(F32)).astype(BF)
    gb1, dq, dkv_keep, dkv_away, dtable, gx1_own, dgain2 = run(
        functools.partial(self_grad, chips, len(dcq_pieces), len(w_cq), heads, 0), (place, order, corder, zorder),
        (after(x1, *denc, middle_pair, *([grad_units] if wide else [])), gb2, gx2_own, gains, wo_rows, query, key, value, lse, near, starts, places, near_ids, *dcq_pieces, *w_cq),
        [full_bf, rows_bf, ((mine_tokens, 2 * cols), F32), ((mine_tokens, 2 * cols), BF), ((heads, BUCKETS, QB), F32), own_f32, ((1, D), F32)],
        [near_f32, ((1, lanes), F32), full_bf, ((D, D), BF), full_f32, rows_bf, ((stream, 2 * cols), F32), triangle, triangle, ((cols, stream), BF)],
        "self_grad", 15)
    if wide:
        grad_units = lax.all_gather(after(grad_units, dcq_pieces[-1]), "ctx", axis=0)
        middle_pair = after(middle_pair, grad_units, gb1)
    middle = sum_z(middle_pair)
    dqkv, dgain1, *dh1 = run(
        functools.partial(self_close, chips), (place,), (x, dq, dkv_keep, sibling(dkv_away, n), wqkv, *denc[1:]),
        [((mine_tokens, 3 * cols), BF), ((1, D), F32), own_f32, *[((tokens + enc_rows, D), BF)] * (chips - 1)], [full_f32], "self_close", 4)

    dtable = jnp.sum(dtable, axis=2).T
    dtable = jnp.pad(dtable.reshape(depth, per, heads), ((0, 0), (0, 8 - per), (0, 4 * width - heads)))
    dgains = jnp.concatenate([dgain1, jnp.where(chip == 0, dgain2, 0.0), dgain3], axis=0)
    dgains = jnp.transpose(dgains.reshape(3, depth, slab), (1, 0, 2))
    dgains = jnp.pad(dgains, ((0, 0), (0, 5), (0, 4 * width - slab)))

    def last_of(mine):
        return jnp.concatenate([dot_tn(h1, side_columns(dqkv, 3, mine)), dot_tn(ob_all, columns(gb1, own if mine else other, width))], axis=1)

    come = sibling(last_of(False).astype(BF), n)
    last = last_of(True) + come.astype(F32)
    last = jnp.concatenate([last.reshape(depth, slab, 4 * width), dtable, dgains], axis=1).astype(BF)
    last = send_z(last)
    dh1[0] = after(dh1[0], last[1])
    arrived, (grad_hidden, _, _) = reduce_norm(dh1, 0, hidden_in[0], gx1_own)
    grad_enc = denc[0]
    for part in arrived:
        grad_enc = grad_enc + part[tokens:].astype(F32)
    if wide:
        grad_ffn_in, grad_ffn_out = run(
            functools.partial(spread_units, depth, piece), (), (grad_units,), [((slab, 2 * FF), F32), ((n * piece, D), F32)], [], "spread_units", 6)
        grad_cross_q, grad_cross_kv, grad_cross_out = run(
            functools.partial(spread_stacked, 0, (1, 2, 1)), (), (lax.all_gather(after(middle, gb1), "ctx", axis=0),),
            [((slab, D), F32), ((slab, 2 * D), F32), ((slab, D), F32)], [], "spread_stacked", 4)
        last = total_z([after(last[0], grad_hidden, grad_ffn_in), *last[1:]])
        grad_self_qkv, grad_self_out, grad_gains, grad_table = run(
            functools.partial(spread, (3, 1), heads), (order,), ctx_gather(last, n),
            [((slab, 3 * D), F32), ((slab, D), F32), ((3, slab), F32), ((per, H), F32)], [], "spread", 4)
    else:
        def place_columns(pieces, groups):
            outs, first = [], 0
            for g in groups:
                value = pieces[:, :slab, first * width : (first + g) * width].reshape(n, slab, g, width)
                outs.append(jnp.transpose(value, (1, 2, 0, 3)).reshape(slab, g * D).astype(F32))
                first += g
            return outs

        pieces = lax.all_gather(total_z(last), "ctx", axis=0)
        grad_self_qkv, grad_self_out = place_columns(pieces, (3, 1))
        extra = pieces[:, slab:].astype(F32)
        grad_gains = jnp.sum(extra[:, 8:11, :slab], axis=0)
        table = jnp.sum(extra[:, :per, :heads].reshape(chips, 2, per, heads), axis=1)
        grad_table = jnp.transpose(table, (1, 0, 2)).reshape(per, H)
        grad_cross_q, grad_cross_kv, grad_cross_out = place_columns(lax.all_gather(middle, "ctx", axis=0), (1, 2, 1))
        grad_ffn_out = lax.all_gather(grad_down, "ctx", axis=0, tiled=True).astype(F32)
        up_cols = lax.all_gather(grad_in, "ctx", axis=0).reshape(n, slab, 2, units)[..., : piece * depth]
        up_cols = up_cols.reshape(n, slab, 2 * depth, piece)
        grad_ffn_in = jnp.transpose(up_cols, (1, 2, 0, 3)).reshape(slab, 2 * FF).astype(F32)
    return (
        result[None],
        grad_hidden[None],
        grad_enc[None],
        grad_self_qkv,
        grad_self_out,
        grad_table,
        grad_cross_q,
        grad_cross_kv,
        grad_cross_out,
        grad_ffn_in,
        grad_ffn_out,
        grad_gains,
    )


def solution(mesh):
    split = P("fsdp", "ctx", None)
    rows = P("fsdp", None)
    return jax.shard_map(
        body,
        mesh=mesh,
        in_specs=(split, split, rows, rows, split) + (rows,) * 8 + (P(None, "fsdp"),),
        out_specs=(split,) * 3 + (rows,) * 8 + (P(None, "fsdp"),),
        check_vma=False,
    )
```
